256 devices in a mesh: particle: 16 (over z_hi, y), space: 16 (over x, z_lo, core).
Axes of the slice: x: 4, y: 4, z: 8 (z_hi: 4, z_lo: 2; z = z_hi * 2 + z_lo), core: 2. Of those that a mesh axis runs over, the one named last changes fastest.
Arguments:
- ensemble: float32 [16, 13, 512, 1024], P('particle', None, 'space'), may hold values from -6 to 6
- ancestors: int32 [16], replicated, may hold values from 0 to 15
- depth_levels: int32 [512, 1024], P('space'), may hold values from 0 to 4
- level_coefs: float32 [3, 4], replicated, may hold values from 0.25 to 1
- altimetry: float32 [3, 64, 512], P(None, 'particle', 'space'), may hold values from -6 to 6
- obs_rows: int32 [3, 64], replicated, may hold values from 0 to 1023, as said below
Outputs:
- forecast: float32 [16, 13, 512, 1024], P('particle', None, 'space')
The draws below stay inside these ranges and needn't reach their ends.
Inputs may be any that keep to these rules, and one draw needn't show every extreme that they name: `obs_rows`: within one step the indices are distinct.
All inputs are finite; a program needn't handle non-finite values.
Results may differ from the reference program's by a relative error of at most 0.00013.
Values sent between devices are 32-bit elements; how exact they have to be, the bound alone decides.
A program may use at most 128 MiB of HBM per device.

```python
import jax
import jax.numpy as jnp
from jax import lax

L = 4
NY = 1024
STEPS = 3
OBS = 64
MEMBERS = 16
NX = 512


def draw_obs_rows(key, part):
    keys = jax.random.split(jax.random.fold_in(key, 7), STEPS)
    return jax.vmap(lambda single: jax.random.permutation(single, NY)[:OBS])(keys).astype(jnp.int32)


def plant(entries, key, low, largest):
    spot = [jax.random.randint(jax.random.fold_in(key, axis), (), 0, length) for axis, length in enumerate(entries.shape)]
    longest = entries.shape.index(max(entries.shape))
    neighbour = spot[:longest] + [(spot[longest] + 1) % entries.shape[longest]] + spot[longest + 1:]
    return entries.at[tuple(spot)].set(low).at[tuple(neighbour)].set(largest)


def shard_levels(stream_key, shape, shards, low, largest):
    def one(position, parts):
        heights = jax.random.uniform(jax.random.fold_in(jax.random.fold_in(stream_key, 6), position), (parts,), jnp.float32, low / len(shards), largest / len(shards))
        return jnp.repeat(jnp.exp(heights), shape[position] // parts).reshape((-1,) + (1,) * (len(shape) - position - 1))

    factor_of = one(*shards[0])
    for cut in shards[1:]:
        factor_of = factor_of * one(*cut)
    return factor_of


def centred(key, shape, width, bound, shards=(), held_as=jnp.bfloat16):
    factor_of = shard_levels(key, shape, shards, -0.22, 0.18) if shards else 1.0
    values = jax.random.normal(key, shape, jnp.float32) * width * factor_of
    return jnp.minimum(jnp.maximum(values, -bound), bound).astype(held_as)


def setup_inputs(seed: int = 0) -> dict:
    key_list = jax.random.split(jax.random.key(seed), 7)
    return {
        "ensemble": centred(key_list[0], (MEMBERS, 3 * L + 1, NX, NY), 1.0, 6.0, ((0, 16), (2, 16)), jnp.float32),
        "ancestors": plant(jax.random.randint(key_list[1], (MEMBERS,), 0, MEMBERS), jax.random.fold_in(key_list[1], 1), 0, MEMBERS - 1).astype(jnp.int32),
        "depth_levels": plant(jax.random.randint(key_list[2], (NX, NY), 0, L + 1), jax.random.fold_in(key_list[2], 1), 0, L).astype(jnp.int32),
        "level_coefs": jnp.clip(jax.random.uniform(key_list[3], (3, L), jnp.float32, 0.25, 1.0), 0.25, 1.0),
        "altimetry": centred(key_list[4], (STEPS, OBS, NX), 1.0, 6.0, ((1, 16), (2, 16)), jnp.float32),
        "obs_rows": draw_obs_rows(jax.random.fold_in(key_list[6], 71), 0),
    }


DT = 0.2
CORIOLIS = 0.5
GRAVITY = 1.0
NUDGE = 0.5


def pad_second(field):
    return jnp.pad(field, [(0, 0)] * (field.ndim - 1) + [(1, 1)])


def gradients(wide):
    center = wide[:, 1:-1]
    east = wide[:, 2:]
    west = wide[:, :-2]
    padded = pad_second(center)
    ddx = (east - west) * 0.5
    ddy = (padded[..., 2:] - padded[..., :-2]) * 0.5
    laplace = east + west + padded[..., 2:] + padded[..., :-2] - 4.0 * center
    return center, ddx, ddy, laplace


def widen(field):
    return jnp.concatenate([field[:, -1:], field, field[:, :1]], axis=1)


def one_step(state, masks, coefs, target, hit):
    levels = masks.shape[0]
    surface = masks[0]
    center, ddx, ddy, laplace = gradients(widen(state))
    east_vel = center[:levels]
    north_vel = center[levels:2 * levels]
    temper = center[2 * levels:3 * levels]
    height = center[3 * levels]
    thick = coefs[0][:, None, None]
    visc = 0.2 * coefs[1][:, None, None]
    kappa = 0.2 * coefs[2][:, None, None]
    spread = ddx[:levels] + ddy[levels:2 * levels]
    height_one = surface * (height - DT * jnp.sum(thick * masks * spread, axis=0))
    height_two = surface * (height_one + NUDGE * hit * (target - height_one))
    unused, grad_x, grad_y, unused_lap = gradients(widen(height_two[None]))
    east_new = masks * (east_vel + DT * (CORIOLIS * north_vel - GRAVITY * grad_x + visc * laplace[:levels]))
    north_new = masks * (north_vel + DT * (-CORIOLIS * east_vel - GRAVITY * grad_y + visc * laplace[levels:2 * levels]))
    temper_new = masks * (temper + DT * (kappa * laplace[2 * levels:3 * levels] - east_vel * ddx[2 * levels:3 * levels] - north_vel * ddy[2 * levels:3 * levels]))
    return jnp.concatenate([east_new, north_new, temper_new, height_two[None]], axis=0)


def reference(ensemble, ancestors, depth_levels, level_coefs, altimetry, obs_rows):
    level_ids = jnp.arange(L, dtype=jnp.int32)
    masks = (level_ids[:, None, None] < depth_levels[None]).astype(jnp.float32)
    full_mask = jnp.concatenate([masks, masks, masks, masks[:1]], axis=0)
    columns = jnp.arange(NY, dtype=jnp.int32)
    targets = []
    hits = []
    for step in range(STEPS):
        onehot = (obs_rows[step][:, None] == columns[None, :]).astype(jnp.float32)
        targets.append(jnp.dot(altimetry[step].T, onehot, precision=lax.Precision.HIGHEST, preferred_element_type=jnp.float32))
        hits.append(jnp.sum(onehot, axis=0)[None, :])
    chosen = jnp.take(ensemble, ancestors.astype(jnp.int32), axis=0)

    def run(member):
        state = member * full_mask
        for step in range(STEPS):
            state = one_step(state, masks, level_coefs, targets[step], hits[step])
        return state

    return lax.map(run, chosen)
```

```python
import jax
import jax.numpy as jnp
from jax import lax
from jax.sharding import PartitionSpec as P

STEPS = 3


DT = 0.2
CORIOLIS = 0.5
GRAVITY = 1.0
NUDGE = 0.5


def with_halo(block, sides, width):
    for axis, dim in sides:
        count = lax.axis_size(axis)
        forward = [(i, i + 1) for i in range(count - 1)]
        forward.append((count - 1, 0))
        backward = [(target, source) for source, target in forward]
        low = lax.ppermute(
            lax.slice_in_dim(block, block.shape[dim] - width, None, axis=dim), axis, forward
        )
        high = lax.ppermute(lax.slice_in_dim(block, 0, width, axis=dim), axis, backward)
        block = jnp.concatenate([low, block, high], axis=dim)
    return block


def pad_second(field):
    return jnp.pad(field, [(0, 0)] * (field.ndim - 1) + [(1, 1)])


def gradients(wide):
    center = wide[:, 1:-1]
    east = wide[:, 2:]
    west = wide[:, :-2]
    padded = pad_second(center)
    ddx = (east - west) * 0.5
    ddy = (padded[..., 2:] - padded[..., :-2]) * 0.5
    laplace = east + west + padded[..., 2:] + padded[..., :-2] - 4.0 * center
    return (center, ddx, ddy, laplace)


def widen_state(field):
    return with_halo(field, (("space", 1),), 1)


def widen_surface(field):
    return with_halo(field, (("space", 1),), 1)


def level_terms(coefs):
    thick = coefs[0][:, None, None]
    visc = 0.2 * coefs[1][:, None, None]
    kappa = 0.2 * coefs[2][:, None, None]
    return (thick, visc, kappa)


def finish(center, ddx, ddy, laplace, masks, visc, kappa, grad_x, grad_y, height_two):
    levels = masks.shape[0]
    east_vel = center[:levels]
    north_vel = center[levels : 2 * levels]
    temper = center[2 * levels : 3 * levels]
    east_new = masks * (
        east_vel + DT * (CORIOLIS * north_vel - GRAVITY * grad_x + visc * laplace[:levels])
    )
    north_new = masks * (
        north_vel
        + DT * (-CORIOLIS * east_vel - GRAVITY * grad_y + visc * laplace[levels : 2 * levels])
    )
    temper_new = masks * (
        temper
        + DT
        * (
            kappa * laplace[2 * levels : 3 * levels]
            - east_vel * ddx[2 * levels : 3 * levels]
            - north_vel * ddy[2 * levels : 3 * levels]
        )
    )
    return jnp.concatenate([east_new, north_new, temper_new, height_two[None]], axis=0)


def one_step(state, masks, coefs, target, hit):
    levels = masks.shape[0]
    surface = masks[0]
    center, ddx, ddy, laplace = gradients(widen_state(state))
    height = center[3 * levels]
    thick, visc, kappa = level_terms(coefs)
    spread = ddx[:levels] + ddy[levels : 2 * levels]
    height_one = surface * (height - DT * jnp.sum(thick * masks * spread, axis=0))
    height_two = surface * (height_one + NUDGE * hit * (target - height_one))
    unused, grad_x, grad_y, unused_lap = gradients(widen_surface(height_two[None]))
    return finish(center, ddx, ddy, laplace, masks, visc, kappa, grad_x, grad_y, height_two)


def resample(tile, ancestors):
    count = lax.axis_size("particle")
    fields, rows, width = tile.shape
    chunk = width // count
    parts = jnp.moveaxis(tile.reshape(fields, rows, count, chunk), 2, 0)
    held = lax.all_to_all(parts, "particle", 0, 0, tiled=True)
    picks = []
    for member in range(count):
        source = ancestors[member]
        inside = (source >= 0) & (source < count)
        piece = lax.dynamic_index_in_dim(held, jnp.clip(source, 0, count - 1), 0, keepdims=True)
        picks.append(jnp.where(inside, piece, jnp.zeros_like(piece)))
    chosen = lax.all_to_all(jnp.concatenate(picks, axis=0), "particle", 0, 0, tiled=True)
    return jnp.moveaxis(chosen, 0, 2).reshape(fields, rows, width)


def per_device(ensemble, ancestors, depth_levels, level_coefs, altimetry, obs_rows):
    levels = level_coefs.shape[1]
    width_y = ensemble.shape[3]
    state = resample(ensemble[0], ancestors)
    all_lines = lax.all_gather(altimetry, "particle", axis=1, tiled=True)
    level_ids = jnp.arange(levels, dtype=jnp.int32)
    masks = (level_ids[:, None, None] < depth_levels[None]).astype(jnp.float32)
    full_mask = jnp.concatenate([masks, masks, masks, masks[:1]], axis=0)
    state = state * full_mask
    columns = jnp.arange(width_y, dtype=jnp.int32)
    for step in range(STEPS):
        lines = all_lines[step]
        onehot = (obs_rows[step][:, None] == columns[None, :]).astype(jnp.float32)
        target = jnp.dot(
            lines.T, onehot, precision=lax.Precision.HIGHEST, preferred_element_type=jnp.float32
        )
        hit = jnp.sum(onehot, axis=0)[None, :]
        state = one_step(state, masks, level_coefs, target, hit)
    return state[None]


def solution(mesh):
    in_specs = (
        P("particle", None, "space", None),
        P(),
        P("space", None),
        P(),
        P(None, "particle", "space"),
        P(),
    )
    out_specs = P("particle", None, "space", None)
    return jax.shard_map(
        per_device, mesh=mesh, in_specs=in_specs, out_specs=out_specs, check_vma=False
    )
```

```python
import functools

import jax
import jax.numpy as jnp
from jax import lax
from jax.experimental import pallas as pl
from jax.experimental.pallas import tpu as pltpu
from jax.sharding import PartitionSpec as P

MESH = pl.DeviceIdType.MESH

STEPS = 3


DT = 0.2
CORIOLIS = 0.5
GRAVITY = 1.0
NUDGE = 0.5


def with_halo(block, sides, width):
    for axis, dim in sides:
        count = lax.axis_size(axis)
        forward = [(i, i + 1) for i in range(count - 1)]
        forward.append((count - 1, 0))
        backward = [(target, source) for source, target in forward]
        low = lax.ppermute(
            lax.slice_in_dim(block, block.shape[dim] - width, None, axis=dim), axis, forward
        )
        high = lax.ppermute(lax.slice_in_dim(block, 0, width, axis=dim), axis, backward)
        block = jnp.concatenate([low, block, high], axis=dim)
    return block


def pad_second(field):
    return jnp.pad(field, [(0, 0)] * (field.ndim - 1) + [(1, 1)])


def gradients(wide):
    center = wide[:, 1:-1]
    east = wide[:, 2:]
    west = wide[:, :-2]
    padded = pad_second(center)
    ddx = (east - west) * 0.5
    ddy = (padded[..., 2:] - padded[..., :-2]) * 0.5
    laplace = east + west + padded[..., 2:] + padded[..., :-2] - 4.0 * center
    return (center, ddx, ddy, laplace)


def widen_state(field):
    return with_halo(field, (("space", 1),), 1)


def widen_surface(field):
    return with_halo(field, (("space", 1),), 1)


def level_terms(coefs):
    thick = coefs[0][:, None, None]
    visc = 0.2 * coefs[1][:, None, None]
    kappa = 0.2 * coefs[2][:, None, None]
    return (thick, visc, kappa)


def finish(center, ddx, ddy, laplace, masks, visc, kappa, grad_x, grad_y, height_two):
    levels = masks.shape[0]
    east_vel = center[:levels]
    north_vel = center[levels : 2 * levels]
    temper = center[2 * levels : 3 * levels]
    east_new = masks * (
        east_vel + DT * (CORIOLIS * north_vel - GRAVITY * grad_x + visc * laplace[:levels])
    )
    north_new = masks * (
        north_vel
        + DT * (-CORIOLIS * east_vel - GRAVITY * grad_y + visc * laplace[levels : 2 * levels])
    )
    temper_new = masks * (
        temper
        + DT
        * (
            kappa * laplace[2 * levels : 3 * levels]
            - east_vel * ddx[2 * levels : 3 * levels]
            - north_vel * ddy[2 * levels : 3 * levels]
        )
    )
    return jnp.concatenate([east_new, north_new, temper_new, height_two[None]], axis=0)


def one_step(state, masks, coefs, target, hit):
    levels = masks.shape[0]
    surface = masks[0]
    center, ddx, ddy, laplace = gradients(widen_state(state))
    height = center[3 * levels]
    thick, visc, kappa = level_terms(coefs)
    spread = ddx[:levels] + ddy[levels : 2 * levels]
    height_one = surface * (height - DT * jnp.sum(thick * masks * spread, axis=0))
    height_two = surface * (height_one + NUDGE * hit * (target - height_one))
    unused, grad_x, grad_y, unused_lap = gradients(widen_surface(height_two[None]))
    return finish(center, ddx, ddy, laplace, masks, visc, kappa, grad_x, grad_y, height_two)


def window(source, grid_cols, rows, cols):
    return (pl.ds((source // grid_cols) * rows, rows), pl.ds((source % grid_cols) * cols, cols))


def exchange_kernel(
    count, grid_cols, anc_ref, ens_ref, alt_ref, out_ref, lines_ref,
    held, outgoing, send1, recv1, send2, recv2, send3, recv3, local,
):
    me = lax.axis_index("particle")
    rows, cols = held.shape[2], held.shape[3]

    barrier = pltpu.get_barrier_semaphore()
    for offset in range(1, count):
        peer = lax.rem(me + offset, count)
        pl.semaphore_signal(barrier, inc=1, device_id={"particle": peer}, device_id_type=MESH)
    pl.semaphore_wait(barrier, count - 1)

    def chunk_of(dest):
        r, c = window(dest, grid_cols, rows, cols)
        return ens_ref.at[:, r, c]

    own = pltpu.make_async_copy(chunk_of(me), held.at[me], local.at[0])
    own.start()
    own_lines = pltpu.make_async_copy(alt_ref, lines_ref.at[me], local.at[1])
    own_lines.start()
    first = []
    for offset in range(1, count):
        peer = lax.rem(me + offset, count)
        copy = pltpu.make_async_remote_copy(
            src_ref=chunk_of(peer), dst_ref=held.at[me], send_sem=send1.at[offset],
            recv_sem=recv1.at[me], device_id={"particle": peer}, device_id_type=MESH,
        )
        copy.start()
        lines = pltpu.make_async_remote_copy(
            src_ref=alt_ref, dst_ref=lines_ref.at[me], send_sem=send3.at[offset],
            recv_sem=recv3.at[me], device_id={"particle": peer}, device_id_type=MESH,
        )
        lines.start()
        first.append((copy, lines))
    own.wait()
    own_lines.wait()
    for offset, (copy, lines) in zip(range(1, count), first):
        sender = lax.rem(me + count - offset, count)
        copy.wait_send()
        lines.wait_send()
        pltpu.make_async_remote_copy(
            src_ref=chunk_of(me), dst_ref=held.at[sender], send_sem=send1.at[offset],
            recv_sem=recv1.at[sender], device_id={"particle": sender}, device_id_type=MESH,
        ).wait_recv()
        pltpu.make_async_remote_copy(
            src_ref=alt_ref, dst_ref=lines_ref.at[sender], send_sem=send3.at[offset],
            recv_sem=recv3.at[sender], device_id={"particle": sender}, device_id_type=MESH,
        ).wait_recv()

    for member in range(count):
        source = jnp.clip(anc_ref[member], 0, count - 1)
        outgoing[member] = held[source]

    r_me, c_me = window(me, grid_cols, rows, cols)
    mine = pltpu.make_async_copy(outgoing.at[me], out_ref.at[:, r_me, c_me], local.at[2])
    mine.start()
    second = []
    for offset in range(1, count):
        peer = lax.rem(me + offset, count)
        copy = pltpu.make_async_remote_copy(
            src_ref=outgoing.at[peer], dst_ref=out_ref.at[:, r_me, c_me],
            send_sem=send2.at[offset], recv_sem=recv2.at[me],
            device_id={"particle": peer}, device_id_type=MESH,
        )
        copy.start()
        second.append(copy)
    mine.wait()
    for offset, copy in zip(range(1, count), second):
        sender = lax.rem(me + count - offset, count)
        r_s, c_s = window(sender, grid_cols, rows, cols)
        copy.wait_send()
        pltpu.make_async_remote_copy(
            src_ref=outgoing.at[me], dst_ref=out_ref.at[:, r_s, c_s],
            send_sem=send2.at[offset], recv_sem=recv2.at[sender],
            device_id={"particle": sender}, device_id_type=MESH,
        ).wait_recv()


def resample(tile, ancestors, altimetry):
    count = lax.axis_size("particle")
    fields, height, width = tile.shape
    grid_rows = 4
    grid_cols = count // grid_rows
    rows, cols = height // grid_rows, width // grid_cols
    sems = pltpu.SemaphoreType.DMA((count,))
    return pl.pallas_call(
        functools.partial(exchange_kernel, count, grid_cols),
        out_shape=(
            jax.ShapeDtypeStruct(tile.shape, tile.dtype),
            jax.ShapeDtypeStruct((count,) + altimetry.shape, altimetry.dtype),
        ),
        in_specs=[
            pl.BlockSpec(memory_space=pltpu.SMEM),
            pl.BlockSpec(memory_space=pl.ANY),
            pl.BlockSpec(memory_space=pltpu.VMEM),
        ],
        out_specs=(
            pl.BlockSpec(memory_space=pl.ANY),
            pl.BlockSpec(memory_space=pltpu.VMEM),
        ),
        scratch_shapes=[
            pltpu.VMEM((count, fields, rows, cols), tile.dtype),
            pltpu.VMEM((count, fields, rows, cols), tile.dtype),
            sems, sems, sems, sems, sems, sems,
            pltpu.SemaphoreType.DMA((3,)),
        ],
        compiler_params=pltpu.CompilerParams(collective_id=0, has_side_effects=True),
    )(ancestors, tile, altimetry)


def per_device(ensemble, ancestors, depth_levels, level_coefs, altimetry, obs_rows):
    levels = level_coefs.shape[1]
    width_y = ensemble.shape[3]
    state, gathered = resample(ensemble[0], ancestors, altimetry)
    all_lines = jnp.moveaxis(gathered, 0, 1).reshape(
        (altimetry.shape[0], -1) + altimetry.shape[2:]
    )
    level_ids = jnp.arange(levels, dtype=jnp.int32)
    masks = (level_ids[:, None, None] < depth_levels[None]).astype(jnp.float32)
    full_mask = jnp.concatenate([masks, masks, masks, masks[:1]], axis=0)
    state = state * full_mask
    columns = jnp.arange(width_y, dtype=jnp.int32)
    for step in range(STEPS):
        lines = all_lines[step]
        onehot = (obs_rows[step][:, None] == columns[None, :]).astype(jnp.float32)
        target = jnp.dot(
            lines.T, onehot, precision=lax.Precision.HIGHEST, preferred_element_type=jnp.float32
        )
        hit = jnp.sum(onehot, axis=0)[None, :]
        state = one_step(state, masks, level_coefs, target, hit)
    return state[None]


def solution(mesh):
    in_specs = (
        P("particle", None, "space", None),
        P(),
        P("space", None),
        P(),
        P(None, "particle", "space"),
        P(),
    )
    out_specs = P("particle", None, "space", None)
    return jax.shard_map(
        per_device, mesh=mesh, in_specs=in_specs, out_specs=out_specs, check_vma=False
    )
```

```python
import functools

import jax
import jax.numpy as jnp
from jax import lax
from jax.experimental import pallas as pl
from jax.experimental.pallas import tpu as pltpu
from jax.sharding import PartitionSpec as P

MESH = pl.DeviceIdType.MESH

STEPS = 3


DT = 0.2
CORIOLIS = 0.5
GRAVITY = 1.0
NUDGE = 0.5


def with_halo(block, sides, width):
    for axis, dim in sides:
        count = lax.axis_size(axis)
        forward = [(i, i + 1) for i in range(count - 1)]
        forward.append((count - 1, 0))
        backward = [(target, source) for source, target in forward]
        low = lax.ppermute(
            lax.slice_in_dim(block, block.shape[dim] - width, None, axis=dim), axis, forward
        )
        high = lax.ppermute(lax.slice_in_dim(block, 0, width, axis=dim), axis, backward)
        block = jnp.concatenate([low, block, high], axis=dim)
    return block


def pad_second(field):
    return jnp.pad(field, [(0, 0)] * (field.ndim - 1) + [(1, 1)])


def gradients(wide):
    center = wide[:, 1:-1]
    east = wide[:, 2:]
    west = wide[:, :-2]
    padded = pad_second(center)
    ddx = (east - west) * 0.5
    ddy = (padded[..., 2:] - padded[..., :-2]) * 0.5
    laplace = east + west + padded[..., 2:] + padded[..., :-2] - 4.0 * center
    return (center, ddx, ddy, laplace)


def widen_state(field):
    return with_halo(field, (("space", 1),), 1)


def widen_surface(field):
    return with_halo(field, (("space", 1),), 1)


def level_terms(coefs):
    thick = coefs[0][:, None, None]
    visc = 0.2 * coefs[1][:, None, None]
    kappa = 0.2 * coefs[2][:, None, None]
    return (thick, visc, kappa)


def finish(center, ddx, ddy, laplace, masks, visc, kappa, grad_x, grad_y, height_two):
    levels = masks.shape[0]
    east_vel = center[:levels]
    north_vel = center[levels : 2 * levels]
    temper = center[2 * levels : 3 * levels]
    east_new = masks * (
        east_vel + DT * (CORIOLIS * north_vel - GRAVITY * grad_x + visc * laplace[:levels])
    )
    north_new = masks * (
        north_vel
        + DT * (-CORIOLIS * east_vel - GRAVITY * grad_y + visc * laplace[levels : 2 * levels])
    )
    temper_new = masks * (
        temper
        + DT
        * (
            kappa * laplace[2 * levels : 3 * levels]
            - east_vel * ddx[2 * levels : 3 * levels]
            - north_vel * ddy[2 * levels : 3 * levels]
        )
    )
    return jnp.concatenate([east_new, north_new, temper_new, height_two[None]], axis=0)


def one_step(state, masks, coefs, target, hit):
    levels = masks.shape[0]
    surface = masks[0]
    center, ddx, ddy, laplace = gradients(widen_state(state))
    height = center[3 * levels]
    thick, visc, kappa = level_terms(coefs)
    spread = ddx[:levels] + ddy[levels : 2 * levels]
    height_one = surface * (height - DT * jnp.sum(thick * masks * spread, axis=0))
    height_two = surface * (height_one + NUDGE * hit * (target - height_one))
    unused, grad_x, grad_y, unused_lap = gradients(widen_surface(height_two[None]))
    return finish(center, ddx, ddy, laplace, masks, visc, kappa, grad_x, grad_y, height_two)


def window(source, grid_cols, rows, cols):
    return (pl.ds((source // grid_cols) * rows, rows), pl.ds((source % grid_cols) * cols, cols))


def exchange_kernel(
    count, grid_cols, anc_ref, ens_ref, alt_ref, out_ref, lines_ref,
    held, outgoing, send1, recv1, send2, recv2, send3, recv3, local,
):
    me = lax.axis_index("particle")
    rows, cols = held.shape[2], held.shape[3]

    barrier = pltpu.get_barrier_semaphore()
    for offset in range(1, count):
        peer = lax.rem(me + offset, count)
        pl.semaphore_signal(barrier, inc=1, device_id={"particle": peer}, device_id_type=MESH)
    pl.semaphore_wait(barrier, count - 1)

    def chunk_of(dest):
        r, c = window(dest, grid_cols, rows, cols)
        return ens_ref.at[:, r, c]

    own = pltpu.make_async_copy(chunk_of(me), held.at[me], local.at[0])
    own.start()
    own_lines = pltpu.make_async_copy(alt_ref, lines_ref.at[me], local.at[1])
    own_lines.start()
    first = []
    for offset in range(1, count):
        peer = lax.rem(me + offset, count)
        copy = pltpu.make_async_remote_copy(
            src_ref=chunk_of(peer), dst_ref=held.at[me], send_sem=send1.at[offset],
            recv_sem=recv1.at[me], device_id={"particle": peer}, device_id_type=MESH,
        )
        copy.start()
        lines = pltpu.make_async_remote_copy(
            src_ref=alt_ref, dst_ref=lines_ref.at[me], send_sem=send3.at[offset],
            recv_sem=recv3.at[me], device_id={"particle": peer}, device_id_type=MESH,
        )
        lines.start()
        first.append((copy, lines))
    own.wait()
    own_lines.wait()
    for offset, (copy, lines) in zip(range(1, count), first):
        sender = lax.rem(me + count - offset, count)
        copy.wait_send()
        lines.wait_send()
        pltpu.make_async_remote_copy(
            src_ref=chunk_of(me), dst_ref=held.at[sender], send_sem=send1.at[offset],
            recv_sem=recv1.at[sender], device_id={"particle": sender}, device_id_type=MESH,
        ).wait_recv()
        pltpu.make_async_remote_copy(
            src_ref=alt_ref, dst_ref=lines_ref.at[sender], send_sem=send3.at[offset],
            recv_sem=recv3.at[sender], device_id={"particle": sender}, device_id_type=MESH,
        ).wait_recv()

    for member in range(count):
        source = jnp.clip(anc_ref[member], 0, count - 1)
        outgoing[member] = held[source]

    r_me, c_me = window(me, grid_cols, rows, cols)
    mine = pltpu.make_async_copy(outgoing.at[me], out_ref.at[:, r_me, c_me], local.at[2])
    mine.start()
    second = []
    for offset in range(1, count):
        peer = lax.rem(me + offset, count)
        copy = pltpu.make_async_remote_copy(
            src_ref=outgoing.at[peer], dst_ref=out_ref.at[:, r_me, c_me],
            send_sem=send2.at[offset], recv_sem=recv2.at[me],
            device_id={"particle": peer}, device_id_type=MESH,
        )
        copy.start()
        second.append(copy)
    mine.wait()
    for offset, copy in zip(range(1, count), second):
        sender = lax.rem(me + count - offset, count)
        r_s, c_s = window(sender, grid_cols, rows, cols)
        copy.wait_send()
        pltpu.make_async_remote_copy(
            src_ref=outgoing.at[me], dst_ref=out_ref.at[:, r_s, c_s],
            send_sem=send2.at[offset], recv_sem=recv2.at[sender],
            device_id={"particle": sender}, device_id_type=MESH,
        ).wait_recv()


def resample(tile, ancestors, altimetry):
    count = lax.axis_size("particle")
    fields, height, width = tile.shape
    grid_rows = 4
    grid_cols = count // grid_rows
    rows, cols = height // grid_rows, width // grid_cols
    sems = pltpu.SemaphoreType.DMA((count,))
    return pl.pallas_call(
        functools.partial(exchange_kernel, count, grid_cols),
        out_shape=(
            jax.ShapeDtypeStruct(tile.shape, tile.dtype),
            jax.ShapeDtypeStruct((count,) + altimetry.shape, altimetry.dtype),
        ),
        in_specs=[
            pl.BlockSpec(memory_space=pltpu.SMEM),
            pl.BlockSpec(memory_space=pl.ANY),
            pl.BlockSpec(memory_space=pltpu.VMEM),
        ],
        out_specs=(
            pl.BlockSpec(memory_space=pl.ANY),
            pl.BlockSpec(memory_space=pltpu.VMEM),
        ),
        scratch_shapes=[
            pltpu.VMEM((count, fields, rows, cols), tile.dtype),
            pltpu.VMEM((count, fields, rows, cols), tile.dtype),
            sems, sems, sems, sems, sems, sems,
            pltpu.SemaphoreType.DMA((3,)),
        ],
        compiler_params=pltpu.CompilerParams(collective_id=0, has_side_effects=True),
    )(ancestors, tile, altimetry)


def wide_step(state, masks, coefs, target, hit):
    levels = masks.shape[0]
    center, ddx, ddy, laplace = gradients(state)
    height = center[3 * levels]
    thick, visc, kappa = level_terms(coefs)
    spread = ddx[:levels] + ddy[levels : 2 * levels]
    surface = masks[0]
    height_one = surface * (height - DT * jnp.sum(thick * masks * spread, axis=0))
    height_two = surface * (height_one + NUDGE * hit * (target - height_one))
    unused, grad_x, grad_y, unused_lap = gradients(height_two[None])
    inner = lambda field: field[:, 1:-1]
    return finish(
        inner(center), inner(ddx), inner(ddy), inner(laplace), inner(masks),
        visc, kappa, grad_x, grad_y, height_two[1:-1],
    )


def per_device(ensemble, ancestors, depth_levels, level_coefs, altimetry, obs_rows):
    levels = level_coefs.shape[1]
    width_y = ensemble.shape[3]
    reach = 2 * STEPS
    state, gathered = resample(ensemble[0], ancestors, altimetry)
    all_lines = jnp.moveaxis(gathered, 0, 1).reshape(
        (altimetry.shape[0], -1) + altimetry.shape[2:]
    )
    state = with_halo(state, (("space", 1),), reach)
    depth = with_halo(depth_levels, (("space", 0),), reach)
    all_lines = with_halo(all_lines, (("space", 2),), reach)
    span = depth.shape[0]
    level_ids = jnp.arange(levels, dtype=jnp.int32)
    masks = (level_ids[:, None, None] < depth[None]).astype(jnp.float32)
    full_mask = jnp.concatenate([masks, masks, masks, masks[:1]], axis=0)
    state = state * full_mask
    columns = jnp.arange(width_y, dtype=jnp.int32)
    for step in range(STEPS):
        low, high = 2 * step + 1, span - 2 * step - 1
        lines = all_lines[step][:, low:high]
        onehot = (obs_rows[step][:, None] == columns[None, :]).astype(jnp.float32)
        target = jnp.dot(
            lines.T, onehot, precision=lax.Precision.HIGHEST, preferred_element_type=jnp.float32
        )
        hit = jnp.sum(onehot, axis=0)[None, :]
        state = wide_step(state, masks[:, low:high], level_coefs, target, hit)
    return state[None]


def solution(mesh):
    in_specs = (
        P("particle", None, "space", None),
        P(),
        P("space", None),
        P(),
        P(None, "particle", "space"),
        P(),
    )
    out_specs = P("particle", None, "space", None)
    return jax.shard_map(
        per_device, mesh=mesh, in_specs=in_specs, out_specs=out_specs, check_vma=False
    )
```

```python
import functools

import jax
import jax.numpy as jnp
from jax import lax
from jax.experimental import pallas as pl
from jax.experimental.pallas import tpu as pltpu
from jax.sharding import PartitionSpec as P

MESH = pl.DeviceIdType.MESH

STEPS = 3


DT = 0.2
CORIOLIS = 0.5
GRAVITY = 1.0
NUDGE = 0.5


def with_halo(block, sides, width):
    for axis, dim in sides:
        count = lax.axis_size(axis)
        forward = [(i, i + 1) for i in range(count - 1)]
        forward.append((count - 1, 0))
        backward = [(target, source) for source, target in forward]
        low = lax.ppermute(
            lax.slice_in_dim(block, block.shape[dim] - width, None, axis=dim), axis, forward
        )
        high = lax.ppermute(lax.slice_in_dim(block, 0, width, axis=dim), axis, backward)
        block = jnp.concatenate([low, block, high], axis=dim)
    return block


def pad_second(field):
    return jnp.pad(field, [(0, 0)] * (field.ndim - 1) + [(1, 1)])


def gradients(wide):
    center = wide[:, 1:-1]
    east = wide[:, 2:]
    west = wide[:, :-2]
    padded = pad_second(center)
    ddx = (east - west) * 0.5
    ddy = (padded[..., 2:] - padded[..., :-2]) * 0.5
    laplace = east + west + padded[..., 2:] + padded[..., :-2] - 4.0 * center
    return (center, ddx, ddy, laplace)


def widen_state(field):
    return with_halo(field, (("space", 1),), 1)


def widen_surface(field):
    return with_halo(field, (("space", 1),), 1)


def level_terms(coefs):
    thick = coefs[0][:, None, None]
    visc = 0.2 * coefs[1][:, None, None]
    kappa = 0.2 * coefs[2][:, None, None]
    return (thick, visc, kappa)


def finish(center, ddx, ddy, laplace, masks, visc, kappa, grad_x, grad_y, height_two):
    levels = masks.shape[0]
    east_vel = center[:levels]
    north_vel = center[levels : 2 * levels]
    temper = center[2 * levels : 3 * levels]
    east_new = masks * (
        east_vel + DT * (CORIOLIS * north_vel - GRAVITY * grad_x + visc * laplace[:levels])
    )
    north_new = masks * (
        north_vel
        + DT * (-CORIOLIS * east_vel - GRAVITY * grad_y + visc * laplace[levels : 2 * levels])
    )
    temper_new = masks * (
        temper
        + DT
        * (
            kappa * laplace[2 * levels : 3 * levels]
            - east_vel * ddx[2 * levels : 3 * levels]
            - north_vel * ddy[2 * levels : 3 * levels]
        )
    )
    return jnp.concatenate([east_new, north_new, temper_new, height_two[None]], axis=0)


def one_step(state, masks, coefs, target, hit):
    levels = masks.shape[0]
    surface = masks[0]
    center, ddx, ddy, laplace = gradients(widen_state(state))
    height = center[3 * levels]
    thick, visc, kappa = level_terms(coefs)
    spread = ddx[:levels] + ddy[levels : 2 * levels]
    height_one = surface * (height - DT * jnp.sum(thick * masks * spread, axis=0))
    height_two = surface * (height_one + NUDGE * hit * (target - height_one))
    unused, grad_x, grad_y, unused_lap = gradients(widen_surface(height_two[None]))
    return finish(center, ddx, ddy, laplace, masks, visc, kappa, grad_x, grad_y, height_two)


def window(source, grid_cols, rows, cols):
    return (pl.ds((source // grid_cols) * rows, rows), pl.ds((source % grid_cols) * cols, cols))


def exchange_kernel(
    count, grid_rows, grid_cols, anc_ref, ens_ref, alt_ref, out_ref, top_ref, bottom_ref, lines_ref,
    held, outgoing, send1, recv1, send2, recv2, send3, recv3, send4, top_sem, bottom_sem, local,
):
    me = lax.axis_index("particle")
    space = lax.axis_index("space")
    spaces = lax.axis_size("space")
    above = lax.rem(space + spaces - 1, spaces)
    below = lax.rem(space + 1, spaces)
    rows, cols = held.shape[2], held.shape[3]
    block_row = me // grid_cols
    block_col = me % grid_cols

    barrier = pltpu.get_barrier_semaphore()
    for offset in range(1, count):
        peer = lax.rem(me + offset, count)
        pl.semaphore_signal(barrier, inc=1, device_id={"particle": peer}, device_id_type=MESH)
    for peer in range(count):
        for side in (above, below):
            pl.semaphore_signal(
                barrier, inc=1, device_id={"particle": peer, "space": side}, device_id_type=MESH
            )
    pl.semaphore_wait(barrier, 3 * count - 1)

    def chunk_of(dest):
        r, c = window(dest, grid_cols, rows, cols)
        return ens_ref.at[:, r, c]

    own = pltpu.make_async_copy(chunk_of(me), held.at[me], local.at[0])
    own.start()
    own_lines = pltpu.make_async_copy(alt_ref, lines_ref.at[me], local.at[1])
    own_lines.start()
    first = []
    for offset in range(1, count):
        peer = lax.rem(me + offset, count)
        copy = pltpu.make_async_remote_copy(
            src_ref=chunk_of(peer), dst_ref=held.at[me], send_sem=send1.at[offset],
            recv_sem=recv1.at[me], device_id={"particle": peer}, device_id_type=MESH,
        )
        copy.start()
        lines = pltpu.make_async_remote_copy(
            src_ref=alt_ref, dst_ref=lines_ref.at[me], send_sem=send3.at[offset],
            recv_sem=recv3.at[me], device_id={"particle": peer}, device_id_type=MESH,
        )
        lines.start()
        first.append((copy, lines))
    own.wait()
    own_lines.wait()
    for offset, (copy, lines) in zip(range(1, count), first):
        sender = lax.rem(me + count - offset, count)
        copy.wait_send()
        lines.wait_send()
        pltpu.make_async_remote_copy(
            src_ref=chunk_of(me), dst_ref=held.at[sender], send_sem=send1.at[offset],
            recv_sem=recv1.at[sender], device_id={"particle": sender}, device_id_type=MESH,
        ).wait_recv()
        pltpu.make_async_remote_copy(
            src_ref=alt_ref, dst_ref=lines_ref.at[sender], send_sem=send3.at[offset],
            recv_sem=recv3.at[sender], device_id={"particle": sender}, device_id_type=MESH,
        ).wait_recv()

    for member in range(count):
        source = jnp.clip(anc_ref[member], 0, count - 1)
        outgoing[member] = held[source]

    r_me, c_me = window(me, grid_cols, rows, cols)
    edge = lambda ref, col: ref.at[:, :, pl.ds(col * cols, cols)]

    def halo_copy(peer, side, target, sem):
        return pltpu.make_async_remote_copy(
            src_ref=outgoing.at[peer], dst_ref=edge(target, block_col),
            send_sem=send4.at[peer], recv_sem=sem.at[block_col],
            device_id={"particle": peer, "space": side}, device_id_type=MESH,
        )

    def send_halo(side, target, sem):
        copies = [halo_copy(peer, side, target, sem) for peer in range(count)]
        for copy in copies:
            copy.start()
        return copies

    @pl.when(block_row == 0)
    def _():
        for copy in send_halo(above, bottom_ref, bottom_sem):
            copy.wait_send()

    @pl.when(block_row == grid_rows - 1)
    def _():
        for copy in send_halo(below, top_ref, top_sem):
            copy.wait_send()

    mine = pltpu.make_async_copy(outgoing.at[me], out_ref.at[:, r_me, c_me], local.at[2])
    mine.start()
    second = []
    for offset in range(1, count):
        peer = lax.rem(me + offset, count)
        copy = pltpu.make_async_remote_copy(
            src_ref=outgoing.at[peer], dst_ref=out_ref.at[:, r_me, c_me],
            send_sem=send2.at[offset], recv_sem=recv2.at[me],
            device_id={"particle": peer}, device_id_type=MESH,
        )
        copy.start()
        second.append(copy)
    mine.wait()
    for offset, copy in zip(range(1, count), second):
        sender = lax.rem(me + count - offset, count)
        r_s, c_s = window(sender, grid_cols, rows, cols)
        copy.wait_send()
        pltpu.make_async_remote_copy(
            src_ref=outgoing.at[me], dst_ref=out_ref.at[:, r_s, c_s],
            send_sem=send2.at[offset], recv_sem=recv2.at[sender],
            device_id={"particle": sender}, device_id_type=MESH,
        ).wait_recv()
    for col in range(grid_cols):
        for target, sem in ((top_ref, top_sem), (bottom_ref, bottom_sem)):
            pltpu.make_async_remote_copy(
                src_ref=outgoing.at[me], dst_ref=edge(target, col), send_sem=send4.at[me],
                recv_sem=sem.at[col], device_id={"particle": me, "space": above},
                device_id_type=MESH,
            ).wait_recv()


def resample(tile, ancestors, altimetry):
    count = lax.axis_size("particle")
    fields, height, width = tile.shape
    grid_rows = 4
    grid_cols = count // grid_rows
    rows, cols = height // grid_rows, width // grid_cols
    sems = pltpu.SemaphoreType.DMA((count,))
    edges = pltpu.SemaphoreType.DMA((grid_cols,))
    return pl.pallas_call(
        functools.partial(exchange_kernel, count, grid_rows, grid_cols),
        out_shape=(
            jax.ShapeDtypeStruct(tile.shape, tile.dtype),
            jax.ShapeDtypeStruct((fields, rows, width), tile.dtype),
            jax.ShapeDtypeStruct((fields, rows, width), tile.dtype),
            jax.ShapeDtypeStruct((count,) + altimetry.shape, altimetry.dtype),
        ),
        in_specs=[
            pl.BlockSpec(memory_space=pltpu.SMEM),
            pl.BlockSpec(memory_space=pl.ANY),
            pl.BlockSpec(memory_space=pltpu.VMEM),
        ],
        out_specs=(
            pl.BlockSpec(memory_space=pl.ANY),
            pl.BlockSpec(memory_space=pl.ANY),
            pl.BlockSpec(memory_space=pl.ANY),
            pl.BlockSpec(memory_space=pltpu.VMEM),
        ),
        scratch_shapes=[
            pltpu.VMEM((count, fields, rows, cols), tile.dtype),
            pltpu.VMEM((count, fields, rows, cols), tile.dtype),
            sems, sems, sems, sems, sems, sems, sems, edges, edges,
            pltpu.SemaphoreType.DMA((3,)),
        ],
        compiler_params=pltpu.CompilerParams(collective_id=0, has_side_effects=True),
    )(ancestors, tile, altimetry)


def wide_step(state, masks, coefs, target, hit):
    levels = masks.shape[0]
    center, ddx, ddy, laplace = gradients(state)
    height = center[3 * levels]
    thick, visc, kappa = level_terms(coefs)
    spread = ddx[:levels] + ddy[levels : 2 * levels]
    surface = masks[0]
    height_one = surface * (height - DT * jnp.sum(thick * masks * spread, axis=0))
    height_two = surface * (height_one + NUDGE * hit * (target - height_one))
    unused, grad_x, grad_y, unused_lap = gradients(height_two[None])
    inner = lambda field: field[:, 1:-1]
    return finish(
        inner(center), inner(ddx), inner(ddy), inner(laplace), inner(masks),
        visc, kappa, grad_x, grad_y, height_two[1:-1],
    )


def per_device(ensemble, ancestors, depth_levels, level_coefs, altimetry, obs_rows):
    levels = level_coefs.shape[1]
    width_y = ensemble.shape[3]
    reach = 2 * STEPS
    depth = with_halo(depth_levels, (("space", 0),), reach)
    wide_lines = with_halo(altimetry, (("space", 2),), reach)
    tile, top, bottom, gathered = resample(ensemble[0], ancestors, wide_lines)
    all_lines = jnp.moveaxis(gathered, 0, 1).reshape(
        (altimetry.shape[0], -1) + wide_lines.shape[2:]
    )
    state = jnp.concatenate(
        [top[:, top.shape[1] - reach :], tile, bottom[:, :reach]], axis=1
    )
    span = depth.shape[0]
    level_ids = jnp.arange(levels, dtype=jnp.int32)
    masks = (level_ids[:, None, None] < depth[None]).astype(jnp.float32)
    full_mask = jnp.concatenate([masks, masks, masks, masks[:1]], axis=0)
    state = state * full_mask
    columns = jnp.arange(width_y, dtype=jnp.int32)
    for step in range(STEPS):
        low, high = 2 * step + 1, span - 2 * step - 1
        lines = all_lines[step][:, low:high]
        onehot = (obs_rows[step][:, None] == columns[None, :]).astype(jnp.float32)
        target = jnp.dot(
            lines.T, onehot, precision=lax.Precision.HIGHEST, preferred_element_type=jnp.float32
        )
        hit = jnp.sum(onehot, axis=0)[None, :]
        state = wide_step(state, masks[:, low:high], level_coefs, target, hit)
    return state[None]


def solution(mesh):
    in_specs = (
        P("particle", None, "space", None),
        P(),
        P("space", None),
        P(),
        P(None, "particle", "space"),
        P(),
    )
    out_specs = P("particle", None, "space", None)
    return jax.shard_map(
        per_device, mesh=mesh, in_specs=in_specs, out_specs=out_specs, check_vma=False
    )
```

```python
import functools

import jax
import jax.numpy as jnp
from jax import lax
from jax.experimental import pallas as pl
from jax.experimental.pallas import tpu as pltpu
from jax.sharding import PartitionSpec as P

MESH = pl.DeviceIdType.MESH

STEPS = 3


DT = 0.2
CORIOLIS = 0.5
GRAVITY = 1.0
NUDGE = 0.5


def with_halo(block, sides, width):
    for axis, dim in sides:
        count = lax.axis_size(axis)
        forward = [(i, i + 1) for i in range(count - 1)]
        forward.append((count - 1, 0))
        backward = [(target, source) for source, target in forward]
        low = lax.ppermute(
            lax.slice_in_dim(block, block.shape[dim] - width, None, axis=dim), axis, forward
        )
        high = lax.ppermute(lax.slice_in_dim(block, 0, width, axis=dim), axis, backward)
        block = jnp.concatenate([low, block, high], axis=dim)
    return block


def pad_second(field):
    return jnp.pad(field, [(0, 0)] * (field.ndim - 1) + [(1, 1)])


def gradients(wide):
    center = wide[:, 1:-1]
    east = wide[:, 2:]
    west = wide[:, :-2]
    padded = pad_second(center)
    ddx = (east - west) * 0.5
    ddy = (padded[..., 2:] - padded[..., :-2]) * 0.5
    laplace = east + west + padded[..., 2:] + padded[..., :-2] - 4.0 * center
    return (center, ddx, ddy, laplace)


def widen_state(field):
    return with_halo(field, (("space", 1),), 1)


def widen_surface(field):
    return with_halo(field, (("space", 1),), 1)


def level_terms(coefs):
    thick = coefs[0][:, None, None]
    visc = 0.2 * coefs[1][:, None, None]
    kappa = 0.2 * coefs[2][:, None, None]
    return (thick, visc, kappa)


def finish(center, ddx, ddy, laplace, masks, visc, kappa, grad_x, grad_y, height_two):
    levels = masks.shape[0]
    east_vel = center[:levels]
    north_vel = center[levels : 2 * levels]
    temper = center[2 * levels : 3 * levels]
    east_new = masks * (
        east_vel + DT * (CORIOLIS * north_vel - GRAVITY * grad_x + visc * laplace[:levels])
    )
    north_new = masks * (
        north_vel
        + DT * (-CORIOLIS * east_vel - GRAVITY * grad_y + visc * laplace[levels : 2 * levels])
    )
    temper_new = masks * (
        temper
        + DT
        * (
            kappa * laplace[2 * levels : 3 * levels]
            - east_vel * ddx[2 * levels : 3 * levels]
            - north_vel * ddy[2 * levels : 3 * levels]
        )
    )
    return jnp.concatenate([east_new, north_new, temper_new, height_two[None]], axis=0)


def one_step(state, masks, coefs, target, hit):
    levels = masks.shape[0]
    surface = masks[0]
    center, ddx, ddy, laplace = gradients(widen_state(state))
    height = center[3 * levels]
    thick, visc, kappa = level_terms(coefs)
    spread = ddx[:levels] + ddy[levels : 2 * levels]
    height_one = surface * (height - DT * jnp.sum(thick * masks * spread, axis=0))
    height_two = surface * (height_one + NUDGE * hit * (target - height_one))
    unused, grad_x, grad_y, unused_lap = gradients(widen_surface(height_two[None]))
    return finish(center, ddx, ddy, laplace, masks, visc, kappa, grad_x, grad_y, height_two)


def window(source, grid_cols, rows, cols):
    return (pl.ds((source // grid_cols) * rows, rows), pl.ds((source % grid_cols) * cols, cols))


def exchange_kernel(
    count, grid_cols, anc_ref, ens_ref, alt_ref, out_ref, lines_ref,
    held, outgoing, send1, recv1, send2, recv2, send3, recv3, local,
):
    me = lax.axis_index("particle")
    rows, cols = held.shape[2], held.shape[3]

    barrier = pltpu.get_barrier_semaphore()
    for offset in range(1, count):
        peer = lax.rem(me + offset, count)
        pl.semaphore_signal(barrier, inc=1, device_id={"particle": peer}, device_id_type=MESH)
    pl.semaphore_wait(barrier, count - 1)

    def chunk_of(dest):
        r, c = window(dest, grid_cols, rows, cols)
        return ens_ref.at[:, r, c]

    own = pltpu.make_async_copy(chunk_of(me), held.at[me], local.at[0])
    own.start()
    own_lines = pltpu.make_async_copy(alt_ref, lines_ref.at[me], local.at[1])
    own_lines.start()
    first = []
    for offset in range(1, count):
        peer = lax.rem(me + offset, count)
        copy = pltpu.make_async_remote_copy(
            src_ref=chunk_of(peer), dst_ref=held.at[me], send_sem=send1.at[offset],
            recv_sem=recv1.at[me], device_id={"particle": peer}, device_id_type=MESH,
        )
        copy.start()
        lines = pltpu.make_async_remote_copy(
            src_ref=alt_ref, dst_ref=lines_ref.at[me], send_sem=send3.at[offset],
            recv_sem=recv3.at[me], device_id={"particle": peer}, device_id_type=MESH,
        )
        lines.start()
        first.append((copy, lines))
    own.wait()
    own_lines.wait()
    for offset, (copy, lines) in zip(range(1, count), first):
        sender = lax.rem(me + count - offset, count)
        copy.wait_send()
        lines.wait_send()
        pltpu.make_async_remote_copy(
            src_ref=chunk_of(me), dst_ref=held.at[sender], send_sem=send1.at[offset],
            recv_sem=recv1.at[sender], device_id={"particle": sender}, device_id_type=MESH,
        ).wait_recv()
        pltpu.make_async_remote_copy(
            src_ref=alt_ref, dst_ref=lines_ref.at[sender], send_sem=send3.at[offset],
            recv_sem=recv3.at[sender], device_id={"particle": sender}, device_id_type=MESH,
        ).wait_recv()

    for member in range(count):
        source = jnp.clip(anc_ref[member], 0, count - 1)
        outgoing[member] = held[source]

    r_me, c_me = window(me, grid_cols, rows, cols)
    mine = pltpu.make_async_copy(outgoing.at[me], out_ref.at[:, r_me, c_me], local.at[2])
    mine.start()
    second = []
    for offset in range(1, count):
        peer = lax.rem(me + offset, count)
        copy = pltpu.make_async_remote_copy(
            src_ref=outgoing.at[peer], dst_ref=out_ref.at[:, r_me, c_me],
            send_sem=send2.at[offset], recv_sem=recv2.at[me],
            device_id={"particle": peer}, device_id_type=MESH,
        )
        copy.start()
        second.append(copy)
    mine.wait()
    for offset, copy in zip(range(1, count), second):
        sender = lax.rem(me + count - offset, count)
        r_s, c_s = window(sender, grid_cols, rows, cols)
        copy.wait_send()
        pltpu.make_async_remote_copy(
            src_ref=outgoing.at[me], dst_ref=out_ref.at[:, r_s, c_s],
            send_sem=send2.at[offset], recv_sem=recv2.at[sender],
            device_id={"particle": sender}, device_id_type=MESH,
        ).wait_recv()


def resample(tile, ancestors, altimetry):
    count = lax.axis_size("particle")
    fields, height, width = tile.shape
    grid_rows = 4
    grid_cols = count // grid_rows
    rows, cols = height // grid_rows, width // grid_cols
    sems = pltpu.SemaphoreType.DMA((count,))
    return pl.pallas_call(
        functools.partial(exchange_kernel, count, grid_cols),
        out_shape=(
            jax.ShapeDtypeStruct(tile.shape, tile.dtype),
            jax.ShapeDtypeStruct((count,) + altimetry.shape, altimetry.dtype),
        ),
        in_specs=[
            pl.BlockSpec(memory_space=pltpu.SMEM),
            pl.BlockSpec(memory_space=pl.ANY),
            pl.BlockSpec(memory_space=pltpu.VMEM),
        ],
        out_specs=(
            pl.BlockSpec(memory_space=pl.ANY),
            pl.BlockSpec(memory_space=pltpu.VMEM),
        ),
        scratch_shapes=[
            pltpu.VMEM((count, fields, rows, cols), tile.dtype),
            pltpu.VMEM((count, fields, rows, cols), tile.dtype),
            sems, sems, sems, sems, sems, sems,
            pltpu.SemaphoreType.DMA((3,)),
        ],
        compiler_params=pltpu.CompilerParams(collective_id=0, has_side_effects=True),
    )(ancestors, tile, altimetry)


def stencil_kernel(coef_ref, tile_ref, aux_ref, top_ref, bottom_ref, hit_ref, out_ref, state, aux):
    fields, rows, width = tile_ref.shape
    extra = aux_ref.shape[0]
    reach = top_ref.shape[1]
    levels = coef_ref.shape[1]
    span = state.shape[1]
    state[:, :reach] = top_ref[:fields]
    state[:, reach : reach + rows] = tile_ref[...]
    state[:, reach + rows :] = bottom_ref[:fields]
    aux[:, :reach] = top_ref[fields:]
    aux[:, reach : reach + rows] = aux_ref[...]
    aux[:, reach + rows :] = bottom_ref[fields:]

    lane = lax.broadcasted_iota(jnp.int32, (span, width), 1)
    first_lane = lane == 0
    last_lane = lane == width - 1

    def east(f):
        return pltpu.roll(f, span - 1, 0)

    def west(f):
        return pltpu.roll(f, 1, 0)

    def north(f):
        return jnp.where(last_lane, 0.0, pltpu.roll(f, width - 1, 1))

    def south(f):
        return jnp.where(first_lane, 0.0, pltpu.roll(f, 1, 1))

    def parts(f):
        e, w, n, s = east(f), west(f), north(f), south(f)
        return (e - w) * 0.5, (n - s) * 0.5, e + w + n + s - 4.0 * f

    depth = aux[extra - 1]
    masks = [(k < depth).astype(jnp.float32) for k in range(levels)]
    surface = masks[0]
    for field in range(fields):
        state[field] = state[field] * masks[field % levels]
    for step in range(STEPS):
        spread = None
        for k in range(levels):
            ddx_u = parts(state[k])[0]
            ddy_v = parts(state[levels + k])[1]
            term = (coef_ref[0, k] * masks[k]) * (ddx_u + ddy_v)
            spread = term if spread is None else spread + term
        height = state[3 * levels]
        height_one = surface * (height - DT * spread)
        hit = hit_ref[step]
        height_two = surface * (height_one + NUDGE * hit * (aux[step] - height_one))
        grad_x, grad_y, unused = parts(height_two)
        for k in range(levels):
            visc = 0.2 * coef_ref[1, k]
            kappa = 0.2 * coef_ref[2, k]
            east_vel = state[k]
            north_vel = state[levels + k]
            temper = state[2 * levels + k]
            unused_x, unused_y, lap_u = parts(east_vel)
            unused_x, unused_y, lap_v = parts(north_vel)
            ddx_t, ddy_t, lap_t = parts(temper)
            state[k] = masks[k] * (
                east_vel + DT * (CORIOLIS * north_vel - grad_x + visc * lap_u)
            )
            state[levels + k] = masks[k] * (
                north_vel + DT * (-CORIOLIS * east_vel - grad_y + visc * lap_v)
            )
            state[2 * levels + k] = masks[k] * (
                temper + DT * (kappa * lap_t - east_vel * ddx_t - north_vel * ddy_t)
            )
        state[3 * levels] = height_two
    out_ref[...] = state[:, reach : reach + rows]


def run_steps(coefs, tile, aux, top, bottom, hits):
    fields, rows, width = tile.shape
    span = rows + 2 * top.shape[1]
    vmem = pl.BlockSpec(memory_space=pltpu.VMEM)
    return pl.pallas_call(
        stencil_kernel,
        out_shape=jax.ShapeDtypeStruct(tile.shape, tile.dtype),
        in_specs=[pl.BlockSpec(memory_space=pltpu.SMEM)] + [vmem] * 5,
        out_specs=vmem,
        scratch_shapes=[
            pltpu.VMEM((fields, span, width), tile.dtype),
            pltpu.VMEM((aux.shape[0], span, width), tile.dtype),
        ],
    )(coefs, tile, aux, top, bottom, hits)


def per_device(ensemble, ancestors, depth_levels, level_coefs, altimetry, obs_rows):
    width_y = ensemble.shape[3]
    reach = 8
    tile, gathered = resample(ensemble[0], ancestors, altimetry)
    all_lines = jnp.moveaxis(gathered, 0, 1).reshape(
        (altimetry.shape[0], -1) + altimetry.shape[2:]
    )
    columns = jnp.arange(width_y, dtype=jnp.int32)
    targets = []
    hits = []
    for step in range(STEPS):
        onehot = (obs_rows[step][:, None] == columns[None, :]).astype(jnp.float32)
        targets.append(
            jnp.dot(
                all_lines[step].T, onehot, precision=lax.Precision.HIGHEST,
                preferred_element_type=jnp.float32,
            )
        )
        hits.append(jnp.sum(onehot, axis=0)[None, :])
    aux = jnp.stack(targets + [depth_levels.astype(jnp.float32)], axis=0)
    count = lax.axis_size("space")
    forward = [(i, (i + 1) % count) for i in range(count)]
    backward = [(target, source) for source, target in forward]
    low = jnp.concatenate([tile[:, :reach], aux[:, :reach]], axis=0)
    high = jnp.concatenate([tile[:, -reach:], aux[:, -reach:]], axis=0)
    top = lax.ppermute(high, "space", forward)
    bottom = lax.ppermute(low, "space", backward)
    state = run_steps(level_coefs, tile, aux, top, bottom, jnp.stack(hits, axis=0))
    return state[None]


def solution(mesh):
    in_specs = (
        P("particle", None, "space", None),
        P(),
        P("space", None),
        P(),
        P(None, "particle", "space"),
        P(),
    )
    out_specs = P("particle", None, "space", None)
    return jax.shard_map(
        per_device, mesh=mesh, in_specs=in_specs, out_specs=out_specs, check_vma=False
    )
```

```python
import functools

import jax
import jax.numpy as jnp
from jax import lax
from jax.experimental import pallas as pl
from jax.experimental.pallas import tpu as pltpu
from jax.sharding import PartitionSpec as P

MESH = pl.DeviceIdType.MESH

STEPS = 3


DT = 0.2
CORIOLIS = 0.5
GRAVITY = 1.0
NUDGE = 0.5


def with_halo(block, sides, width):
    for axis, dim in sides:
        count = lax.axis_size(axis)
        forward = [(i, i + 1) for i in range(count - 1)]
        forward.append((count - 1, 0))
        backward = [(target, source) for source, target in forward]
        low = lax.ppermute(
            lax.slice_in_dim(block, block.shape[dim] - width, None, axis=dim), axis, forward
        )
        high = lax.ppermute(lax.slice_in_dim(block, 0, width, axis=dim), axis, backward)
        block = jnp.concatenate([low, block, high], axis=dim)
    return block


def pad_second(field):
    return jnp.pad(field, [(0, 0)] * (field.ndim - 1) + [(1, 1)])


def gradients(wide):
    center = wide[:, 1:-1]
    east = wide[:, 2:]
    west = wide[:, :-2]
    padded = pad_second(center)
    ddx = (east - west) * 0.5
    ddy = (padded[..., 2:] - padded[..., :-2]) * 0.5
    laplace = east + west + padded[..., 2:] + padded[..., :-2] - 4.0 * center
    return (center, ddx, ddy, laplace)


def widen_state(field):
    return with_halo(field, (("space", 1),), 1)


def widen_surface(field):
    return with_halo(field, (("space", 1),), 1)


def level_terms(coefs):
    thick = coefs[0][:, None, None]
    visc = 0.2 * coefs[1][:, None, None]
    kappa = 0.2 * coefs[2][:, None, None]
    return (thick, visc, kappa)


def finish(center, ddx, ddy, laplace, masks, visc, kappa, grad_x, grad_y, height_two):
    levels = masks.shape[0]
    east_vel = center[:levels]
    north_vel = center[levels : 2 * levels]
    temper = center[2 * levels : 3 * levels]
    east_new = masks * (
        east_vel + DT * (CORIOLIS * north_vel - GRAVITY * grad_x + visc * laplace[:levels])
    )
    north_new = masks * (
        north_vel
        + DT * (-CORIOLIS * east_vel - GRAVITY * grad_y + visc * laplace[levels : 2 * levels])
    )
    temper_new = masks * (
        temper
        + DT
        * (
            kappa * laplace[2 * levels : 3 * levels]
            - east_vel * ddx[2 * levels : 3 * levels]
            - north_vel * ddy[2 * levels : 3 * levels]
        )
    )
    return jnp.concatenate([east_new, north_new, temper_new, height_two[None]], axis=0)


def one_step(state, masks, coefs, target, hit):
    levels = masks.shape[0]
    surface = masks[0]
    center, ddx, ddy, laplace = gradients(widen_state(state))
    height = center[3 * levels]
    thick, visc, kappa = level_terms(coefs)
    spread = ddx[:levels] + ddy[levels : 2 * levels]
    height_one = surface * (height - DT * jnp.sum(thick * masks * spread, axis=0))
    height_two = surface * (height_one + NUDGE * hit * (target - height_one))
    unused, grad_x, grad_y, unused_lap = gradients(widen_surface(height_two[None]))
    return finish(center, ddx, ddy, laplace, masks, visc, kappa, grad_x, grad_y, height_two)


def window(source, grid_cols, rows, cols):
    return (pl.ds((source // grid_cols) * rows, rows), pl.ds((source % grid_cols) * cols, cols))


def exchange_kernel(
    count, grid_cols, groups, anc_ref, ens_ref, alt_ref, out_ref, lines_ref,
    held_a, held_b, outgoing_a, outgoing_b, send1, recv1, send2, recv2, send3, recv3, local,
):
    me = lax.axis_index("particle")
    held = (held_a, held_b)
    outgoing = (outgoing_a, outgoing_b)
    rows, cols = held_a.shape[2], held_a.shape[3]

    barrier = pltpu.get_barrier_semaphore()
    for offset in range(1, count):
        peer = lax.rem(me + offset, count)
        pl.semaphore_signal(barrier, inc=1, device_id={"particle": peer}, device_id_type=MESH)
    pl.semaphore_wait(barrier, count - 1)

    def chunk_of(dest, fields):
        r, c = window(dest, grid_cols, rows, cols)
        return ens_ref.at[fields, r, c]

    def first_copy(group, fields, offset, peer):
        return pltpu.make_async_remote_copy(
            src_ref=chunk_of(peer, fields), dst_ref=held[group].at[me],
            send_sem=send1.at[group, offset], recv_sem=recv1.at[group, me],
            device_id={"particle": peer}, device_id_type=MESH,
        )

    def second_copy(group, fields, offset, peer):
        r_me, c_me = window(me, grid_cols, rows, cols)
        return pltpu.make_async_remote_copy(
            src_ref=outgoing[group].at[peer], dst_ref=out_ref.at[fields, r_me, c_me],
            send_sem=send2.at[group, offset], recv_sem=recv2.at[group, me],
            device_id={"particle": peer}, device_id_type=MESH,
        )

    own_lines = pltpu.make_async_copy(alt_ref, lines_ref.at[me], local.at[0])
    own_lines.start()
    line_copies = []
    for offset in range(1, count):
        peer = lax.rem(me + offset, count)
        lines = pltpu.make_async_remote_copy(
            src_ref=alt_ref, dst_ref=lines_ref.at[me], send_sem=send3.at[offset],
            recv_sem=recv3.at[me], device_id={"particle": peer}, device_id_type=MESH,
        )
        lines.start()
        line_copies.append(lines)

    own_parts = []
    firsts = []
    for group, fields in enumerate(groups):
        own = pltpu.make_async_copy(chunk_of(me, fields), held[group].at[me], local.at[1 + group])
        own.start()
        own_parts.append(own)
        copies = []
        for offset in range(1, count):
            copy = first_copy(group, fields, offset, lax.rem(me + offset, count))
            copy.start()
            copies.append(copy)
        firsts.append(copies)

    seconds = []
    for group, fields in enumerate(groups):
        own_parts[group].wait()
        for offset, copy in zip(range(1, count), firsts[group]):
            sender = lax.rem(me + count - offset, count)
            copy.wait_send()
            pltpu.make_async_remote_copy(
                src_ref=chunk_of(me, fields), dst_ref=held[group].at[sender],
                send_sem=send1.at[group, offset], recv_sem=recv1.at[group, sender],
                device_id={"particle": sender}, device_id_type=MESH,
            ).wait_recv()
        for member in range(count):
            source = jnp.clip(anc_ref[member], 0, count - 1)
            outgoing[group][member] = held[group][source]
        r_me, c_me = window(me, grid_cols, rows, cols)
        mine = pltpu.make_async_copy(
            outgoing[group].at[me], out_ref.at[fields, r_me, c_me], local.at[3 + group]
        )
        mine.start()
        copies = [mine]
        for offset in range(1, count):
            copy = second_copy(group, fields, offset, lax.rem(me + offset, count))
            copy.start()
            copies.append(copy)
        seconds.append(copies)

    own_lines.wait()
    for offset, lines in zip(range(1, count), line_copies):
        sender = lax.rem(me + count - offset, count)
        lines.wait_send()
        pltpu.make_async_remote_copy(
            src_ref=alt_ref, dst_ref=lines_ref.at[sender], send_sem=send3.at[offset],
            recv_sem=recv3.at[sender], device_id={"particle": sender}, device_id_type=MESH,
        ).wait_recv()
    for group, fields in enumerate(groups):
        seconds[group][0].wait()
        for offset, copy in zip(range(1, count), seconds[group][1:]):
            sender = lax.rem(me + count - offset, count)
            r_s, c_s = window(sender, grid_cols, rows, cols)
            copy.wait_send()
            pltpu.make_async_remote_copy(
                src_ref=outgoing[group].at[me], dst_ref=out_ref.at[fields, r_s, c_s],
                send_sem=send2.at[group, offset], recv_sem=recv2.at[group, sender],
                device_id={"particle": sender}, device_id_type=MESH,
            ).wait_recv()


def resample(tile, ancestors, altimetry):
    count = lax.axis_size("particle")
    fields, height, width = tile.shape
    grid_rows = 4
    grid_cols = count // grid_rows
    rows, cols = height // grid_rows, width // grid_cols
    split = (fields + 1) // 2
    groups = (pl.ds(0, split), pl.ds(split, fields - split))
    sems = pltpu.SemaphoreType.DMA((count,))
    grouped = pltpu.SemaphoreType.DMA((len(groups), count))
    return pl.pallas_call(
        functools.partial(exchange_kernel, count, grid_cols, groups),
        out_shape=(
            jax.ShapeDtypeStruct(tile.shape, tile.dtype),
            jax.ShapeDtypeStruct((count,) + altimetry.shape, altimetry.dtype),
        ),
        in_specs=[
            pl.BlockSpec(memory_space=pltpu.SMEM),
            pl.BlockSpec(memory_space=pl.ANY),
            pl.BlockSpec(memory_space=pltpu.VMEM),
        ],
        out_specs=(
            pl.BlockSpec(memory_space=pl.ANY),
            pl.BlockSpec(memory_space=pltpu.VMEM),
        ),
        scratch_shapes=[
            pltpu.VMEM((count, split, rows, cols), tile.dtype),
            pltpu.VMEM((count, fields - split, rows, cols), tile.dtype),
            pltpu.VMEM((count, split, rows, cols), tile.dtype),
            pltpu.VMEM((count, fields - split, rows, cols), tile.dtype),
            grouped, grouped, grouped, grouped, sems, sems,
            pltpu.SemaphoreType.DMA((1 + 2 * len(groups),)),
        ],
        compiler_params=pltpu.CompilerParams(collective_id=0, has_side_effects=True),
    )(ancestors, tile, altimetry)


def stencil_kernel(coef_ref, tile_ref, aux_ref, top_ref, bottom_ref, hit_ref, out_ref, state, aux):
    fields, rows, width = tile_ref.shape
    extra = aux_ref.shape[0]
    reach = top_ref.shape[1]
    levels = coef_ref.shape[1]
    span = state.shape[1]
    state[:, :reach] = top_ref[:fields]
    state[:, reach : reach + rows] = tile_ref[...]
    state[:, reach + rows :] = bottom_ref[:fields]
    aux[:, :reach] = top_ref[fields:]
    aux[:, reach : reach + rows] = aux_ref[...]
    aux[:, reach + rows :] = bottom_ref[fields:]

    lane = lax.broadcasted_iota(jnp.int32, (span, width), 1)
    first_lane = lane == 0
    last_lane = lane == width - 1

    def east(f):
        return pltpu.roll(f, span - 1, 0)

    def west(f):
        return pltpu.roll(f, 1, 0)

    def north(f):
        return jnp.where(last_lane, 0.0, pltpu.roll(f, width - 1, 1))

    def south(f):
        return jnp.where(first_lane, 0.0, pltpu.roll(f, 1, 1))

    def parts(f):
        e, w, n, s = east(f), west(f), north(f), south(f)
        return (e - w) * 0.5, (n - s) * 0.5, e + w + n + s - 4.0 * f

    depth = aux[extra - 1]
    masks = [(k < depth).astype(jnp.float32) for k in range(levels)]
    surface = masks[0]
    for field in range(fields):
        state[field] = state[field] * masks[field % levels]
    for step in range(STEPS):
        spread = None
        for k in range(levels):
            ddx_u = parts(state[k])[0]
            ddy_v = parts(state[levels + k])[1]
            term = (coef_ref[0, k] * masks[k]) * (ddx_u + ddy_v)
            spread = term if spread is None else spread + term
        height = state[3 * levels]
        height_one = surface * (height - DT * spread)
        hit = hit_ref[step]
        height_two = surface * (height_one + NUDGE * hit * (aux[step] - height_one))
        grad_x, grad_y, unused = parts(height_two)
        for k in range(levels):
            visc = 0.2 * coef_ref[1, k]
            kappa = 0.2 * coef_ref[2, k]
            east_vel = state[k]
            north_vel = state[levels + k]
            temper = state[2 * levels + k]
            unused_x, unused_y, lap_u = parts(east_vel)
            unused_x, unused_y, lap_v = parts(north_vel)
            ddx_t, ddy_t, lap_t = parts(temper)
            state[k] = masks[k] * (
                east_vel + DT * (CORIOLIS * north_vel - grad_x + visc * lap_u)
            )
            state[levels + k] = masks[k] * (
                north_vel + DT * (-CORIOLIS * east_vel - grad_y + visc * lap_v)
            )
            state[2 * levels + k] = masks[k] * (
                temper + DT * (kappa * lap_t - east_vel * ddx_t - north_vel * ddy_t)
            )
        state[3 * levels] = height_two
    out_ref[...] = state[:, reach : reach + rows]


def run_steps(coefs, tile, aux, top, bottom, hits):
    fields, rows, width = tile.shape
    span = rows + 2 * top.shape[1]
    vmem = pl.BlockSpec(memory_space=pltpu.VMEM)
    return pl.pallas_call(
        stencil_kernel,
        out_shape=jax.ShapeDtypeStruct(tile.shape, tile.dtype),
        in_specs=[pl.BlockSpec(memory_space=pltpu.SMEM)] + [vmem] * 5,
        out_specs=vmem,
        scratch_shapes=[
            pltpu.VMEM((fields, span, width), tile.dtype),
            pltpu.VMEM((aux.shape[0], span, width), tile.dtype),
        ],
    )(coefs, tile, aux, top, bottom, hits)


def per_device(ensemble, ancestors, depth_levels, level_coefs, altimetry, obs_rows):
    width_y = ensemble.shape[3]
    reach = 8
    tile, gathered = resample(ensemble[0], ancestors, altimetry)
    all_lines = jnp.moveaxis(gathered, 0, 1).reshape(
        (altimetry.shape[0], -1) + altimetry.shape[2:]
    )
    columns = jnp.arange(width_y, dtype=jnp.int32)
    targets = []
    hits = []
    for step in range(STEPS):
        onehot = (obs_rows[step][:, None] == columns[None, :]).astype(jnp.float32)
        targets.append(
            jnp.dot(
                all_lines[step].T, onehot, precision=lax.Precision.HIGHEST,
                preferred_element_type=jnp.float32,
            )
        )
        hits.append(jnp.sum(onehot, axis=0)[None, :])
    aux = jnp.stack(targets + [depth_levels.astype(jnp.float32)], axis=0)
    count = lax.axis_size("space")
    forward = [(i, (i + 1) % count) for i in range(count)]
    backward = [(target, source) for source, target in forward]
    low = jnp.concatenate([tile[:, :reach], aux[:, :reach]], axis=0)
    high = jnp.concatenate([tile[:, -reach:], aux[:, -reach:]], axis=0)
    top = lax.ppermute(high, "space", forward)
    bottom = lax.ppermute(low, "space", backward)
    state = run_steps(level_coefs, tile, aux, top, bottom, jnp.stack(hits, axis=0))
    return state[None]


def solution(mesh):
    in_specs = (
        P("particle", None, "space", None),
        P(),
        P("space", None),
        P(),
        P(None, "particle", "space"),
        P(),
    )
    out_specs = P("particle", None, "space", None)
    return jax.shard_map(
        per_device, mesh=mesh, in_specs=in_specs, out_specs=out_specs, check_vma=False
    )
```

```python
import functools

import jax
import jax.numpy as jnp
from jax import lax
from jax.experimental import pallas as pl
from jax.experimental.pallas import tpu as pltpu
from jax.sharding import PartitionSpec as P

MESH = pl.DeviceIdType.MESH

STEPS = 3


DT = 0.2
CORIOLIS = 0.5
GRAVITY = 1.0
NUDGE = 0.5


def with_halo(block, sides, width):
    for axis, dim in sides:
        count = lax.axis_size(axis)
        forward = [(i, i + 1) for i in range(count - 1)]
        forward.append((count - 1, 0))
        backward = [(target, source) for source, target in forward]
        low = lax.ppermute(
            lax.slice_in_dim(block, block.shape[dim] - width, None, axis=dim), axis, forward
        )
        high = lax.ppermute(lax.slice_in_dim(block, 0, width, axis=dim), axis, backward)
        block = jnp.concatenate([low, block, high], axis=dim)
    return block


def pad_second(field):
    return jnp.pad(field, [(0, 0)] * (field.ndim - 1) + [(1, 1)])


def gradients(wide):
    center = wide[:, 1:-1]
    east = wide[:, 2:]
    west = wide[:, :-2]
    padded = pad_second(center)
    ddx = (east - west) * 0.5
    ddy = (padded[..., 2:] - padded[..., :-2]) * 0.5
    laplace = east + west + padded[..., 2:] + padded[..., :-2] - 4.0 * center
    return (center, ddx, ddy, laplace)


def widen_state(field):
    return with_halo(field, (("space", 1),), 1)


def widen_surface(field):
    return with_halo(field, (("space", 1),), 1)


def level_terms(coefs):
    thick = coefs[0][:, None, None]
    visc = 0.2 * coefs[1][:, None, None]
    kappa = 0.2 * coefs[2][:, None, None]
    return (thick, visc, kappa)


def finish(center, ddx, ddy, laplace, masks, visc, kappa, grad_x, grad_y, height_two):
    levels = masks.shape[0]
    east_vel = center[:levels]
    north_vel = center[levels : 2 * levels]
    temper = center[2 * levels : 3 * levels]
    east_new = masks * (
        east_vel + DT * (CORIOLIS * north_vel - GRAVITY * grad_x + visc * laplace[:levels])
    )
    north_new = masks * (
        north_vel
        + DT * (-CORIOLIS * east_vel - GRAVITY * grad_y + visc * laplace[levels : 2 * levels])
    )
    temper_new = masks * (
        temper
        + DT
        * (
            kappa * laplace[2 * levels : 3 * levels]
            - east_vel * ddx[2 * levels : 3 * levels]
            - north_vel * ddy[2 * levels : 3 * levels]
        )
    )
    return jnp.concatenate([east_new, north_new, temper_new, height_two[None]], axis=0)


def one_step(state, masks, coefs, target, hit):
    levels = masks.shape[0]
    surface = masks[0]
    center, ddx, ddy, laplace = gradients(widen_state(state))
    height = center[3 * levels]
    thick, visc, kappa = level_terms(coefs)
    spread = ddx[:levels] + ddy[levels : 2 * levels]
    height_one = surface * (height - DT * jnp.sum(thick * masks * spread, axis=0))
    height_two = surface * (height_one + NUDGE * hit * (target - height_one))
    unused, grad_x, grad_y, unused_lap = gradients(widen_surface(height_two[None]))
    return finish(center, ddx, ddy, laplace, masks, visc, kappa, grad_x, grad_y, height_two)


def window(source, grid_cols, rows, cols):
    return (pl.ds((source // grid_cols) * rows, rows), pl.ds((source % grid_cols) * cols, cols))


def exchange_kernel(
    count, grid_cols, groups, anc_ref, ens_ref, out_ref,
    held_a, held_b, outgoing_a, outgoing_b, send1, recv1, send2, recv2, local,
):
    me = lax.axis_index("particle")
    held = (held_a, held_b)
    outgoing = (outgoing_a, outgoing_b)
    rows, cols = held_a.shape[2], held_a.shape[3]

    barrier = pltpu.get_barrier_semaphore()
    for offset in range(1, count):
        peer = lax.rem(me + offset, count)
        pl.semaphore_signal(barrier, inc=1, device_id={"particle": peer}, device_id_type=MESH)
    pl.semaphore_wait(barrier, count - 1)

    def chunk_of(dest, fields):
        r, c = window(dest, grid_cols, rows, cols)
        return ens_ref.at[fields, r, c]

    def first_copy(group, fields, offset, peer):
        return pltpu.make_async_remote_copy(
            src_ref=chunk_of(peer, fields), dst_ref=held[group].at[me],
            send_sem=send1.at[group, offset], recv_sem=recv1.at[group, me],
            device_id={"particle": peer}, device_id_type=MESH,
        )

    def second_copy(group, fields, offset, peer):
        r_me, c_me = window(me, grid_cols, rows, cols)
        return pltpu.make_async_remote_copy(
            src_ref=outgoing[group].at[peer], dst_ref=out_ref.at[fields, r_me, c_me],
            send_sem=send2.at[group, offset], recv_sem=recv2.at[group, me],
            device_id={"particle": peer}, device_id_type=MESH,
        )

    own_parts = []
    firsts = []
    for group, fields in enumerate(groups):
        own = pltpu.make_async_copy(chunk_of(me, fields), held[group].at[me], local.at[1 + group])
        own.start()
        own_parts.append(own)
        copies = []
        for offset in range(1, count):
            copy = first_copy(group, fields, offset, lax.rem(me + offset, count))
            copy.start()
            copies.append(copy)
        firsts.append(copies)

    seconds = []
    for group, fields in enumerate(groups):
        own_parts[group].wait()
        for offset, copy in zip(range(1, count), firsts[group]):
            sender = lax.rem(me + count - offset, count)
            copy.wait_send()
            pltpu.make_async_remote_copy(
                src_ref=chunk_of(me, fields), dst_ref=held[group].at[sender],
                send_sem=send1.at[group, offset], recv_sem=recv1.at[group, sender],
                device_id={"particle": sender}, device_id_type=MESH,
            ).wait_recv()
        for member in range(count):
            source = jnp.clip(anc_ref[member], 0, count - 1)
            outgoing[group][member] = held[group][source]
        r_me, c_me = window(me, grid_cols, rows, cols)
        mine = pltpu.make_async_copy(
            outgoing[group].at[me], out_ref.at[fields, r_me, c_me], local.at[3 + group]
        )
        mine.start()
        copies = [mine]
        for offset in range(1, count):
            copy = second_copy(group, fields, offset, lax.rem(me + offset, count))
            copy.start()
            copies.append(copy)
        seconds.append(copies)

    for group, fields in enumerate(groups):
        seconds[group][0].wait()
        for offset, copy in zip(range(1, count), seconds[group][1:]):
            sender = lax.rem(me + count - offset, count)
            r_s, c_s = window(sender, grid_cols, rows, cols)
            copy.wait_send()
            pltpu.make_async_remote_copy(
                src_ref=outgoing[group].at[me], dst_ref=out_ref.at[fields, r_s, c_s],
                send_sem=send2.at[group, offset], recv_sem=recv2.at[group, sender],
                device_id={"particle": sender}, device_id_type=MESH,
            ).wait_recv()


def gather_kernel(count, alt_ref, lines_ref, send, recv, local):
    me = lax.axis_index("particle")
    barrier = pltpu.get_barrier_semaphore()
    for offset in range(1, count):
        peer = lax.rem(me + offset, count)
        pl.semaphore_signal(barrier, inc=1, device_id={"particle": peer}, device_id_type=MESH)
    pl.semaphore_wait(barrier, count - 1)
    own = pltpu.make_async_copy(alt_ref, lines_ref.at[me], local.at[0])
    own.start()
    copies = []
    for offset in range(1, count):
        peer = lax.rem(me + offset, count)
        copy = pltpu.make_async_remote_copy(
            src_ref=alt_ref, dst_ref=lines_ref.at[me], send_sem=send.at[offset],
            recv_sem=recv.at[me], device_id={"particle": peer}, device_id_type=MESH,
        )
        copy.start()
        copies.append(copy)
    own.wait()
    for offset, copy in zip(range(1, count), copies):
        sender = lax.rem(me + count - offset, count)
        copy.wait_send()
        pltpu.make_async_remote_copy(
            src_ref=alt_ref, dst_ref=lines_ref.at[sender], send_sem=send.at[offset],
            recv_sem=recv.at[sender], device_id={"particle": sender}, device_id_type=MESH,
        ).wait_recv()


def gather_lines(altimetry):
    count = lax.axis_size("particle")
    sems = pltpu.SemaphoreType.DMA((count,))
    return pl.pallas_call(
        functools.partial(gather_kernel, count),
        out_shape=jax.ShapeDtypeStruct((count,) + altimetry.shape, altimetry.dtype),
        in_specs=[pl.BlockSpec(memory_space=pltpu.VMEM)],
        out_specs=pl.BlockSpec(memory_space=pltpu.VMEM),
        scratch_shapes=[sems, sems, pltpu.SemaphoreType.DMA((1,))],
        compiler_params=pltpu.CompilerParams(collective_id=1, has_side_effects=True),
    )(altimetry)


def resample(tile, ancestors):
    count = lax.axis_size("particle")
    fields, height, width = tile.shape
    grid_rows = 4
    grid_cols = count // grid_rows
    rows, cols = height // grid_rows, width // grid_cols
    split = (fields + 1) // 2
    groups = (pl.ds(0, split), pl.ds(split, fields - split))
    grouped = pltpu.SemaphoreType.DMA((len(groups), count))
    return pl.pallas_call(
        functools.partial(exchange_kernel, count, grid_cols, groups),
        out_shape=jax.ShapeDtypeStruct(tile.shape, tile.dtype),
        in_specs=[
            pl.BlockSpec(memory_space=pltpu.SMEM),
            pl.BlockSpec(memory_space=pl.ANY),
        ],
        out_specs=pl.BlockSpec(memory_space=pl.ANY),
        scratch_shapes=[
            pltpu.VMEM((count, split, rows, cols), tile.dtype),
            pltpu.VMEM((count, fields - split, rows, cols), tile.dtype),
            pltpu.VMEM((count, split, rows, cols), tile.dtype),
            pltpu.VMEM((count, fields - split, rows, cols), tile.dtype),
            grouped, grouped, grouped, grouped,
            pltpu.SemaphoreType.DMA((1 + 2 * len(groups),)),
        ],
        compiler_params=pltpu.CompilerParams(collective_id=0, has_side_effects=True),
    )(ancestors, tile)


def stencil_kernel(coef_ref, tile_ref, aux_ref, top_ref, bottom_ref, hit_ref, out_ref, state, aux):
    fields, rows, width = tile_ref.shape
    extra = aux_ref.shape[0]
    reach = top_ref.shape[1]
    levels = coef_ref.shape[1]
    span = state.shape[1]
    state[:, :reach] = top_ref[:fields]
    state[:, reach : reach + rows] = tile_ref[...]
    state[:, reach + rows :] = bottom_ref[:fields]
    aux[:, :reach] = top_ref[fields:]
    aux[:, reach : reach + rows] = aux_ref[...]
    aux[:, reach + rows :] = bottom_ref[fields:]

    lane = lax.broadcasted_iota(jnp.int32, (span, width), 1)
    first_lane = lane == 0
    last_lane = lane == width - 1

    def east(f):
        return pltpu.roll(f, span - 1, 0)

    def west(f):
        return pltpu.roll(f, 1, 0)

    def north(f):
        return jnp.where(last_lane, 0.0, pltpu.roll(f, width - 1, 1))

    def south(f):
        return jnp.where(first_lane, 0.0, pltpu.roll(f, 1, 1))

    def parts(f):
        e, w, n, s = east(f), west(f), north(f), south(f)
        return (e - w) * 0.5, (n - s) * 0.5, e + w + n + s - 4.0 * f

    depth = aux[extra - 1]
    masks = [(k < depth).astype(jnp.float32) for k in range(levels)]
    surface = masks[0]
    for field in range(fields):
        state[field] = state[field] * masks[field % levels]
    for step in range(STEPS):
        spread = None
        for k in range(levels):
            ddx_u = parts(state[k])[0]
            ddy_v = parts(state[levels + k])[1]
            term = (coef_ref[0, k] * masks[k]) * (ddx_u + ddy_v)
            spread = term if spread is None else spread + term
        height = state[3 * levels]
        height_one = surface * (height - DT * spread)
        hit = hit_ref[step]
        height_two = surface * (height_one + NUDGE * hit * (aux[step] - height_one))
        grad_x, grad_y, unused = parts(height_two)
        for k in range(levels):
            visc = 0.2 * coef_ref[1, k]
            kappa = 0.2 * coef_ref[2, k]
            east_vel = state[k]
            north_vel = state[levels + k]
            temper = state[2 * levels + k]
            unused_x, unused_y, lap_u = parts(east_vel)
            unused_x, unused_y, lap_v = parts(north_vel)
            ddx_t, ddy_t, lap_t = parts(temper)
            state[k] = masks[k] * (
                east_vel + DT * (CORIOLIS * north_vel - grad_x + visc * lap_u)
            )
            state[levels + k] = masks[k] * (
                north_vel + DT * (-CORIOLIS * east_vel - grad_y + visc * lap_v)
            )
            state[2 * levels + k] = masks[k] * (
                temper + DT * (kappa * lap_t - east_vel * ddx_t - north_vel * ddy_t)
            )
        state[3 * levels] = height_two
    out_ref[...] = state[:, reach : reach + rows]


def run_steps(coefs, tile, aux, top, bottom, hits):
    fields, rows, width = tile.shape
    span = rows + 2 * top.shape[1]
    vmem = pl.BlockSpec(memory_space=pltpu.VMEM)
    return pl.pallas_call(
        stencil_kernel,
        out_shape=jax.ShapeDtypeStruct(tile.shape, tile.dtype),
        in_specs=[pl.BlockSpec(memory_space=pltpu.SMEM)] + [vmem] * 5,
        out_specs=vmem,
        scratch_shapes=[
            pltpu.VMEM((fields, span, width), tile.dtype),
            pltpu.VMEM((aux.shape[0], span, width), tile.dtype),
        ],
    )(coefs, tile, aux, top, bottom, hits)


def per_device(ensemble, ancestors, depth_levels, level_coefs, altimetry, obs_rows):
    width_y = ensemble.shape[3]
    reach = 8
    member = ensemble[0]
    fields, rows = member.shape[0], member.shape[1]
    depth = depth_levels.astype(jnp.float32)[None]
    count = lax.axis_size("space")
    forward = [(i, (i + 1) % count) for i in range(count)]
    backward = [(target, source) for source, target in forward]
    low = jnp.concatenate([member[:, :reach], depth[:, :reach]], axis=0)
    high = jnp.concatenate([member[:, -reach:], depth[:, -reach:]], axis=0)
    top_in = lax.ppermute(high, "space", forward)
    bottom_in = lax.ppermute(low, "space", backward)
    wide_lines = with_halo(altimetry, (("space", 2),), reach)
    gathered = gather_lines(wide_lines)
    all_lines = jnp.moveaxis(gathered, 0, 1).reshape(
        (altimetry.shape[0], -1) + wide_lines.shape[2:]
    )
    columns = jnp.arange(width_y, dtype=jnp.int32)
    targets = []
    hits = []
    for step in range(STEPS):
        onehot = (obs_rows[step][:, None] == columns[None, :]).astype(jnp.float32)
        targets.append(
            jnp.dot(
                all_lines[step].T, onehot, precision=lax.Precision.HIGHEST,
                preferred_element_type=jnp.float32,
            )
        )
        hits.append(jnp.sum(onehot, axis=0)[None, :])
    targets = jnp.stack(targets, axis=0)
    aux = jnp.concatenate([targets[:, reach : reach + rows], depth], axis=0)
    top = jnp.concatenate([top_in[:fields], targets[:, :reach], top_in[fields:]], axis=0)
    bottom = jnp.concatenate(
        [bottom_in[:fields], targets[:, reach + rows :], bottom_in[fields:]], axis=0
    )
    result = run_steps(level_coefs, member, aux, top, bottom, jnp.stack(hits, axis=0))
    return resample(result, ancestors)[None]


def solution(mesh):
    in_specs = (
        P("particle", None, "space", None),
        P(),
        P("space", None),
        P(),
        P(None, "particle", "space"),
        P(),
    )
    out_specs = P("particle", None, "space", None)
    return jax.shard_map(
        per_device, mesh=mesh, in_specs=in_specs, out_specs=out_specs, check_vma=False
    )
```

```python
import functools

import jax
import jax.numpy as jnp
from jax import lax
from jax.experimental import pallas as pl
from jax.experimental.pallas import tpu as pltpu
from jax.sharding import PartitionSpec as P

MESH = pl.DeviceIdType.MESH

STEPS = 3


DT = 0.2
CORIOLIS = 0.5
GRAVITY = 1.0
NUDGE = 0.5


def with_halo(block, sides, width):
    for axis, dim in sides:
        count = lax.axis_size(axis)
        forward = [(i, i + 1) for i in range(count - 1)]
        forward.append((count - 1, 0))
        backward = [(target, source) for source, target in forward]
        low = lax.ppermute(
            lax.slice_in_dim(block, block.shape[dim] - width, None, axis=dim), axis, forward
        )
        high = lax.ppermute(lax.slice_in_dim(block, 0, width, axis=dim), axis, backward)
        block = jnp.concatenate([low, block, high], axis=dim)
    return block


def pad_second(field):
    return jnp.pad(field, [(0, 0)] * (field.ndim - 1) + [(1, 1)])


def gradients(wide):
    center = wide[:, 1:-1]
    east = wide[:, 2:]
    west = wide[:, :-2]
    padded = pad_second(center)
    ddx = (east - west) * 0.5
    ddy = (padded[..., 2:] - padded[..., :-2]) * 0.5
    laplace = east + west + padded[..., 2:] + padded[..., :-2] - 4.0 * center
    return (center, ddx, ddy, laplace)


def widen_state(field):
    return with_halo(field, (("space", 1),), 1)


def widen_surface(field):
    return with_halo(field, (("space", 1),), 1)


def level_terms(coefs):
    thick = coefs[0][:, None, None]
    visc = 0.2 * coefs[1][:, None, None]
    kappa = 0.2 * coefs[2][:, None, None]
    return (thick, visc, kappa)


def finish(center, ddx, ddy, laplace, masks, visc, kappa, grad_x, grad_y, height_two):
    levels = masks.shape[0]
    east_vel = center[:levels]
    north_vel = center[levels : 2 * levels]
    temper = center[2 * levels : 3 * levels]
    east_new = masks * (
        east_vel + DT * (CORIOLIS * north_vel - GRAVITY * grad_x + visc * laplace[:levels])
    )
    north_new = masks * (
        north_vel
        + DT * (-CORIOLIS * east_vel - GRAVITY * grad_y + visc * laplace[levels : 2 * levels])
    )
    temper_new = masks * (
        temper
        + DT
        * (
            kappa * laplace[2 * levels : 3 * levels]
            - east_vel * ddx[2 * levels : 3 * levels]
            - north_vel * ddy[2 * levels : 3 * levels]
        )
    )
    return jnp.concatenate([east_new, north_new, temper_new, height_two[None]], axis=0)


def one_step(state, masks, coefs, target, hit):
    levels = masks.shape[0]
    surface = masks[0]
    center, ddx, ddy, laplace = gradients(widen_state(state))
    height = center[3 * levels]
    thick, visc, kappa = level_terms(coefs)
    spread = ddx[:levels] + ddy[levels : 2 * levels]
    height_one = surface * (height - DT * jnp.sum(thick * masks * spread, axis=0))
    height_two = surface * (height_one + NUDGE * hit * (target - height_one))
    unused, grad_x, grad_y, unused_lap = gradients(widen_surface(height_two[None]))
    return finish(center, ddx, ddy, laplace, masks, visc, kappa, grad_x, grad_y, height_two)


def window(source, grid_cols, rows, cols):
    return (pl.ds((source // grid_cols) * rows, rows), pl.ds((source % grid_cols) * cols, cols))


def exchange_kernel(
    count, grid_cols, groups, reach, anc_ref, ens_ref, alt_ref, depth_ref,
    out_ref, top_ref, bottom_ref, lines_ref, depth_top_ref, depth_bottom_ref,
    held_a, held_b, outgoing_a, outgoing_b, alt_near,
    send1, recv1, send2, recv2, send3, recv3, edge_send, edge_recv, local,
):
    me = lax.axis_index("particle")
    space = lax.axis_index("space")
    spaces = lax.axis_size("space")
    above = lax.rem(space + spaces - 1, spaces)
    below = lax.rem(space + 1, spaces)
    held = (held_a, held_b)
    outgoing = (outgoing_a, outgoing_b)
    rows, cols = held_a.shape[2], held_a.shape[3]
    height = out_ref.shape[1]

    barrier = pltpu.get_barrier_semaphore()
    for offset in range(1, count):
        peer = lax.rem(me + offset, count)
        pl.semaphore_signal(barrier, inc=1, device_id={"particle": peer}, device_id_type=MESH)
    for side in (above, below):
        pl.semaphore_signal(barrier, inc=1, device_id={"space": side}, device_id_type=MESH)
    pl.semaphore_wait(barrier, count + 1)

    def neighbour_copy(src, dst, slot, side):
        return pltpu.make_async_remote_copy(
            src_ref=src, dst_ref=dst, send_sem=edge_send.at[slot], recv_sem=edge_recv.at[slot],
            device_id={"space": side}, device_id_type=MESH,
        )

    early = [
        neighbour_copy(depth_ref.at[pl.ds(0, reach)], depth_bottom_ref, 0, above),
        neighbour_copy(depth_ref.at[pl.ds(height - reach, reach)], depth_top_ref, 1, below),
        neighbour_copy(alt_ref, alt_near.at[1], 2, above),
        neighbour_copy(alt_ref, alt_near.at[0], 3, below),
    ]
    for copy in early:
        copy.start()

    def chunk_of(dest, fields):
        r, c = window(dest, grid_cols, rows, cols)
        return ens_ref.at[fields, r, c]

    def first_copy(group, fields, offset, peer):
        return pltpu.make_async_remote_copy(
            src_ref=chunk_of(peer, fields), dst_ref=held[group].at[me],
            send_sem=send1.at[group, offset], recv_sem=recv1.at[group, me],
            device_id={"particle": peer}, device_id_type=MESH,
        )

    def second_copy(group, fields, offset, peer):
        r_me, c_me = window(me, grid_cols, rows, cols)
        return pltpu.make_async_remote_copy(
            src_ref=outgoing[group].at[peer], dst_ref=out_ref.at[fields, r_me, c_me],
            send_sem=send2.at[group, offset], recv_sem=recv2.at[group, me],
            device_id={"particle": peer}, device_id_type=MESH,
        )

    own_parts = []
    firsts = []
    for group, fields in enumerate(groups):
        own = pltpu.make_async_copy(chunk_of(me, fields), held[group].at[me], local.at[1 + group])
        own.start()
        own_parts.append(own)
        copies = []
        for offset in range(1, count):
            copy = first_copy(group, fields, offset, lax.rem(me + offset, count))
            copy.start()
            copies.append(copy)
        firsts.append(copies)

    for copy in early:
        copy.wait()
    pieces = (alt_ref, alt_near.at[0], alt_near.at[1])
    own_lines = []
    line_copies = []
    for kind, piece in enumerate(pieces):
        own = pltpu.make_async_copy(piece, lines_ref.at[kind, me], local.at[5 + kind])
        own.start()
        own_lines.append(own)
        for offset in range(1, count):
            peer = lax.rem(me + offset, count)
            lines = pltpu.make_async_remote_copy(
                src_ref=piece, dst_ref=lines_ref.at[kind, me], send_sem=send3.at[kind, offset],
                recv_sem=recv3.at[kind, me], device_id={"particle": peer}, device_id_type=MESH,
            )
            lines.start()
            line_copies.append((kind, offset, piece, lines))

    seconds = []
    for group, fields in enumerate(groups):
        own_parts[group].wait()
        for offset, copy in zip(range(1, count), firsts[group]):
            sender = lax.rem(me + count - offset, count)
            copy.wait_send()
            pltpu.make_async_remote_copy(
                src_ref=chunk_of(me, fields), dst_ref=held[group].at[sender],
                send_sem=send1.at[group, offset], recv_sem=recv1.at[group, sender],
                device_id={"particle": sender}, device_id_type=MESH,
            ).wait_recv()
        for member in range(count):
            source = jnp.clip(anc_ref[member], 0, count - 1)
            outgoing[group][member] = held[group][source]
        r_me, c_me = window(me, grid_cols, rows, cols)
        mine = pltpu.make_async_copy(
            outgoing[group].at[me], out_ref.at[fields, r_me, c_me], local.at[3 + group]
        )
        mine.start()
        copies = [mine]
        for offset in range(1, count):
            copy = second_copy(group, fields, offset, lax.rem(me + offset, count))
            copy.start()
            copies.append(copy)
        seconds.append(copies)

    for own in own_lines:
        own.wait()
    for kind, offset, piece, lines in line_copies:
        sender = lax.rem(me + count - offset, count)
        lines.wait_send()
        pltpu.make_async_remote_copy(
            src_ref=piece, dst_ref=lines_ref.at[kind, sender], send_sem=send3.at[kind, offset],
            recv_sem=recv3.at[kind, sender], device_id={"particle": sender}, device_id_type=MESH,
        ).wait_recv()
    for group, fields in enumerate(groups):
        seconds[group][0].wait()
        for offset, copy in zip(range(1, count), seconds[group][1:]):
            sender = lax.rem(me + count - offset, count)
            r_s, c_s = window(sender, grid_cols, rows, cols)
            copy.wait_send()
            pltpu.make_async_remote_copy(
                src_ref=outgoing[group].at[me], dst_ref=out_ref.at[fields, r_s, c_s],
                send_sem=send2.at[group, offset], recv_sem=recv2.at[group, sender],
                device_id={"particle": sender}, device_id_type=MESH,
            ).wait_recv()

    late = [
        neighbour_copy(out_ref.at[:, pl.ds(0, reach)], bottom_ref, 4, above),
        neighbour_copy(out_ref.at[:, pl.ds(height - reach, reach)], top_ref, 5, below),
    ]
    for copy in late:
        copy.start()
    for copy in late:
        copy.wait()


def resample(tile, ancestors, altimetry, depth, reach):
    count = lax.axis_size("particle")
    fields, height, width = tile.shape
    grid_rows = 4
    grid_cols = count // grid_rows
    rows, cols = height // grid_rows, width // grid_cols
    split = (fields + 1) // 2
    groups = (pl.ds(0, split), pl.ds(split, fields - split))
    grouped = pltpu.SemaphoreType.DMA((len(groups), count))
    any_space = pl.BlockSpec(memory_space=pl.ANY)
    vmem = pl.BlockSpec(memory_space=pltpu.VMEM)
    return pl.pallas_call(
        functools.partial(exchange_kernel, count, grid_cols, groups, reach),
        out_shape=(
            jax.ShapeDtypeStruct(tile.shape, tile.dtype),
            jax.ShapeDtypeStruct((fields, reach, width), tile.dtype),
            jax.ShapeDtypeStruct((fields, reach, width), tile.dtype),
            jax.ShapeDtypeStruct((3, count) + altimetry.shape, altimetry.dtype),
            jax.ShapeDtypeStruct((reach, width), depth.dtype),
            jax.ShapeDtypeStruct((reach, width), depth.dtype),
        ),
        in_specs=[pl.BlockSpec(memory_space=pltpu.SMEM), any_space, vmem, any_space],
        out_specs=(any_space, any_space, any_space, vmem, any_space, any_space),
        scratch_shapes=[
            pltpu.VMEM((count, split, rows, cols), tile.dtype),
            pltpu.VMEM((count, fields - split, rows, cols), tile.dtype),
            pltpu.VMEM((count, split, rows, cols), tile.dtype),
            pltpu.VMEM((count, fields - split, rows, cols), tile.dtype),
            pltpu.VMEM((2,) + altimetry.shape, altimetry.dtype),
            grouped, grouped, grouped, grouped,
            pltpu.SemaphoreType.DMA((3, count)),
            pltpu.SemaphoreType.DMA((3, count)),
            pltpu.SemaphoreType.DMA((6,)),
            pltpu.SemaphoreType.DMA((6,)),
            pltpu.SemaphoreType.DMA((8,)),
        ],
        compiler_params=pltpu.CompilerParams(collective_id=0, has_side_effects=True),
    )(ancestors, tile, altimetry, depth)


def stencil_kernel(coef_ref, tile_ref, aux_ref, top_ref, bottom_ref, hit_ref, out_ref, state, aux):
    fields, rows, width = tile_ref.shape
    extra = aux_ref.shape[0]
    reach = top_ref.shape[1]
    levels = coef_ref.shape[1]
    span = state.shape[1]
    state[:, :reach] = top_ref[:fields]
    state[:, reach : reach + rows] = tile_ref[...]
    state[:, reach + rows :] = bottom_ref[:fields]
    aux[:, :reach] = top_ref[fields:]
    aux[:, reach : reach + rows] = aux_ref[...]
    aux[:, reach + rows :] = bottom_ref[fields:]

    lane = lax.broadcasted_iota(jnp.int32, (span, width), 1)
    first_lane = lane == 0
    last_lane = lane == width - 1

    def east(f):
        return pltpu.roll(f, span - 1, 0)

    def west(f):
        return pltpu.roll(f, 1, 0)

    def north(f):
        return jnp.where(last_lane, 0.0, pltpu.roll(f, width - 1, 1))

    def south(f):
        return jnp.where(first_lane, 0.0, pltpu.roll(f, 1, 1))

    def parts(f):
        e, w, n, s = east(f), west(f), north(f), south(f)
        return (e - w) * 0.5, (n - s) * 0.5, e + w + n + s - 4.0 * f

    depth = aux[extra - 1]
    masks = [(k < depth).astype(jnp.float32) for k in range(levels)]
    surface = masks[0]
    for field in range(fields):
        state[field] = state[field] * masks[field % levels]
    for step in range(STEPS):
        spread = None
        for k in range(levels):
            ddx_u = parts(state[k])[0]
            ddy_v = parts(state[levels + k])[1]
            term = (coef_ref[0, k] * masks[k]) * (ddx_u + ddy_v)
            spread = term if spread is None else spread + term
        height = state[3 * levels]
        height_one = surface * (height - DT * spread)
        hit = hit_ref[step]
        height_two = surface * (height_one + NUDGE * hit * (aux[step] - height_one))
        grad_x, grad_y, unused = parts(height_two)
        for k in range(levels):
            visc = 0.2 * coef_ref[1, k]
            kappa = 0.2 * coef_ref[2, k]
            east_vel = state[k]
            north_vel = state[levels + k]
            temper = state[2 * levels + k]
            unused_x, unused_y, lap_u = parts(east_vel)
            unused_x, unused_y, lap_v = parts(north_vel)
            ddx_t, ddy_t, lap_t = parts(temper)
            state[k] = masks[k] * (
                east_vel + DT * (CORIOLIS * north_vel - grad_x + visc * lap_u)
            )
            state[levels + k] = masks[k] * (
                north_vel + DT * (-CORIOLIS * east_vel - grad_y + visc * lap_v)
            )
            state[2 * levels + k] = masks[k] * (
                temper + DT * (kappa * lap_t - east_vel * ddx_t - north_vel * ddy_t)
            )
        state[3 * levels] = height_two
    out_ref[...] = state[:, reach : reach + rows]


def run_steps(coefs, tile, aux, top, bottom, hits):
    fields, rows, width = tile.shape
    span = rows + 2 * top.shape[1]
    vmem = pl.BlockSpec(memory_space=pltpu.VMEM)
    return pl.pallas_call(
        stencil_kernel,
        out_shape=jax.ShapeDtypeStruct(tile.shape, tile.dtype),
        in_specs=[pl.BlockSpec(memory_space=pltpu.SMEM)] + [vmem] * 5,
        out_specs=vmem,
        scratch_shapes=[
            pltpu.VMEM((fields, span, width), tile.dtype),
            pltpu.VMEM((aux.shape[0], span, width), tile.dtype),
        ],
    )(coefs, tile, aux, top, bottom, hits)


def per_device(ensemble, ancestors, depth_levels, level_coefs, altimetry, obs_rows):
    width_y = ensemble.shape[3]
    reach = 8
    depth = depth_levels.astype(jnp.float32)
    tile, top, bottom, gathered, depth_top, depth_bottom = resample(
        ensemble[0], ancestors, altimetry, depth, reach
    )
    fields, rows = tile.shape[0], tile.shape[1]
    own_lines, from_above, from_below = (
        jnp.moveaxis(piece, 0, 1).reshape((altimetry.shape[0], -1) + altimetry.shape[2:])
        for piece in gathered
    )
    all_lines = jnp.concatenate(
        [from_above[..., -reach:], own_lines, from_below[..., :reach]], axis=-1
    )
    columns = jnp.arange(width_y, dtype=jnp.int32)
    targets = []
    hits = []
    for step in range(STEPS):
        onehot = (obs_rows[step][:, None] == columns[None, :]).astype(jnp.float32)
        targets.append(
            jnp.dot(
                all_lines[step].T, onehot, precision=lax.Precision.HIGHEST,
                preferred_element_type=jnp.float32,
            )
        )
        hits.append(jnp.sum(onehot, axis=0)[None, :])
    targets = jnp.stack(targets, axis=0)
    aux = jnp.concatenate([targets[:, reach : reach + rows], depth[None]], axis=0)
    top = jnp.concatenate([top, targets[:, :reach], depth_top[None]], axis=0)
    bottom = jnp.concatenate([bottom, targets[:, reach + rows :], depth_bottom[None]], axis=0)
    state = run_steps(level_coefs, tile, aux, top, bottom, jnp.stack(hits, axis=0))
    return state[None]


def solution(mesh):
    in_specs = (
        P("particle", None, "space", None),
        P(),
        P("space", None),
        P(),
        P(None, "particle", "space"),
        P(),
    )
    out_specs = P("particle", None, "space", None)
    return jax.shard_map(
        per_device, mesh=mesh, in_specs=in_specs, out_specs=out_specs, check_vma=False
    )
```

```python
import functools

import jax
import jax.numpy as jnp
from jax import lax
from jax.experimental import pallas as pl
from jax.experimental.pallas import tpu as pltpu
from jax.sharding import PartitionSpec as P

MESH = pl.DeviceIdType.MESH

STEPS = 3


DT = 0.2
CORIOLIS = 0.5
GRAVITY = 1.0
NUDGE = 0.5


def with_halo(block, sides, width):
    for axis, dim in sides:
        count = lax.axis_size(axis)
        forward = [(i, i + 1) for i in range(count - 1)]
        forward.append((count - 1, 0))
        backward = [(target, source) for source, target in forward]
        low = lax.ppermute(
            lax.slice_in_dim(block, block.shape[dim] - width, None, axis=dim), axis, forward
        )
        high = lax.ppermute(lax.slice_in_dim(block, 0, width, axis=dim), axis, backward)
        block = jnp.concatenate([low, block, high], axis=dim)
    return block


def pad_second(field):
    return jnp.pad(field, [(0, 0)] * (field.ndim - 1) + [(1, 1)])


def gradients(wide):
    center = wide[:, 1:-1]
    east = wide[:, 2:]
    west = wide[:, :-2]
    padded = pad_second(center)
    ddx = (east - west) * 0.5
    ddy = (padded[..., 2:] - padded[..., :-2]) * 0.5
    laplace = east + west + padded[..., 2:] + padded[..., :-2] - 4.0 * center
    return (center, ddx, ddy, laplace)


def widen_state(field):
    return with_halo(field, (("space", 1),), 1)


def widen_surface(field):
    return with_halo(field, (("space", 1),), 1)


def level_terms(coefs):
    thick = coefs[0][:, None, None]
    visc = 0.2 * coefs[1][:, None, None]
    kappa = 0.2 * coefs[2][:, None, None]
    return (thick, visc, kappa)


def finish(center, ddx, ddy, laplace, masks, visc, kappa, grad_x, grad_y, height_two):
    levels = masks.shape[0]
    east_vel = center[:levels]
    north_vel = center[levels : 2 * levels]
    temper = center[2 * levels : 3 * levels]
    east_new = masks * (
        east_vel + DT * (CORIOLIS * north_vel - GRAVITY * grad_x + visc * laplace[:levels])
    )
    north_new = masks * (
        north_vel
        + DT * (-CORIOLIS * east_vel - GRAVITY * grad_y + visc * laplace[levels : 2 * levels])
    )
    temper_new = masks * (
        temper
        + DT
        * (
            kappa * laplace[2 * levels : 3 * levels]
            - east_vel * ddx[2 * levels : 3 * levels]
            - north_vel * ddy[2 * levels : 3 * levels]
        )
    )
    return jnp.concatenate([east_new, north_new, temper_new, height_two[None]], axis=0)


def one_step(state, masks, coefs, target, hit):
    levels = masks.shape[0]
    surface = masks[0]
    center, ddx, ddy, laplace = gradients(widen_state(state))
    height = center[3 * levels]
    thick, visc, kappa = level_terms(coefs)
    spread = ddx[:levels] + ddy[levels : 2 * levels]
    height_one = surface * (height - DT * jnp.sum(thick * masks * spread, axis=0))
    height_two = surface * (height_one + NUDGE * hit * (target - height_one))
    unused, grad_x, grad_y, unused_lap = gradients(widen_surface(height_two[None]))
    return finish(center, ddx, ddy, laplace, masks, visc, kappa, grad_x, grad_y, height_two)


def window(source, grid_cols, rows, cols):
    return (pl.ds((source // grid_cols) * rows, rows), pl.ds((source % grid_cols) * cols, cols))


def exchange_kernel(
    count, grid_cols, groups, reach, anc_ref, ens_ref, alt_ref, depth_ref,
    out_ref, top_ref, bottom_ref, lines_ref, depth_top_ref, depth_bottom_ref,
    held_a, held_b, outgoing_a, outgoing_b, alt_near,
    send1, recv1, send2, recv2, send3, recv3, edge_send, edge_recv, local,
):
    me = lax.axis_index("particle")
    space = lax.axis_index("space")
    spaces = lax.axis_size("space")
    above = lax.rem(space + spaces - 1, spaces)
    below = lax.rem(space + 1, spaces)
    held = (held_a, held_b)
    outgoing = (outgoing_a, outgoing_b)
    rows, cols = held_a.shape[2], held_a.shape[3]
    height = out_ref.shape[1]

    barrier = pltpu.get_barrier_semaphore()
    for offset in range(1, count):
        peer = lax.rem(me + offset, count)
        pl.semaphore_signal(barrier, inc=1, device_id={"particle": peer}, device_id_type=MESH)
    for side in (above, below):
        pl.semaphore_signal(barrier, inc=1, device_id={"space": side}, device_id_type=MESH)
    pl.semaphore_wait(barrier, count + 1)

    def neighbour_copy(src, dst, slot, side):
        return pltpu.make_async_remote_copy(
            src_ref=src, dst_ref=dst, send_sem=edge_send.at[slot], recv_sem=edge_recv.at[slot],
            device_id={"space": side}, device_id_type=MESH,
        )

    early = [
        neighbour_copy(depth_ref.at[pl.ds(0, reach)], depth_bottom_ref, 0, above),
        neighbour_copy(depth_ref.at[pl.ds(height - reach, reach)], depth_top_ref, 1, below),
        neighbour_copy(alt_ref, alt_near.at[1], 2, above),
        neighbour_copy(alt_ref, alt_near.at[0], 3, below),
    ]
    for copy in early:
        copy.start()

    def chunk_of(dest, fields):
        r, c = window(dest, grid_cols, rows, cols)
        return ens_ref.at[fields, r, c]

    def first_copy(group, fields, offset, peer):
        return pltpu.make_async_remote_copy(
            src_ref=chunk_of(peer, fields), dst_ref=held[group].at[me],
            send_sem=send1.at[group, offset], recv_sem=recv1.at[group, me],
            device_id={"particle": peer}, device_id_type=MESH,
        )

    def second_copy(group, fields, offset, peer):
        r_me, c_me = window(me, grid_cols, rows, cols)
        return pltpu.make_async_remote_copy(
            src_ref=outgoing[group].at[peer], dst_ref=out_ref.at[fields, r_me, c_me],
            send_sem=send2.at[group, offset], recv_sem=recv2.at[group, me],
            device_id={"particle": peer}, device_id_type=MESH,
        )

    own_parts = []
    firsts = []
    for group, fields in enumerate(groups):
        own = pltpu.make_async_copy(chunk_of(me, fields), held[group].at[me], local.at[1 + group])
        own.start()
        own_parts.append(own)
        copies = []
        for offset in range(1, count):
            copy = first_copy(group, fields, offset, lax.rem(me + offset, count))
            copy.start()
            copies.append(copy)
        firsts.append(copies)

    for copy in early:
        copy.wait()
    pieces = (alt_ref, alt_near.at[0], alt_near.at[1])
    own_lines = []
    line_copies = []
    for kind, piece in enumerate(pieces):
        own = pltpu.make_async_copy(piece, lines_ref.at[kind, me], local.at[5 + kind])
        own.start()
        own_lines.append(own)
        for offset in range(1, count):
            peer = lax.rem(me + offset, count)
            lines = pltpu.make_async_remote_copy(
                src_ref=piece, dst_ref=lines_ref.at[kind, me], send_sem=send3.at[kind, offset],
                recv_sem=recv3.at[kind, me], device_id={"particle": peer}, device_id_type=MESH,
            )
            lines.start()
            line_copies.append((kind, offset, piece, lines))

    seconds = []
    for group, fields in enumerate(groups):
        own_parts[group].wait()
        for offset, copy in zip(range(1, count), firsts[group]):
            sender = lax.rem(me + count - offset, count)
            copy.wait_send()
            pltpu.make_async_remote_copy(
                src_ref=chunk_of(me, fields), dst_ref=held[group].at[sender],
                send_sem=send1.at[group, offset], recv_sem=recv1.at[group, sender],
                device_id={"particle": sender}, device_id_type=MESH,
            ).wait_recv()
        for member in range(count):
            source = jnp.clip(anc_ref[member], 0, count - 1)
            outgoing[group][member] = held[group][source]
        r_me, c_me = window(me, grid_cols, rows, cols)
        mine = pltpu.make_async_copy(
            outgoing[group].at[me], out_ref.at[fields, r_me, c_me], local.at[3 + group]
        )
        mine.start()
        copies = [mine]
        for offset in range(1, count):
            copy = second_copy(group, fields, offset, lax.rem(me + offset, count))
            copy.start()
            copies.append(copy)
        seconds.append(copies)

    for own in own_lines:
        own.wait()
    for kind, offset, piece, lines in line_copies:
        sender = lax.rem(me + count - offset, count)
        lines.wait_send()
        pltpu.make_async_remote_copy(
            src_ref=piece, dst_ref=lines_ref.at[kind, sender], send_sem=send3.at[kind, offset],
            recv_sem=recv3.at[kind, sender], device_id={"particle": sender}, device_id_type=MESH,
        ).wait_recv()
    late = []
    for group, fields in enumerate(groups):
        seconds[group][0].wait()
        for offset, copy in zip(range(1, count), seconds[group][1:]):
            sender = lax.rem(me + count - offset, count)
            r_s, c_s = window(sender, grid_cols, rows, cols)
            copy.wait_send()
            pltpu.make_async_remote_copy(
                src_ref=outgoing[group].at[me], dst_ref=out_ref.at[fields, r_s, c_s],
                send_sem=send2.at[group, offset], recv_sem=recv2.at[group, sender],
                device_id={"particle": sender}, device_id_type=MESH,
            ).wait_recv()
        edges = [
            neighbour_copy(
                out_ref.at[fields, pl.ds(0, reach)], bottom_ref.at[fields], 4 + 2 * group, above
            ),
            neighbour_copy(
                out_ref.at[fields, pl.ds(height - reach, reach)], top_ref.at[fields],
                5 + 2 * group, below,
            ),
        ]
        for copy in edges:
            copy.start()
        late.extend(edges)
    for copy in late:
        copy.wait()


def resample(tile, ancestors, altimetry, depth, reach):
    count = lax.axis_size("particle")
    fields, height, width = tile.shape
    grid_rows = 4
    grid_cols = count // grid_rows
    rows, cols = height // grid_rows, width // grid_cols
    split = (fields + 1) // 2
    groups = (pl.ds(0, split), pl.ds(split, fields - split))
    grouped = pltpu.SemaphoreType.DMA((len(groups), count))
    any_space = pl.BlockSpec(memory_space=pl.ANY)
    vmem = pl.BlockSpec(memory_space=pltpu.VMEM)
    return pl.pallas_call(
        functools.partial(exchange_kernel, count, grid_cols, groups, reach),
        out_shape=(
            jax.ShapeDtypeStruct(tile.shape, tile.dtype),
            jax.ShapeDtypeStruct((fields, reach, width), tile.dtype),
            jax.ShapeDtypeStruct((fields, reach, width), tile.dtype),
            jax.ShapeDtypeStruct((3, count) + altimetry.shape, altimetry.dtype),
            jax.ShapeDtypeStruct((reach, width), depth.dtype),
            jax.ShapeDtypeStruct((reach, width), depth.dtype),
        ),
        in_specs=[pl.BlockSpec(memory_space=pltpu.SMEM), any_space, vmem, any_space],
        out_specs=(any_space, any_space, any_space, vmem, any_space, any_space),
        scratch_shapes=[
            pltpu.VMEM((count, split, rows, cols), tile.dtype),
            pltpu.VMEM((count, fields - split, rows, cols), tile.dtype),
            pltpu.VMEM((count, split, rows, cols), tile.dtype),
            pltpu.VMEM((count, fields - split, rows, cols), tile.dtype),
            pltpu.VMEM((2,) + altimetry.shape, altimetry.dtype),
            grouped, grouped, grouped, grouped,
            pltpu.SemaphoreType.DMA((3, count)),
            pltpu.SemaphoreType.DMA((3, count)),
            pltpu.SemaphoreType.DMA((4 + 2 * len(groups),)),
            pltpu.SemaphoreType.DMA((4 + 2 * len(groups),)),
            pltpu.SemaphoreType.DMA((8,)),
        ],
        compiler_params=pltpu.CompilerParams(collective_id=0, has_side_effects=True),
    )(ancestors, tile, altimetry, depth)


def stencil_kernel(coef_ref, tile_ref, aux_ref, top_ref, bottom_ref, hit_ref, out_ref, state, aux):
    fields, rows, width = tile_ref.shape
    extra = aux_ref.shape[0]
    reach = top_ref.shape[1]
    levels = coef_ref.shape[1]
    span = state.shape[1]
    state[:, :reach] = top_ref[:fields]
    state[:, reach : reach + rows] = tile_ref[...]
    state[:, reach + rows :] = bottom_ref[:fields]
    aux[:, :reach] = top_ref[fields:]
    aux[:, reach : reach + rows] = aux_ref[...]
    aux[:, reach + rows :] = bottom_ref[fields:]

    lane = lax.broadcasted_iota(jnp.int32, (span, width), 1)
    first_lane = lane == 0
    last_lane = lane == width - 1

    def east(f):
        return pltpu.roll(f, span - 1, 0)

    def west(f):
        return pltpu.roll(f, 1, 0)

    def north(f):
        return jnp.where(last_lane, 0.0, pltpu.roll(f, width - 1, 1))

    def south(f):
        return jnp.where(first_lane, 0.0, pltpu.roll(f, 1, 1))

    def parts(f):
        e, w, n, s = east(f), west(f), north(f), south(f)
        return (e - w) * 0.5, (n - s) * 0.5, e + w + n + s - 4.0 * f

    depth = aux[extra - 1]
    masks = [(k < depth).astype(jnp.float32) for k in range(levels)]
    surface = masks[0]
    for field in range(fields):
        state[field] = state[field] * masks[field % levels]
    for step in range(STEPS):
        spread = None
        for k in range(levels):
            ddx_u = parts(state[k])[0]
            ddy_v = parts(state[levels + k])[1]
            term = (coef_ref[0, k] * masks[k]) * (ddx_u + ddy_v)
            spread = term if spread is None else spread + term
        height = state[3 * levels]
        height_one = surface * (height - DT * spread)
        hit = hit_ref[step]
        height_two = surface * (height_one + NUDGE * hit * (aux[step] - height_one))
        grad_x, grad_y, unused = parts(height_two)
        for k in range(levels):
            visc = 0.2 * coef_ref[1, k]
            kappa = 0.2 * coef_ref[2, k]
            east_vel = state[k]
            north_vel = state[levels + k]
            temper = state[2 * levels + k]
            unused_x, unused_y, lap_u = parts(east_vel)
            unused_x, unused_y, lap_v = parts(north_vel)
            ddx_t, ddy_t, lap_t = parts(temper)
            state[k] = masks[k] * (
                east_vel + DT * (CORIOLIS * north_vel - grad_x + visc * lap_u)
            )
            state[levels + k] = masks[k] * (
                north_vel + DT * (-CORIOLIS * east_vel - grad_y + visc * lap_v)
            )
            state[2 * levels + k] = masks[k] * (
                temper + DT * (kappa * lap_t - east_vel * ddx_t - north_vel * ddy_t)
            )
        state[3 * levels] = height_two
    out_ref[...] = state[:, reach : reach + rows]


def run_steps(coefs, tile, aux, top, bottom, hits):
    fields, rows, width = tile.shape
    span = rows + 2 * top.shape[1]
    vmem = pl.BlockSpec(memory_space=pltpu.VMEM)
    return pl.pallas_call(
        stencil_kernel,
        out_shape=jax.ShapeDtypeStruct(tile.shape, tile.dtype),
        in_specs=[pl.BlockSpec(memory_space=pltpu.SMEM)] + [vmem] * 5,
        out_specs=vmem,
        scratch_shapes=[
            pltpu.VMEM((fields, span, width), tile.dtype),
            pltpu.VMEM((aux.shape[0], span, width), tile.dtype),
        ],
    )(coefs, tile, aux, top, bottom, hits)


def per_device(ensemble, ancestors, depth_levels, level_coefs, altimetry, obs_rows):
    width_y = ensemble.shape[3]
    reach = 8
    depth = depth_levels.astype(jnp.float32)
    tile, top, bottom, gathered, depth_top, depth_bottom = resample(
        ensemble[0], ancestors, altimetry, depth, reach
    )
    fields, rows = tile.shape[0], tile.shape[1]
    own_lines, from_above, from_below = (
        jnp.moveaxis(piece, 0, 1).reshape((altimetry.shape[0], -1) + altimetry.shape[2:])
        for piece in gathered
    )
    all_lines = jnp.concatenate(
        [from_above[..., -reach:], own_lines, from_below[..., :reach]], axis=-1
    )
    columns = jnp.arange(width_y, dtype=jnp.int32)
    targets = []
    hits = []
    for step in range(STEPS):
        onehot = (obs_rows[step][:, None] == columns[None, :]).astype(jnp.float32)
        targets.append(
            jnp.dot(
                all_lines[step].T, onehot, precision=lax.Precision.HIGHEST,
                preferred_element_type=jnp.float32,
            )
        )
        hits.append(jnp.sum(onehot, axis=0)[None, :])
    targets = jnp.stack(targets, axis=0)
    aux = jnp.concatenate([targets[:, reach : reach + rows], depth[None]], axis=0)
    top = jnp.concatenate([top, targets[:, :reach], depth_top[None]], axis=0)
    bottom = jnp.concatenate([bottom, targets[:, reach + rows :], depth_bottom[None]], axis=0)
    state = run_steps(level_coefs, tile, aux, top, bottom, jnp.stack(hits, axis=0))
    return state[None]


def solution(mesh):
    in_specs = (
        P("particle", None, "space", None),
        P(),
        P("space", None),
        P(),
        P(None, "particle", "space"),
        P(),
    )
    out_specs = P("particle", None, "space", None)
    return jax.shard_map(
        per_device, mesh=mesh, in_specs=in_specs, out_specs=out_specs, check_vma=False
    )
```

```python
import functools

import jax
import jax.numpy as jnp
from jax import lax
from jax.experimental import pallas as pl
from jax.experimental.pallas import tpu as pltpu
from jax.sharding import PartitionSpec as P

MESH = pl.DeviceIdType.MESH

STEPS = 3


DT = 0.2
CORIOLIS = 0.5
GRAVITY = 1.0
NUDGE = 0.5


def with_halo(block, sides, width):
    for axis, dim in sides:
        count = lax.axis_size(axis)
        forward = [(i, i + 1) for i in range(count - 1)]
        forward.append((count - 1, 0))
        backward = [(target, source) for source, target in forward]
        low = lax.ppermute(
            lax.slice_in_dim(block, block.shape[dim] - width, None, axis=dim), axis, forward
        )
        high = lax.ppermute(lax.slice_in_dim(block, 0, width, axis=dim), axis, backward)
        block = jnp.concatenate([low, block, high], axis=dim)
    return block


def pad_second(field):
    return jnp.pad(field, [(0, 0)] * (field.ndim - 1) + [(1, 1)])


def gradients(wide):
    center = wide[:, 1:-1]
    east = wide[:, 2:]
    west = wide[:, :-2]
    padded = pad_second(center)
    ddx = (east - west) * 0.5
    ddy = (padded[..., 2:] - padded[..., :-2]) * 0.5
    laplace = east + west + padded[..., 2:] + padded[..., :-2] - 4.0 * center
    return (center, ddx, ddy, laplace)


def widen_state(field):
    return with_halo(field, (("space", 1),), 1)


def widen_surface(field):
    return with_halo(field, (("space", 1),), 1)


def level_terms(coefs):
    thick = coefs[0][:, None, None]
    visc = 0.2 * coefs[1][:, None, None]
    kappa = 0.2 * coefs[2][:, None, None]
    return (thick, visc, kappa)


def finish(center, ddx, ddy, laplace, masks, visc, kappa, grad_x, grad_y, height_two):
    levels = masks.shape[0]
    east_vel = center[:levels]
    north_vel = center[levels : 2 * levels]
    temper = center[2 * levels : 3 * levels]
    east_new = masks * (
        east_vel + DT * (CORIOLIS * north_vel - GRAVITY * grad_x + visc * laplace[:levels])
    )
    north_new = masks * (
        north_vel
        + DT * (-CORIOLIS * east_vel - GRAVITY * grad_y + visc * laplace[levels : 2 * levels])
    )
    temper_new = masks * (
        temper
        + DT
        * (
            kappa * laplace[2 * levels : 3 * levels]
            - east_vel * ddx[2 * levels : 3 * levels]
            - north_vel * ddy[2 * levels : 3 * levels]
        )
    )
    return jnp.concatenate([east_new, north_new, temper_new, height_two[None]], axis=0)


def one_step(state, masks, coefs, target, hit):
    levels = masks.shape[0]
    surface = masks[0]
    center, ddx, ddy, laplace = gradients(widen_state(state))
    height = center[3 * levels]
    thick, visc, kappa = level_terms(coefs)
    spread = ddx[:levels] + ddy[levels : 2 * levels]
    height_one = surface * (height - DT * jnp.sum(thick * masks * spread, axis=0))
    height_two = surface * (height_one + NUDGE * hit * (target - height_one))
    unused, grad_x, grad_y, unused_lap = gradients(widen_surface(height_two[None]))
    return finish(center, ddx, ddy, laplace, masks, visc, kappa, grad_x, grad_y, height_two)


def window(source, grid_cols, rows, cols):
    return (pl.ds((source // grid_cols) * rows, rows), pl.ds((source % grid_cols) * cols, cols))


def exchange_kernel(
    count, grid_cols, groups, anc_ref, ens_ref, alt_ref, out_ref, lines_ref, *scratch,
):
    me = lax.axis_index("particle")
    held = scratch[: len(groups)]
    outgoing = scratch[len(groups) : 2 * len(groups)]
    send1, recv1, send2, recv2, send3, recv3, local = scratch[2 * len(groups) :]
    rows, cols = held[0].shape[2], held[0].shape[3]

    barrier = pltpu.get_barrier_semaphore()
    for offset in range(1, count):
        peer = lax.rem(me + offset, count)
        pl.semaphore_signal(barrier, inc=1, device_id={"particle": peer}, device_id_type=MESH)
    pl.semaphore_wait(barrier, count - 1)

    def chunk_of(dest, fields):
        r, c = window(dest, grid_cols, rows, cols)
        return ens_ref.at[fields, r, c]

    def first_copy(group, fields, offset, peer):
        return pltpu.make_async_remote_copy(
            src_ref=chunk_of(peer, fields), dst_ref=held[group].at[me],
            send_sem=send1.at[group, offset], recv_sem=recv1.at[group, me],
            device_id={"particle": peer}, device_id_type=MESH,
        )

    def second_copy(group, fields, offset, peer):
        r_me, c_me = window(me, grid_cols, rows, cols)
        return pltpu.make_async_remote_copy(
            src_ref=outgoing[group].at[peer], dst_ref=out_ref.at[fields, r_me, c_me],
            send_sem=send2.at[group, offset], recv_sem=recv2.at[group, me],
            device_id={"particle": peer}, device_id_type=MESH,
        )

    own_lines = pltpu.make_async_copy(alt_ref, lines_ref.at[me], local.at[0])
    own_lines.start()
    line_copies = []
    for offset in range(1, count):
        peer = lax.rem(me + offset, count)
        lines = pltpu.make_async_remote_copy(
            src_ref=alt_ref, dst_ref=lines_ref.at[me], send_sem=send3.at[offset],
            recv_sem=recv3.at[me], device_id={"particle": peer}, device_id_type=MESH,
        )
        lines.start()
        line_copies.append(lines)

    own_parts = []
    firsts = []
    for group, fields in enumerate(groups):
        own = pltpu.make_async_copy(chunk_of(me, fields), held[group].at[me], local.at[1 + group])
        own.start()
        own_parts.append(own)
        copies = []
        for offset in range(1, count):
            copy = first_copy(group, fields, offset, lax.rem(me + offset, count))
            copy.start()
            copies.append(copy)
        firsts.append(copies)

    seconds = []
    for group, fields in enumerate(groups):
        own_parts[group].wait()
        for offset, copy in zip(range(1, count), firsts[group]):
            sender = lax.rem(me + count - offset, count)
            copy.wait_send()
            pltpu.make_async_remote_copy(
                src_ref=chunk_of(me, fields), dst_ref=held[group].at[sender],
                send_sem=send1.at[group, offset], recv_sem=recv1.at[group, sender],
                device_id={"particle": sender}, device_id_type=MESH,
            ).wait_recv()
        for member in range(count):
            source = jnp.clip(anc_ref[member], 0, count - 1)
            outgoing[group][member] = held[group][source]
        r_me, c_me = window(me, grid_cols, rows, cols)
        mine = pltpu.make_async_copy(
            outgoing[group].at[me], out_ref.at[fields, r_me, c_me], local.at[1 + len(groups) + group]
        )
        mine.start()
        copies = [mine]
        for offset in range(1, count):
            copy = second_copy(group, fields, offset, lax.rem(me + offset, count))
            copy.start()
            copies.append(copy)
        seconds.append(copies)

    own_lines.wait()
    for offset, lines in zip(range(1, count), line_copies):
        sender = lax.rem(me + count - offset, count)
        lines.wait_send()
        pltpu.make_async_remote_copy(
            src_ref=alt_ref, dst_ref=lines_ref.at[sender], send_sem=send3.at[offset],
            recv_sem=recv3.at[sender], device_id={"particle": sender}, device_id_type=MESH,
        ).wait_recv()
    for group, fields in enumerate(groups):
        seconds[group][0].wait()
        for offset, copy in zip(range(1, count), seconds[group][1:]):
            sender = lax.rem(me + count - offset, count)
            r_s, c_s = window(sender, grid_cols, rows, cols)
            copy.wait_send()
            pltpu.make_async_remote_copy(
                src_ref=outgoing[group].at[me], dst_ref=out_ref.at[fields, r_s, c_s],
                send_sem=send2.at[group, offset], recv_sem=recv2.at[group, sender],
                device_id={"particle": sender}, device_id_type=MESH,
            ).wait_recv()


def resample(tile, ancestors, altimetry):
    count = lax.axis_size("particle")
    fields, height, width = tile.shape
    grid_rows = 4
    grid_cols = count // grid_rows
    rows, cols = height // grid_rows, width // grid_cols
    parts = 4
    sizes = [fields // parts + (1 if g < fields % parts else 0) for g in range(parts)]
    starts = [sum(sizes[:g]) for g in range(parts)]
    groups = tuple(pl.ds(start, size) for start, size in zip(starts, sizes))
    buffers = [pltpu.VMEM((count, size, rows, cols), tile.dtype) for size in sizes]
    sems = pltpu.SemaphoreType.DMA((count,))
    grouped = pltpu.SemaphoreType.DMA((len(groups), count))
    return pl.pallas_call(
        functools.partial(exchange_kernel, count, grid_cols, groups),
        out_shape=(
            jax.ShapeDtypeStruct(tile.shape, tile.dtype),
            jax.ShapeDtypeStruct((count,) + altimetry.shape, altimetry.dtype),
        ),
        in_specs=[
            pl.BlockSpec(memory_space=pltpu.SMEM),
            pl.BlockSpec(memory_space=pl.ANY),
            pl.BlockSpec(memory_space=pltpu.VMEM),
        ],
        out_specs=(
            pl.BlockSpec(memory_space=pl.ANY),
            pl.BlockSpec(memory_space=pltpu.VMEM),
        ),
        scratch_shapes=[
            *buffers,
            *buffers,
            grouped, grouped, grouped, grouped, sems, sems,
            pltpu.SemaphoreType.DMA((1 + 2 * len(groups),)),
        ],
        compiler_params=pltpu.CompilerParams(collective_id=0, has_side_effects=True),
    )(ancestors, tile, altimetry)


def stencil_kernel(coef_ref, tile_ref, aux_ref, top_ref, bottom_ref, hit_ref, out_ref, state, aux):
    fields, rows, width = tile_ref.shape
    extra = aux_ref.shape[0]
    reach = top_ref.shape[1]
    levels = coef_ref.shape[1]
    span = state.shape[1]
    state[:, :reach] = top_ref[:fields]
    state[:, reach : reach + rows] = tile_ref[...]
    state[:, reach + rows :] = bottom_ref[:fields]
    aux[:, :reach] = top_ref[fields:]
    aux[:, reach : reach + rows] = aux_ref[...]
    aux[:, reach + rows :] = bottom_ref[fields:]

    lane = lax.broadcasted_iota(jnp.int32, (span, width), 1)
    first_lane = lane == 0
    last_lane = lane == width - 1

    def east(f):
        return pltpu.roll(f, span - 1, 0)

    def west(f):
        return pltpu.roll(f, 1, 0)

    def north(f):
        return jnp.where(last_lane, 0.0, pltpu.roll(f, width - 1, 1))

    def south(f):
        return jnp.where(first_lane, 0.0, pltpu.roll(f, 1, 1))

    def parts(f):
        e, w, n, s = east(f), west(f), north(f), south(f)
        return (e - w) * 0.5, (n - s) * 0.5, e + w + n + s - 4.0 * f

    depth = aux[extra - 1]
    masks = [(k < depth).astype(jnp.float32) for k in range(levels)]
    surface = masks[0]
    for field in range(fields):
        state[field] = state[field] * masks[field % levels]
    for step in range(STEPS):
        spread = None
        for k in range(levels):
            ddx_u = parts(state[k])[0]
            ddy_v = parts(state[levels + k])[1]
            term = (coef_ref[0, k] * masks[k]) * (ddx_u + ddy_v)
            spread = term if spread is None else spread + term
        height = state[3 * levels]
        height_one = surface * (height - DT * spread)
        hit = hit_ref[step]
        height_two = surface * (height_one + NUDGE * hit * (aux[step] - height_one))
        grad_x, grad_y, unused = parts(height_two)
        for k in range(levels):
            visc = 0.2 * coef_ref[1, k]
            kappa = 0.2 * coef_ref[2, k]
            east_vel = state[k]
            north_vel = state[levels + k]
            temper = state[2 * levels + k]
            unused_x, unused_y, lap_u = parts(east_vel)
            unused_x, unused_y, lap_v = parts(north_vel)
            ddx_t, ddy_t, lap_t = parts(temper)
            state[k] = masks[k] * (
                east_vel + DT * (CORIOLIS * north_vel - grad_x + visc * lap_u)
            )
            state[levels + k] = masks[k] * (
                north_vel + DT * (-CORIOLIS * east_vel - grad_y + visc * lap_v)
            )
            state[2 * levels + k] = masks[k] * (
                temper + DT * (kappa * lap_t - east_vel * ddx_t - north_vel * ddy_t)
            )
        state[3 * levels] = height_two
    out_ref[...] = state[:, reach : reach + rows]


def run_steps(coefs, tile, aux, top, bottom, hits):
    fields, rows, width = tile.shape
    span = rows + 2 * top.shape[1]
    vmem = pl.BlockSpec(memory_space=pltpu.VMEM)
    return pl.pallas_call(
        stencil_kernel,
        out_shape=jax.ShapeDtypeStruct(tile.shape, tile.dtype),
        in_specs=[pl.BlockSpec(memory_space=pltpu.SMEM)] + [vmem] * 5,
        out_specs=vmem,
        scratch_shapes=[
            pltpu.VMEM((fields, span, width), tile.dtype),
            pltpu.VMEM((aux.shape[0], span, width), tile.dtype),
        ],
    )(coefs, tile, aux, top, bottom, hits)


def per_device(ensemble, ancestors, depth_levels, level_coefs, altimetry, obs_rows):
    width_y = ensemble.shape[3]
    reach = 8
    tile, gathered = resample(ensemble[0], ancestors, altimetry)
    all_lines = jnp.moveaxis(gathered, 0, 1).reshape(
        (altimetry.shape[0], -1) + altimetry.shape[2:]
    )
    columns = jnp.arange(width_y, dtype=jnp.int32)
    targets = []
    hits = []
    for step in range(STEPS):
        onehot = (obs_rows[step][:, None] == columns[None, :]).astype(jnp.float32)
        targets.append(
            jnp.dot(
                all_lines[step].T, onehot, precision=lax.Precision.HIGHEST,
                preferred_element_type=jnp.float32,
            )
        )
        hits.append(jnp.sum(onehot, axis=0)[None, :])
    aux = jnp.stack(targets + [depth_levels.astype(jnp.float32)], axis=0)
    count = lax.axis_size("space")
    forward = [(i, (i + 1) % count) for i in range(count)]
    backward = [(target, source) for source, target in forward]
    low = jnp.concatenate([tile[:, :reach], aux[:, :reach]], axis=0)
    high = jnp.concatenate([tile[:, -reach:], aux[:, -reach:]], axis=0)
    top = lax.ppermute(high, "space", forward)
    bottom = lax.ppermute(low, "space", backward)
    state = run_steps(level_coefs, tile, aux, top, bottom, jnp.stack(hits, axis=0))
    return state[None]


def solution(mesh):
    in_specs = (
        P("particle", None, "space", None),
        P(),
        P("space", None),
        P(),
        P(None, "particle", "space"),
        P(),
    )
    out_specs = P("particle", None, "space", None)
    return jax.shard_map(
        per_device, mesh=mesh, in_specs=in_specs, out_specs=out_specs, check_vma=False
    )
```

```python
import functools

import jax
import jax.numpy as jnp
from jax import lax
from jax.experimental import pallas as pl
from jax.experimental.pallas import tpu as pltpu
from jax.sharding import PartitionSpec as P

MESH = pl.DeviceIdType.MESH

STEPS = 3


DT = 0.2
CORIOLIS = 0.5
GRAVITY = 1.0
NUDGE = 0.5


def with_halo(block, sides, width):
    for axis, dim in sides:
        count = lax.axis_size(axis)
        forward = [(i, i + 1) for i in range(count - 1)]
        forward.append((count - 1, 0))
        backward = [(target, source) for source, target in forward]
        low = lax.ppermute(
            lax.slice_in_dim(block, block.shape[dim] - width, None, axis=dim), axis, forward
        )
        high = lax.ppermute(lax.slice_in_dim(block, 0, width, axis=dim), axis, backward)
        block = jnp.concatenate([low, block, high], axis=dim)
    return block


def pad_second(field):
    return jnp.pad(field, [(0, 0)] * (field.ndim - 1) + [(1, 1)])


def gradients(wide):
    center = wide[:, 1:-1]
    east = wide[:, 2:]
    west = wide[:, :-2]
    padded = pad_second(center)
    ddx = (east - west) * 0.5
    ddy = (padded[..., 2:] - padded[..., :-2]) * 0.5
    laplace = east + west + padded[..., 2:] + padded[..., :-2] - 4.0 * center
    return (center, ddx, ddy, laplace)


def widen_state(field):
    return with_halo(field, (("space", 1),), 1)


def widen_surface(field):
    return with_halo(field, (("space", 1),), 1)


def level_terms(coefs):
    thick = coefs[0][:, None, None]
    visc = 0.2 * coefs[1][:, None, None]
    kappa = 0.2 * coefs[2][:, None, None]
    return (thick, visc, kappa)


def finish(center, ddx, ddy, laplace, masks, visc, kappa, grad_x, grad_y, height_two):
    levels = masks.shape[0]
    east_vel = center[:levels]
    north_vel = center[levels : 2 * levels]
    temper = center[2 * levels : 3 * levels]
    east_new = masks * (
        east_vel + DT * (CORIOLIS * north_vel - GRAVITY * grad_x + visc * laplace[:levels])
    )
    north_new = masks * (
        north_vel
        + DT * (-CORIOLIS * east_vel - GRAVITY * grad_y + visc * laplace[levels : 2 * levels])
    )
    temper_new = masks * (
        temper
        + DT
        * (
            kappa * laplace[2 * levels : 3 * levels]
            - east_vel * ddx[2 * levels : 3 * levels]
            - north_vel * ddy[2 * levels : 3 * levels]
        )
    )
    return jnp.concatenate([east_new, north_new, temper_new, height_two[None]], axis=0)


def one_step(state, masks, coefs, target, hit):
    levels = masks.shape[0]
    surface = masks[0]
    center, ddx, ddy, laplace = gradients(widen_state(state))
    height = center[3 * levels]
    thick, visc, kappa = level_terms(coefs)
    spread = ddx[:levels] + ddy[levels : 2 * levels]
    height_one = surface * (height - DT * jnp.sum(thick * masks * spread, axis=0))
    height_two = surface * (height_one + NUDGE * hit * (target - height_one))
    unused, grad_x, grad_y, unused_lap = gradients(widen_surface(height_two[None]))
    return finish(center, ddx, ddy, laplace, masks, visc, kappa, grad_x, grad_y, height_two)


def window(source, grid_cols, rows, cols):
    return (pl.ds((source // grid_cols) * rows, rows), pl.ds((source % grid_cols) * cols, cols))


def exchange_kernel(
    count, grid_cols, groups, anc_ref, ens_ref, alt_ref, out_ref, lines_ref,
    held_a, held_b, outgoing_a, outgoing_b, send1, recv1, send2, recv2, send3, recv3, local,
):
    me = lax.axis_index("particle")
    held = (held_a, held_b)
    outgoing = (outgoing_a, outgoing_b)
    rows, cols = held_a.shape[2], held_a.shape[3]

    barrier = pltpu.get_barrier_semaphore()
    for offset in range(1, count):
        peer = lax.rem(me + offset, count)
        pl.semaphore_signal(barrier, inc=1, device_id={"particle": peer}, device_id_type=MESH)
    pl.semaphore_wait(barrier, count - 1)

    def chunk_of(dest, fields):
        r, c = window(dest, grid_cols, rows, cols)
        return ens_ref.at[fields, r, c]

    def first_copy(group, fields, offset, peer):
        return pltpu.make_async_remote_copy(
            src_ref=chunk_of(peer, fields), dst_ref=held[group].at[me],
            send_sem=send1.at[group, offset], recv_sem=recv1.at[group, me],
            device_id={"particle": peer}, device_id_type=MESH,
        )

    def second_copy(group, fields, offset, peer):
        r_me, c_me = window(me, grid_cols, rows, cols)
        return pltpu.make_async_remote_copy(
            src_ref=outgoing[group].at[peer], dst_ref=out_ref.at[fields, r_me, c_me],
            send_sem=send2.at[group, offset], recv_sem=recv2.at[group, me],
            device_id={"particle": peer}, device_id_type=MESH,
        )

    own_lines = pltpu.make_async_copy(alt_ref, lines_ref.at[me], local.at[0])
    own_lines.start()
    line_copies = []
    for offset in range(1, count):
        peer = lax.rem(me + offset, count)
        lines = pltpu.make_async_remote_copy(
            src_ref=alt_ref, dst_ref=lines_ref.at[me], send_sem=send3.at[offset],
            recv_sem=recv3.at[me], device_id={"particle": peer}, device_id_type=MESH,
        )
        lines.start()
        line_copies.append(lines)

    own_parts = []
    firsts = []
    for group, fields in enumerate(groups):
        own = pltpu.make_async_copy(chunk_of(me, fields), held[group].at[me], local.at[1 + group])
        own.start()
        own_parts.append(own)
        copies = []
        for offset in range(1, count):
            copy = first_copy(group, fields, offset, lax.rem(me + offset, count))
            copy.start()
            copies.append(copy)
        firsts.append(copies)

    seconds = []
    for group, fields in enumerate(groups):
        own_parts[group].wait()
        for offset, copy in zip(range(1, count), firsts[group]):
            sender = lax.rem(me + count - offset, count)
            copy.wait_send()
            pltpu.make_async_remote_copy(
                src_ref=chunk_of(me, fields), dst_ref=held[group].at[sender],
                send_sem=send1.at[group, offset], recv_sem=recv1.at[group, sender],
                device_id={"particle": sender}, device_id_type=MESH,
            ).wait_recv()
        for member in range(count):
            source = jnp.clip(anc_ref[member], 0, count - 1)
            outgoing[group][member] = held[group][source]
        r_me, c_me = window(me, grid_cols, rows, cols)
        mine = pltpu.make_async_copy(
            outgoing[group].at[me], out_ref.at[fields, r_me, c_me], local.at[3 + group]
        )
        mine.start()
        copies = [mine]
        for offset in range(1, count):
            copy = second_copy(group, fields, offset, lax.rem(me + offset, count))
            copy.start()
            copies.append(copy)
        seconds.append(copies)

    own_lines.wait()
    for offset, lines in zip(range(1, count), line_copies):
        sender = lax.rem(me + count - offset, count)
        lines.wait_send()
        pltpu.make_async_remote_copy(
            src_ref=alt_ref, dst_ref=lines_ref.at[sender], send_sem=send3.at[offset],
            recv_sem=recv3.at[sender], device_id={"particle": sender}, device_id_type=MESH,
        ).wait_recv()
    for group, fields in enumerate(groups):
        seconds[group][0].wait()
        for offset, copy in zip(range(1, count), seconds[group][1:]):
            sender = lax.rem(me + count - offset, count)
            r_s, c_s = window(sender, grid_cols, rows, cols)
            copy.wait_send()
            pltpu.make_async_remote_copy(
                src_ref=outgoing[group].at[me], dst_ref=out_ref.at[fields, r_s, c_s],
                send_sem=send2.at[group, offset], recv_sem=recv2.at[group, sender],
                device_id={"particle": sender}, device_id_type=MESH,
            ).wait_recv()


def resample(tile, ancestors, altimetry):
    count = lax.axis_size("particle")
    fields, height, width = tile.shape
    grid_rows = 4
    grid_cols = count // grid_rows
    rows, cols = height // grid_rows, width // grid_cols
    split = (fields + 1) // 2
    groups = (pl.ds(0, split), pl.ds(split, fields - split))
    sems = pltpu.SemaphoreType.DMA((count,))
    grouped = pltpu.SemaphoreType.DMA((len(groups), count))
    return pl.pallas_call(
        functools.partial(exchange_kernel, count, grid_cols, groups),
        out_shape=(
            jax.ShapeDtypeStruct(tile.shape, tile.dtype),
            jax.ShapeDtypeStruct((count,) + altimetry.shape, altimetry.dtype),
        ),
        in_specs=[
            pl.BlockSpec(memory_space=pltpu.SMEM),
            pl.BlockSpec(memory_space=pl.ANY),
            pl.BlockSpec(memory_space=pltpu.VMEM),
        ],
        out_specs=(
            pl.BlockSpec(memory_space=pl.ANY),
            pl.BlockSpec(memory_space=pltpu.VMEM),
        ),
        scratch_shapes=[
            pltpu.VMEM((count, split, rows, cols), tile.dtype),
            pltpu.VMEM((count, fields - split, rows, cols), tile.dtype),
            pltpu.VMEM((count, split, rows, cols), tile.dtype),
            pltpu.VMEM((count, fields - split, rows, cols), tile.dtype),
            grouped, grouped, grouped, grouped, sems, sems,
            pltpu.SemaphoreType.DMA((1 + 2 * len(groups),)),
        ],
        compiler_params=pltpu.CompilerParams(collective_id=0, has_side_effects=True),
    )(ancestors, tile, altimetry)


def stencil_kernel(coef_ref, tile_ref, aux_ref, hit_ref, out_ref, state, aux, send, recv):
    fields, rows, width = tile_ref.shape
    extra = aux_ref.shape[0]
    levels = coef_ref.shape[1]
    span = state.shape[1]
    reach = (span - rows) // 2
    space = lax.axis_index("space")
    spaces = lax.axis_size("space")
    above = lax.rem(space + spaces - 1, spaces)
    below = lax.rem(space + 1, spaces)

    barrier = pltpu.get_barrier_semaphore()
    for side in (above, below):
        pl.semaphore_signal(barrier, inc=1, device_id={"space": side}, device_id_type=MESH)
    pl.semaphore_wait(barrier, 2)

    edges = []
    for slot, (source, target) in enumerate(((tile_ref, state), (aux_ref, aux))):
        for turn, (side, start, land) in enumerate(
            ((above, 0, reach + rows), (below, rows - reach, 0))
        ):
            copy = pltpu.make_async_remote_copy(
                src_ref=source.at[:, pl.ds(start, reach)],
                dst_ref=target.at[:, pl.ds(land, reach)],
                send_sem=send.at[2 * slot + turn], recv_sem=recv.at[2 * slot + turn],
                device_id={"space": side}, device_id_type=MESH,
            )
            copy.start()
            edges.append(copy)
    state[:, reach : reach + rows] = tile_ref[...]
    aux[:, reach : reach + rows] = aux_ref[...]
    for copy in edges:
        copy.wait()

    lane = lax.broadcasted_iota(jnp.int32, (span, width), 1)
    first_lane = lane == 0
    last_lane = lane == width - 1

    def east(f):
        return pltpu.roll(f, span - 1, 0)

    def west(f):
        return pltpu.roll(f, 1, 0)

    def north(f):
        return jnp.where(last_lane, 0.0, pltpu.roll(f, width - 1, 1))

    def south(f):
        return jnp.where(first_lane, 0.0, pltpu.roll(f, 1, 1))

    def parts(f):
        e, w, n, s = east(f), west(f), north(f), south(f)
        return (e - w) * 0.5, (n - s) * 0.5, e + w + n + s - 4.0 * f

    depth = aux[extra - 1]
    masks = [(k < depth).astype(jnp.float32) for k in range(levels)]
    surface = masks[0]
    for field in range(fields):
        state[field] = state[field] * masks[field % levels]
    for step in range(STEPS):
        spread = None
        for k in range(levels):
            ddx_u = parts(state[k])[0]
            ddy_v = parts(state[levels + k])[1]
            term = (coef_ref[0, k] * masks[k]) * (ddx_u + ddy_v)
            spread = term if spread is None else spread + term
        height = state[3 * levels]
        height_one = surface * (height - DT * spread)
        hit = hit_ref[step]
        height_two = surface * (height_one + NUDGE * hit * (aux[step] - height_one))
        grad_x, grad_y, unused = parts(height_two)
        for k in range(levels):
            visc = 0.2 * coef_ref[1, k]
            kappa = 0.2 * coef_ref[2, k]
            east_vel = state[k]
            north_vel = state[levels + k]
            temper = state[2 * levels + k]
            unused_x, unused_y, lap_u = parts(east_vel)
            unused_x, unused_y, lap_v = parts(north_vel)
            ddx_t, ddy_t, lap_t = parts(temper)
            state[k] = masks[k] * (
                east_vel + DT * (CORIOLIS * north_vel - grad_x + visc * lap_u)
            )
            state[levels + k] = masks[k] * (
                north_vel + DT * (-CORIOLIS * east_vel - grad_y + visc * lap_v)
            )
            state[2 * levels + k] = masks[k] * (
                temper + DT * (kappa * lap_t - east_vel * ddx_t - north_vel * ddy_t)
            )
        state[3 * levels] = height_two
    out_ref[...] = state[:, reach : reach + rows]


def run_steps(coefs, tile, aux, hits, reach):
    fields, rows, width = tile.shape
    span = rows + 2 * reach
    vmem = pl.BlockSpec(memory_space=pltpu.VMEM)
    edge_sems = pltpu.SemaphoreType.DMA((4,))
    return pl.pallas_call(
        stencil_kernel,
        out_shape=jax.ShapeDtypeStruct(tile.shape, tile.dtype),
        in_specs=[pl.BlockSpec(memory_space=pltpu.SMEM)] + [vmem] * 3,
        out_specs=vmem,
        scratch_shapes=[
            pltpu.VMEM((fields, span, width), tile.dtype),
            pltpu.VMEM((aux.shape[0], span, width), tile.dtype),
            edge_sems,
            edge_sems,
        ],
        compiler_params=pltpu.CompilerParams(collective_id=1, has_side_effects=True),
    )(coefs, tile, aux, hits)


def per_device(ensemble, ancestors, depth_levels, level_coefs, altimetry, obs_rows):
    width_y = ensemble.shape[3]
    reach = 8
    tile, gathered = resample(ensemble[0], ancestors, altimetry)
    all_lines = jnp.moveaxis(gathered, 0, 1).reshape(
        (altimetry.shape[0], -1) + altimetry.shape[2:]
    )
    columns = jnp.arange(width_y, dtype=jnp.int32)
    targets = []
    hits = []
    for step in range(STEPS):
        onehot = (obs_rows[step][:, None] == columns[None, :]).astype(jnp.float32)
        targets.append(
            jnp.dot(
                all_lines[step].T, onehot, precision=lax.Precision.HIGHEST,
                preferred_element_type=jnp.float32,
            )
        )
        hits.append(jnp.sum(onehot, axis=0)[None, :])
    aux = jnp.stack(targets + [depth_levels.astype(jnp.float32)], axis=0)
    state = run_steps(level_coefs, tile, aux, jnp.stack(hits, axis=0), reach)
    return state[None]


def solution(mesh):
    in_specs = (
        P("particle", None, "space", None),
        P(),
        P("space", None),
        P(),
        P(None, "particle", "space"),
        P(),
    )
    out_specs = P("particle", None, "space", None)
    return jax.shard_map(
        per_device, mesh=mesh, in_specs=in_specs, out_specs=out_specs, check_vma=False
    )
```

```python
import functools

import jax
import jax.numpy as jnp
from jax import lax
from jax.experimental import pallas as pl
from jax.experimental.pallas import tpu as pltpu
from jax.sharding import PartitionSpec as P

MESH = pl.DeviceIdType.MESH

STEPS = 3


DT = 0.2
CORIOLIS = 0.5
GRAVITY = 1.0
NUDGE = 0.5


def with_halo(block, sides, width):
    for axis, dim in sides:
        count = lax.axis_size(axis)
        forward = [(i, i + 1) for i in range(count - 1)]
        forward.append((count - 1, 0))
        backward = [(target, source) for source, target in forward]
        low = lax.ppermute(
            lax.slice_in_dim(block, block.shape[dim] - width, None, axis=dim), axis, forward
        )
        high = lax.ppermute(lax.slice_in_dim(block, 0, width, axis=dim), axis, backward)
        block = jnp.concatenate([low, block, high], axis=dim)
    return block


def pad_second(field):
    return jnp.pad(field, [(0, 0)] * (field.ndim - 1) + [(1, 1)])


def gradients(wide):
    center = wide[:, 1:-1]
    east = wide[:, 2:]
    west = wide[:, :-2]
    padded = pad_second(center)
    ddx = (east - west) * 0.5
    ddy = (padded[..., 2:] - padded[..., :-2]) * 0.5
    laplace = east + west + padded[..., 2:] + padded[..., :-2] - 4.0 * center
    return (center, ddx, ddy, laplace)


def widen_state(field):
    return with_halo(field, (("space", 1),), 1)


def widen_surface(field):
    return with_halo(field, (("space", 1),), 1)


def level_terms(coefs):
    thick = coefs[0][:, None, None]
    visc = 0.2 * coefs[1][:, None, None]
    kappa = 0.2 * coefs[2][:, None, None]
    return (thick, visc, kappa)


def finish(center, ddx, ddy, laplace, masks, visc, kappa, grad_x, grad_y, height_two):
    levels = masks.shape[0]
    east_vel = center[:levels]
    north_vel = center[levels : 2 * levels]
    temper = center[2 * levels : 3 * levels]
    east_new = masks * (
        east_vel + DT * (CORIOLIS * north_vel - GRAVITY * grad_x + visc * laplace[:levels])
    )
    north_new = masks * (
        north_vel
        + DT * (-CORIOLIS * east_vel - GRAVITY * grad_y + visc * laplace[levels : 2 * levels])
    )
    temper_new = masks * (
        temper
        + DT
        * (
            kappa * laplace[2 * levels : 3 * levels]
            - east_vel * ddx[2 * levels : 3 * levels]
            - north_vel * ddy[2 * levels : 3 * levels]
        )
    )
    return jnp.concatenate([east_new, north_new, temper_new, height_two[None]], axis=0)


def one_step(state, masks, coefs, target, hit):
    levels = masks.shape[0]
    surface = masks[0]
    center, ddx, ddy, laplace = gradients(widen_state(state))
    height = center[3 * levels]
    thick, visc, kappa = level_terms(coefs)
    spread = ddx[:levels] + ddy[levels : 2 * levels]
    height_one = surface * (height - DT * jnp.sum(thick * masks * spread, axis=0))
    height_two = surface * (height_one + NUDGE * hit * (target - height_one))
    unused, grad_x, grad_y, unused_lap = gradients(widen_surface(height_two[None]))
    return finish(center, ddx, ddy, laplace, masks, visc, kappa, grad_x, grad_y, height_two)


def window(source, grid_cols, rows, cols):
    return (pl.ds((source // grid_cols) * rows, rows), pl.ds((source % grid_cols) * cols, cols))


def exchange_kernel(
    count, grid_cols, groups, anc_ref, ens_ref, alt_ref, out_ref, lines_ref,
    held_a, held_b, outgoing_a, outgoing_b, send1, recv1, send2, recv2, send3, recv3, local,
):
    me = lax.axis_index("particle")
    held = (held_a, held_b)
    outgoing = (outgoing_a, outgoing_b)
    rows, cols = held_a.shape[2], held_a.shape[3]

    barrier = pltpu.get_barrier_semaphore()
    for offset in range(1, count):
        peer = lax.rem(me + offset, count)
        pl.semaphore_signal(barrier, inc=1, device_id={"particle": peer}, device_id_type=MESH)
    pl.semaphore_wait(barrier, count - 1)

    def chunk_of(dest, fields):
        r, c = window(dest, grid_cols, rows, cols)
        return ens_ref.at[fields, r, c]

    def first_copy(group, fields, offset, peer):
        return pltpu.make_async_remote_copy(
            src_ref=chunk_of(peer, fields), dst_ref=held[group].at[me],
            send_sem=send1.at[group, offset], recv_sem=recv1.at[group, me],
            device_id={"particle": peer}, device_id_type=MESH,
        )

    def second_copy(group, fields, offset, peer):
        r_me, c_me = window(me, grid_cols, rows, cols)
        return pltpu.make_async_remote_copy(
            src_ref=outgoing[group].at[peer], dst_ref=out_ref.at[fields, r_me, c_me],
            send_sem=send2.at[group, offset], recv_sem=recv2.at[group, me],
            device_id={"particle": peer}, device_id_type=MESH,
        )

    own_lines = pltpu.make_async_copy(alt_ref, lines_ref.at[me], local.at[0])
    own_lines.start()
    line_copies = []
    for offset in range(1, count):
        peer = lax.rem(me + offset, count)
        lines = pltpu.make_async_remote_copy(
            src_ref=alt_ref, dst_ref=lines_ref.at[me], send_sem=send3.at[offset],
            recv_sem=recv3.at[me], device_id={"particle": peer}, device_id_type=MESH,
        )
        lines.start()
        line_copies.append(lines)

    own_parts = []
    firsts = []
    for group, fields in enumerate(groups):
        own = pltpu.make_async_copy(chunk_of(me, fields), held[group].at[me], local.at[1 + group])
        own.start()
        own_parts.append(own)
        copies = []
        for offset in range(1, count):
            copy = first_copy(group, fields, offset, lax.rem(me + offset, count))
            copy.start()
            copies.append(copy)
        firsts.append(copies)

    seconds = []
    for group, fields in enumerate(groups):
        own_parts[group].wait()
        for offset, copy in zip(range(1, count), firsts[group]):
            sender = lax.rem(me + count - offset, count)
            copy.wait_send()
            pltpu.make_async_remote_copy(
                src_ref=chunk_of(me, fields), dst_ref=held[group].at[sender],
                send_sem=send1.at[group, offset], recv_sem=recv1.at[group, sender],
                device_id={"particle": sender}, device_id_type=MESH,
            ).wait_recv()
        for member in range(count):
            source = jnp.clip(anc_ref[member], 0, count - 1)
            outgoing[group][member] = held[group][source]
        r_me, c_me = window(me, grid_cols, rows, cols)
        mine = pltpu.make_async_copy(
            outgoing[group].at[me], out_ref.at[fields, r_me, c_me], local.at[3 + group]
        )
        mine.start()
        copies = [mine]
        for offset in range(1, count):
            copy = second_copy(group, fields, offset, lax.rem(me + offset, count))
            copy.start()
            copies.append(copy)
        seconds.append(copies)

    own_lines.wait()
    for offset, lines in zip(range(1, count), line_copies):
        sender = lax.rem(me + count - offset, count)
        lines.wait_send()
        pltpu.make_async_remote_copy(
            src_ref=alt_ref, dst_ref=lines_ref.at[sender], send_sem=send3.at[offset],
            recv_sem=recv3.at[sender], device_id={"particle": sender}, device_id_type=MESH,
        ).wait_recv()
    for group, fields in enumerate(groups):
        seconds[group][0].wait()
        for offset, copy in zip(range(1, count), seconds[group][1:]):
            sender = lax.rem(me + count - offset, count)
            r_s, c_s = window(sender, grid_cols, rows, cols)
            copy.wait_send()
            pltpu.make_async_remote_copy(
                src_ref=outgoing[group].at[me], dst_ref=out_ref.at[fields, r_s, c_s],
                send_sem=send2.at[group, offset], recv_sem=recv2.at[group, sender],
                device_id={"particle": sender}, device_id_type=MESH,
            ).wait_recv()


def resample(tile, ancestors, altimetry):
    count = lax.axis_size("particle")
    fields, height, width = tile.shape
    grid_rows = 4
    grid_cols = count // grid_rows
    rows, cols = height // grid_rows, width // grid_cols
    split = (fields + 1) // 2
    groups = (pl.ds(0, split), pl.ds(split, fields - split))
    sems = pltpu.SemaphoreType.DMA((count,))
    grouped = pltpu.SemaphoreType.DMA((len(groups), count))
    return pl.pallas_call(
        functools.partial(exchange_kernel, count, grid_cols, groups),
        out_shape=(
            jax.ShapeDtypeStruct(tile.shape, tile.dtype),
            jax.ShapeDtypeStruct((count,) + altimetry.shape, altimetry.dtype),
        ),
        in_specs=[
            pl.BlockSpec(memory_space=pltpu.SMEM),
            pl.BlockSpec(memory_space=pl.ANY),
            pl.BlockSpec(memory_space=pltpu.VMEM),
        ],
        out_specs=(
            pl.BlockSpec(memory_space=pl.ANY),
            pl.BlockSpec(memory_space=pltpu.VMEM),
        ),
        scratch_shapes=[
            pltpu.VMEM((count, split, rows, cols), tile.dtype),
            pltpu.VMEM((count, fields - split, rows, cols), tile.dtype),
            pltpu.VMEM((count, split, rows, cols), tile.dtype),
            pltpu.VMEM((count, fields - split, rows, cols), tile.dtype),
            grouped, grouped, grouped, grouped, sems, sems,
            pltpu.SemaphoreType.DMA((1 + 2 * len(groups),)),
        ],
        compiler_params=pltpu.CompilerParams(collective_id=0, has_side_effects=True),
    )(ancestors, tile, altimetry)


def stencil_kernel(coef_ref, tile_ref, aux_ref, top_ref, bottom_ref, hit_ref, out_ref, state, aux):
    fields, rows, width = tile_ref.shape
    extra = aux_ref.shape[0]
    reach = top_ref.shape[1]
    levels = coef_ref.shape[1]
    span = state.shape[1]
    state[:, :reach] = top_ref[:fields]
    state[:, reach : reach + rows] = tile_ref[...]
    state[:, reach + rows :] = bottom_ref[:fields]
    aux[:, :reach] = top_ref[fields:]
    aux[:, reach : reach + rows] = aux_ref[...]
    aux[:, reach + rows :] = bottom_ref[fields:]

    lane = lax.broadcasted_iota(jnp.int32, (span, width), 1)
    first_lane = lane == 0
    last_lane = lane == width - 1

    def east(f):
        return pltpu.roll(f, span - 1, 0)

    def west(f):
        return pltpu.roll(f, 1, 0)

    def north(f):
        return jnp.where(last_lane, 0.0, pltpu.roll(f, width - 1, 1))

    def south(f):
        return jnp.where(first_lane, 0.0, pltpu.roll(f, 1, 1))

    def parts(f):
        e, w, n, s = east(f), west(f), north(f), south(f)
        return (e - w) * 0.5, (n - s) * 0.5, e + w + n + s - 4.0 * f

    depth = aux[extra - 1]
    masks = [(k < depth).astype(jnp.float32) for k in range(levels)]
    surface = masks[0]
    for field in range(fields):
        state[field] = state[field] * masks[field % levels]
    for step in range(STEPS):
        spread = None
        shifted = []
        for k in range(levels):
            east_vel = state[k]
            north_vel = state[levels + k]
            ddx_u, unused_y, lap_u = parts(east_vel)
            unused_x, ddy_v, lap_v = parts(north_vel)
            shifted.append((east_vel, north_vel, lap_u, lap_v))
            term = (coef_ref[0, k] * masks[k]) * (ddx_u + ddy_v)
            spread = term if spread is None else spread + term
        height = state[3 * levels]
        height_one = surface * (height - DT * spread)
        hit = hit_ref[step]
        height_two = surface * (height_one + NUDGE * hit * (aux[step] - height_one))
        grad_x, grad_y, unused = parts(height_two)
        for k in range(levels):
            visc = 0.2 * coef_ref[1, k]
            kappa = 0.2 * coef_ref[2, k]
            east_vel, north_vel, lap_u, lap_v = shifted[k]
            temper = state[2 * levels + k]
            ddx_t, ddy_t, lap_t = parts(temper)
            state[k] = masks[k] * (
                east_vel + DT * (CORIOLIS * north_vel - grad_x + visc * lap_u)
            )
            state[levels + k] = masks[k] * (
                north_vel + DT * (-CORIOLIS * east_vel - grad_y + visc * lap_v)
            )
            state[2 * levels + k] = masks[k] * (
                temper + DT * (kappa * lap_t - east_vel * ddx_t - north_vel * ddy_t)
            )
        state[3 * levels] = height_two
    out_ref[...] = state[:, reach : reach + rows]


def run_steps(coefs, tile, aux, top, bottom, hits):
    fields, rows, width = tile.shape
    span = rows + 2 * top.shape[1]
    vmem = pl.BlockSpec(memory_space=pltpu.VMEM)
    return pl.pallas_call(
        stencil_kernel,
        out_shape=jax.ShapeDtypeStruct(tile.shape, tile.dtype),
        in_specs=[pl.BlockSpec(memory_space=pltpu.SMEM)] + [vmem] * 5,
        out_specs=vmem,
        scratch_shapes=[
            pltpu.VMEM((fields, span, width), tile.dtype),
            pltpu.VMEM((aux.shape[0], span, width), tile.dtype),
        ],
    )(coefs, tile, aux, top, bottom, hits)


def per_device(ensemble, ancestors, depth_levels, level_coefs, altimetry, obs_rows):
    width_y = ensemble.shape[3]
    reach = 8
    tile, gathered = resample(ensemble[0], ancestors, altimetry)
    all_lines = jnp.moveaxis(gathered, 0, 1).reshape(
        (altimetry.shape[0], -1) + altimetry.shape[2:]
    )
    columns = jnp.arange(width_y, dtype=jnp.int32)
    targets = []
    hits = []
    for step in range(STEPS):
        onehot = (obs_rows[step][:, None] == columns[None, :]).astype(jnp.float32)
        targets.append(
            jnp.dot(
                all_lines[step].T, onehot, precision=lax.Precision.HIGHEST,
                preferred_element_type=jnp.float32,
            )
        )
        hits.append(jnp.sum(onehot, axis=0)[None, :])
    aux = jnp.stack(targets + [depth_levels.astype(jnp.float32)], axis=0)
    count = lax.axis_size("space")
    forward = [(i, (i + 1) % count) for i in range(count)]
    backward = [(target, source) for source, target in forward]
    low = jnp.concatenate([tile[:, :reach], aux[:, :reach]], axis=0)
    high = jnp.concatenate([tile[:, -reach:], aux[:, -reach:]], axis=0)
    top = lax.ppermute(high, "space", forward)
    bottom = lax.ppermute(low, "space", backward)
    state = run_steps(level_coefs, tile, aux, top, bottom, jnp.stack(hits, axis=0))
    return state[None]


def solution(mesh):
    in_specs = (
        P("particle", None, "space", None),
        P(),
        P("space", None),
        P(),
        P(None, "particle", "space"),
        P(),
    )
    out_specs = P("particle", None, "space", None)
    return jax.shard_map(
        per_device, mesh=mesh, in_specs=in_specs, out_specs=out_specs, check_vma=False
    )
```

```python
import functools

import jax
import jax.numpy as jnp
from jax import lax
from jax.experimental import pallas as pl
from jax.experimental.pallas import tpu as pltpu
from jax.sharding import PartitionSpec as P

MESH = pl.DeviceIdType.MESH

STEPS = 3


DT = 0.2
CORIOLIS = 0.5
GRAVITY = 1.0
NUDGE = 0.5


def with_halo(block, sides, width):
    for axis, dim in sides:
        count = lax.axis_size(axis)
        forward = [(i, i + 1) for i in range(count - 1)]
        forward.append((count - 1, 0))
        backward = [(target, source) for source, target in forward]
        low = lax.ppermute(
            lax.slice_in_dim(block, block.shape[dim] - width, None, axis=dim), axis, forward
        )
        high = lax.ppermute(lax.slice_in_dim(block, 0, width, axis=dim), axis, backward)
        block = jnp.concatenate([low, block, high], axis=dim)
    return block


def pad_second(field):
    return jnp.pad(field, [(0, 0)] * (field.ndim - 1) + [(1, 1)])


def gradients(wide):
    center = wide[:, 1:-1]
    east = wide[:, 2:]
    west = wide[:, :-2]
    padded = pad_second(center)
    ddx = (east - west) * 0.5
    ddy = (padded[..., 2:] - padded[..., :-2]) * 0.5
    laplace = east + west + padded[..., 2:] + padded[..., :-2] - 4.0 * center
    return (center, ddx, ddy, laplace)


def widen_state(field):
    return with_halo(field, (("space", 1),), 1)


def widen_surface(field):
    return with_halo(field, (("space", 1),), 1)


def level_terms(coefs):
    thick = coefs[0][:, None, None]
    visc = 0.2 * coefs[1][:, None, None]
    kappa = 0.2 * coefs[2][:, None, None]
    return (thick, visc, kappa)


def finish(center, ddx, ddy, laplace, masks, visc, kappa, grad_x, grad_y, height_two):
    levels = masks.shape[0]
    east_vel = center[:levels]
    north_vel = center[levels : 2 * levels]
    temper = center[2 * levels : 3 * levels]
    east_new = masks * (
        east_vel + DT * (CORIOLIS * north_vel - GRAVITY * grad_x + visc * laplace[:levels])
    )
    north_new = masks * (
        north_vel
        + DT * (-CORIOLIS * east_vel - GRAVITY * grad_y + visc * laplace[levels : 2 * levels])
    )
    temper_new = masks * (
        temper
        + DT
        * (
            kappa * laplace[2 * levels : 3 * levels]
            - east_vel * ddx[2 * levels : 3 * levels]
            - north_vel * ddy[2 * levels : 3 * levels]
        )
    )
    return jnp.concatenate([east_new, north_new, temper_new, height_two[None]], axis=0)


def one_step(state, masks, coefs, target, hit):
    levels = masks.shape[0]
    surface = masks[0]
    center, ddx, ddy, laplace = gradients(widen_state(state))
    height = center[3 * levels]
    thick, visc, kappa = level_terms(coefs)
    spread = ddx[:levels] + ddy[levels : 2 * levels]
    height_one = surface * (height - DT * jnp.sum(thick * masks * spread, axis=0))
    height_two = surface * (height_one + NUDGE * hit * (target - height_one))
    unused, grad_x, grad_y, unused_lap = gradients(widen_surface(height_two[None]))
    return finish(center, ddx, ddy, laplace, masks, visc, kappa, grad_x, grad_y, height_two)


def window(source, grid_cols, rows, cols):
    return (pl.ds((source // grid_cols) * rows, rows), pl.ds((source % grid_cols) * cols, cols))


def exchange_kernel(
    count, grid_cols, groups, anc_ref, ens_ref, alt_ref, out_ref, lines_ref,
    held_a, held_b, outgoing_a, outgoing_b, send1, recv1, send2, recv2, send3, recv3, local,
):
    me = lax.axis_index("particle")
    held = (held_a, held_b)
    outgoing = (outgoing_a, outgoing_b)
    rows, cols = held_a.shape[2], held_a.shape[3]

    barrier = pltpu.get_barrier_semaphore()
    for offset in range(1, count):
        peer = lax.rem(me + offset, count)
        pl.semaphore_signal(barrier, inc=1, device_id={"particle": peer}, device_id_type=MESH)
    pl.semaphore_wait(barrier, count - 1)

    def chunk_of(dest, fields):
        r, c = window(dest, grid_cols, rows, cols)
        return ens_ref.at[fields, r, c]

    def first_copy(group, fields, offset, peer):
        return pltpu.make_async_remote_copy(
            src_ref=chunk_of(peer, fields), dst_ref=held[group].at[me],
            send_sem=send1.at[group, offset], recv_sem=recv1.at[group, me],
            device_id={"particle": peer}, device_id_type=MESH,
        )

    def second_copy(group, fields, offset, peer):
        r_me, c_me = window(me, grid_cols, rows, cols)
        return pltpu.make_async_remote_copy(
            src_ref=outgoing[group].at[peer], dst_ref=out_ref.at[fields, r_me, c_me],
            send_sem=send2.at[group, offset], recv_sem=recv2.at[group, me],
            device_id={"particle": peer}, device_id_type=MESH,
        )

    own_lines = pltpu.make_async_copy(alt_ref, lines_ref.at[me], local.at[0])
    own_lines.start()
    line_copies = []
    for offset in range(1, count):
        peer = lax.rem(me + offset, count)
        lines = pltpu.make_async_remote_copy(
            src_ref=alt_ref, dst_ref=lines_ref.at[me], send_sem=send3.at[offset],
            recv_sem=recv3.at[me], device_id={"particle": peer}, device_id_type=MESH,
        )
        lines.start()
        line_copies.append(lines)

    own_parts = []
    firsts = []
    for group, fields in enumerate(groups):
        own = pltpu.make_async_copy(chunk_of(me, fields), held[group].at[me], local.at[1 + group])
        own.start()
        own_parts.append(own)
        copies = []
        for offset in range(1, count):
            copy = first_copy(group, fields, offset, lax.rem(me + offset, count))
            copy.start()
            copies.append(copy)
        firsts.append(copies)

    seconds = []
    for group, fields in enumerate(groups):
        own_parts[group].wait()
        for offset, copy in zip(range(1, count), firsts[group]):
            sender = lax.rem(me + count - offset, count)
            copy.wait_send()
            pltpu.make_async_remote_copy(
                src_ref=chunk_of(me, fields), dst_ref=held[group].at[sender],
                send_sem=send1.at[group, offset], recv_sem=recv1.at[group, sender],
                device_id={"particle": sender}, device_id_type=MESH,
            ).wait_recv()
        for member in range(count):
            source = jnp.clip(anc_ref[member], 0, count - 1)
            outgoing[group][member] = held[group][source]
        r_me, c_me = window(me, grid_cols, rows, cols)
        mine = pltpu.make_async_copy(
            outgoing[group].at[me], out_ref.at[fields, r_me, c_me], local.at[3 + group]
        )
        mine.start()
        copies = [mine]
        for offset in range(1, count):
            copy = second_copy(group, fields, offset, lax.rem(me + offset, count))
            copy.start()
            copies.append(copy)
        seconds.append(copies)

    own_lines.wait()
    for offset, lines in zip(range(1, count), line_copies):
        sender = lax.rem(me + count - offset, count)
        lines.wait_send()
        pltpu.make_async_remote_copy(
            src_ref=alt_ref, dst_ref=lines_ref.at[sender], send_sem=send3.at[offset],
            recv_sem=recv3.at[sender], device_id={"particle": sender}, device_id_type=MESH,
        ).wait_recv()
    for group, fields in enumerate(groups):
        seconds[group][0].wait()
        for offset, copy in zip(range(1, count), seconds[group][1:]):
            sender = lax.rem(me + count - offset, count)
            r_s, c_s = window(sender, grid_cols, rows, cols)
            copy.wait_send()
            pltpu.make_async_remote_copy(
                src_ref=outgoing[group].at[me], dst_ref=out_ref.at[fields, r_s, c_s],
                send_sem=send2.at[group, offset], recv_sem=recv2.at[group, sender],
                device_id={"particle": sender}, device_id_type=MESH,
            ).wait_recv()


def resample(tile, ancestors, altimetry):
    count = lax.axis_size("particle")
    fields, height, width = tile.shape
    grid_rows = 4
    grid_cols = count // grid_rows
    rows, cols = height // grid_rows, width // grid_cols
    split = (fields + 1) // 2
    groups = (pl.ds(0, split), pl.ds(split, fields - split))
    sems = pltpu.SemaphoreType.DMA((count,))
    grouped = pltpu.SemaphoreType.DMA((len(groups), count))
    return pl.pallas_call(
        functools.partial(exchange_kernel, count, grid_cols, groups),
        out_shape=(
            jax.ShapeDtypeStruct(tile.shape, tile.dtype),
            jax.ShapeDtypeStruct((count,) + altimetry.shape, altimetry.dtype),
        ),
        in_specs=[
            pl.BlockSpec(memory_space=pltpu.SMEM),
            pl.BlockSpec(memory_space=pl.ANY),
            pl.BlockSpec(memory_space=pltpu.VMEM),
        ],
        out_specs=(
            pl.BlockSpec(memory_space=pl.ANY),
            pl.BlockSpec(memory_space=pltpu.VMEM),
        ),
        scratch_shapes=[
            pltpu.VMEM((count, split, rows, cols), tile.dtype),
            pltpu.VMEM((count, fields - split, rows, cols), tile.dtype),
            pltpu.VMEM((count, split, rows, cols), tile.dtype),
            pltpu.VMEM((count, fields - split, rows, cols), tile.dtype),
            grouped, grouped, grouped, grouped, sems, sems,
            pltpu.SemaphoreType.DMA((1 + 2 * len(groups),)),
        ],
        compiler_params=pltpu.CompilerParams(collective_id=0, has_side_effects=True),
    )(ancestors, tile, altimetry)


def stencil_kernel(coef_ref, tile_ref, aux_ref, top_ref, bottom_ref, hit_ref, out_ref, state, aux):
    fields, rows, width = tile_ref.shape
    extra = aux_ref.shape[0]
    levels = coef_ref.shape[1]
    span = state.shape[1]
    reach = (span - rows) // 2
    sent = top_ref.shape[1]
    spare = reach - sent
    for target in (state, aux):
        target[:, :spare] = jnp.zeros((target.shape[0], spare, width), jnp.float32)
        target[:, span - spare :] = jnp.zeros((target.shape[0], spare, width), jnp.float32)
    state[:, spare:reach] = top_ref[:fields]
    state[:, reach : reach + rows] = tile_ref[...]
    state[:, reach + rows : reach + rows + sent] = bottom_ref[:fields]
    aux[:, spare:reach] = top_ref[fields:]
    aux[:, reach : reach + rows] = aux_ref[...]
    aux[:, reach + rows : reach + rows + sent] = bottom_ref[fields:]

    lane = lax.broadcasted_iota(jnp.int32, (span, width), 1)
    first_lane = lane == 0
    last_lane = lane == width - 1

    def east(f):
        return pltpu.roll(f, span - 1, 0)

    def west(f):
        return pltpu.roll(f, 1, 0)

    def north(f):
        return jnp.where(last_lane, 0.0, pltpu.roll(f, width - 1, 1))

    def south(f):
        return jnp.where(first_lane, 0.0, pltpu.roll(f, 1, 1))

    def parts(f):
        e, w, n, s = east(f), west(f), north(f), south(f)
        return (e - w) * 0.5, (n - s) * 0.5, e + w + n + s - 4.0 * f

    depth = aux[extra - 1]
    masks = [(k < depth).astype(jnp.float32) for k in range(levels)]
    surface = masks[0]
    for field in range(fields):
        state[field] = state[field] * masks[field % levels]
    for step in range(STEPS):
        spread = None
        shifted = []
        for k in range(levels):
            east_vel = state[k]
            north_vel = state[levels + k]
            ddx_u, unused_y, lap_u = parts(east_vel)
            unused_x, ddy_v, lap_v = parts(north_vel)
            shifted.append((east_vel, north_vel, lap_u, lap_v))
            term = (coef_ref[0, k] * masks[k]) * (ddx_u + ddy_v)
            spread = term if spread is None else spread + term
        height = state[3 * levels]
        height_one = surface * (height - DT * spread)
        hit = hit_ref[step]
        height_two = surface * (height_one + NUDGE * hit * (aux[step] - height_one))
        grad_x, grad_y, unused = parts(height_two)
        for k in range(levels):
            visc = 0.2 * coef_ref[1, k]
            kappa = 0.2 * coef_ref[2, k]
            east_vel, north_vel, lap_u, lap_v = shifted[k]
            temper = state[2 * levels + k]
            ddx_t, ddy_t, lap_t = parts(temper)
            state[k] = masks[k] * (
                east_vel + DT * (CORIOLIS * north_vel - grad_x + visc * lap_u)
            )
            state[levels + k] = masks[k] * (
                north_vel + DT * (-CORIOLIS * east_vel - grad_y + visc * lap_v)
            )
            state[2 * levels + k] = masks[k] * (
                temper + DT * (kappa * lap_t - east_vel * ddx_t - north_vel * ddy_t)
            )
        state[3 * levels] = height_two
    out_ref[...] = state[:, reach : reach + rows]


def run_steps(coefs, tile, aux, top, bottom, hits, reach):
    fields, rows, width = tile.shape
    span = rows + 2 * reach
    vmem = pl.BlockSpec(memory_space=pltpu.VMEM)
    return pl.pallas_call(
        stencil_kernel,
        out_shape=jax.ShapeDtypeStruct(tile.shape, tile.dtype),
        in_specs=[pl.BlockSpec(memory_space=pltpu.SMEM)] + [vmem] * 5,
        out_specs=vmem,
        scratch_shapes=[
            pltpu.VMEM((fields, span, width), tile.dtype),
            pltpu.VMEM((aux.shape[0], span, width), tile.dtype),
        ],
    )(coefs, tile, aux, top, bottom, hits)


def per_device(ensemble, ancestors, depth_levels, level_coefs, altimetry, obs_rows):
    width_y = ensemble.shape[3]
    reach = 8
    tile, gathered = resample(ensemble[0], ancestors, altimetry)
    all_lines = jnp.moveaxis(gathered, 0, 1).reshape(
        (altimetry.shape[0], -1) + altimetry.shape[2:]
    )
    columns = jnp.arange(width_y, dtype=jnp.int32)
    targets = []
    hits = []
    for step in range(STEPS):
        onehot = (obs_rows[step][:, None] == columns[None, :]).astype(jnp.float32)
        targets.append(
            jnp.dot(
                all_lines[step].T, onehot, precision=lax.Precision.HIGHEST,
                preferred_element_type=jnp.float32,
            )
        )
        hits.append(jnp.sum(onehot, axis=0)[None, :])
    aux = jnp.stack(targets + [depth_levels.astype(jnp.float32)], axis=0)
    count = lax.axis_size("space")
    forward = [(i, (i + 1) % count) for i in range(count)]
    backward = [(target, source) for source, target in forward]
    sent = 2 * STEPS
    low = jnp.concatenate([tile[:, :sent], aux[:, :sent]], axis=0)
    high = jnp.concatenate([tile[:, -sent:], aux[:, -sent:]], axis=0)
    top = lax.ppermute(high, "space", forward)
    bottom = lax.ppermute(low, "space", backward)
    state = run_steps(level_coefs, tile, aux, top, bottom, jnp.stack(hits, axis=0), reach)
    return state[None]


def solution(mesh):
    in_specs = (
        P("particle", None, "space", None),
        P(),
        P("space", None),
        P(),
        P(None, "particle", "space"),
        P(),
    )
    out_specs = P("particle", None, "space", None)
    return jax.shard_map(
        per_device, mesh=mesh, in_specs=in_specs, out_specs=out_specs, check_vma=False
    )
```

```python
import functools

import jax
import jax.numpy as jnp
from jax import lax
from jax.experimental import pallas as pl
from jax.experimental.pallas import tpu as pltpu
from jax.sharding import PartitionSpec as P

MESH = pl.DeviceIdType.MESH

STEPS = 3


DT = 0.2
CORIOLIS = 0.5
GRAVITY = 1.0
NUDGE = 0.5


def with_halo(block, sides, width):
    for axis, dim in sides:
        count = lax.axis_size(axis)
        forward = [(i, i + 1) for i in range(count - 1)]
        forward.append((count - 1, 0))
        backward = [(target, source) for source, target in forward]
        low = lax.ppermute(
            lax.slice_in_dim(block, block.shape[dim] - width, None, axis=dim), axis, forward
        )
        high = lax.ppermute(lax.slice_in_dim(block, 0, width, axis=dim), axis, backward)
        block = jnp.concatenate([low, block, high], axis=dim)
    return block


def pad_second(field):
    return jnp.pad(field, [(0, 0)] * (field.ndim - 1) + [(1, 1)])


def gradients(wide):
    center = wide[:, 1:-1]
    east = wide[:, 2:]
    west = wide[:, :-2]
    padded = pad_second(center)
    ddx = (east - west) * 0.5
    ddy = (padded[..., 2:] - padded[..., :-2]) * 0.5
    laplace = east + west + padded[..., 2:] + padded[..., :-2] - 4.0 * center
    return (center, ddx, ddy, laplace)


def widen_state(field):
    return with_halo(field, (("space", 1),), 1)


def widen_surface(field):
    return with_halo(field, (("space", 1),), 1)


def level_terms(coefs):
    thick = coefs[0][:, None, None]
    visc = 0.2 * coefs[1][:, None, None]
    kappa = 0.2 * coefs[2][:, None, None]
    return (thick, visc, kappa)


def finish(center, ddx, ddy, laplace, masks, visc, kappa, grad_x, grad_y, height_two):
    levels = masks.shape[0]
    east_vel = center[:levels]
    north_vel = center[levels : 2 * levels]
    temper = center[2 * levels : 3 * levels]
    east_new = masks * (
        east_vel + DT * (CORIOLIS * north_vel - GRAVITY * grad_x + visc * laplace[:levels])
    )
    north_new = masks * (
        north_vel
        + DT * (-CORIOLIS * east_vel - GRAVITY * grad_y + visc * laplace[levels : 2 * levels])
    )
    temper_new = masks * (
        temper
        + DT
        * (
            kappa * laplace[2 * levels : 3 * levels]
            - east_vel * ddx[2 * levels : 3 * levels]
            - north_vel * ddy[2 * levels : 3 * levels]
        )
    )
    return jnp.concatenate([east_new, north_new, temper_new, height_two[None]], axis=0)


def one_step(state, masks, coefs, target, hit):
    levels = masks.shape[0]
    surface = masks[0]
    center, ddx, ddy, laplace = gradients(widen_state(state))
    height = center[3 * levels]
    thick, visc, kappa = level_terms(coefs)
    spread = ddx[:levels] + ddy[levels : 2 * levels]
    height_one = surface * (height - DT * jnp.sum(thick * masks * spread, axis=0))
    height_two = surface * (height_one + NUDGE * hit * (target - height_one))
    unused, grad_x, grad_y, unused_lap = gradients(widen_surface(height_two[None]))
    return finish(center, ddx, ddy, laplace, masks, visc, kappa, grad_x, grad_y, height_two)


def window(source, grid_cols, rows, cols):
    return (pl.ds((source // grid_cols) * rows, rows), pl.ds((source % grid_cols) * cols, cols))


def exchange_kernel(
    count, grid_cols, groups, anc_ref, ens_ref, alt_ref, out_ref, lines_ref,
    held_a, held_b, outgoing_a, outgoing_b, send1, recv1, send2, recv2, send3, recv3, local,
):
    me = lax.axis_index("particle")
    held = (held_a, held_b)
    outgoing = (outgoing_a, outgoing_b)
    rows, cols = held_a.shape[2], held_a.shape[3]

    barrier = pltpu.get_barrier_semaphore()
    for offset in range(1, count):
        peer = lax.rem(me + offset, count)
        pl.semaphore_signal(barrier, inc=1, device_id={"particle": peer}, device_id_type=MESH)
    pl.semaphore_wait(barrier, count - 1)

    side = 4
    routes = sorted(
        ((dz, dy) for dz in range(count // side) for dy in range(side) if dz or dy),
        key=lambda pair: -(2 * min(pair[0], count // side - pair[0]) + min(pair[1], side - pair[1])),
    )

    def peer_at(route, sign):
        dz, dy = route
        zs = count // side
        z = lax.rem(me // side + zs + sign * dz, zs)
        y = lax.rem(me % side + side + sign * dy, side)
        return z * side + y

    def chunk_of(dest, fields):
        r, c = window(dest, grid_cols, rows, cols)
        return ens_ref.at[fields, r, c]

    def first_copy(group, fields, offset, peer):
        return pltpu.make_async_remote_copy(
            src_ref=chunk_of(peer, fields), dst_ref=held[group].at[me],
            send_sem=send1.at[group, offset], recv_sem=recv1.at[group, me],
            device_id={"particle": peer}, device_id_type=MESH,
        )

    def second_copy(group, fields, offset, peer):
        r_me, c_me = window(me, grid_cols, rows, cols)
        return pltpu.make_async_remote_copy(
            src_ref=outgoing[group].at[peer], dst_ref=out_ref.at[fields, r_me, c_me],
            send_sem=send2.at[group, offset], recv_sem=recv2.at[group, me],
            device_id={"particle": peer}, device_id_type=MESH,
        )

    own_lines = pltpu.make_async_copy(alt_ref, lines_ref.at[me], local.at[0])
    own_lines.start()
    line_copies = []
    for offset in range(1, count):
        peer = lax.rem(me + offset, count)
        lines = pltpu.make_async_remote_copy(
            src_ref=alt_ref, dst_ref=lines_ref.at[me], send_sem=send3.at[offset],
            recv_sem=recv3.at[me], device_id={"particle": peer}, device_id_type=MESH,
        )
        lines.start()
        line_copies.append(lines)

    own_parts = []
    firsts = []
    for group, fields in enumerate(groups):
        own = pltpu.make_async_copy(chunk_of(me, fields), held[group].at[me], local.at[1 + group])
        own.start()
        own_parts.append(own)
        copies = []
        for offset, route in enumerate(routes, start=1):
            copy = first_copy(group, fields, offset, peer_at(route, 1))
            copy.start()
            copies.append(copy)
        firsts.append(copies)

    seconds = []
    for group, fields in enumerate(groups):
        own_parts[group].wait()
        for offset, route, copy in zip(range(1, count), routes, firsts[group]):
            sender = peer_at(route, -1)
            copy.wait_send()
            pltpu.make_async_remote_copy(
                src_ref=chunk_of(me, fields), dst_ref=held[group].at[sender],
                send_sem=send1.at[group, offset], recv_sem=recv1.at[group, sender],
                device_id={"particle": sender}, device_id_type=MESH,
            ).wait_recv()
        for member in range(count):
            source = jnp.clip(anc_ref[member], 0, count - 1)
            outgoing[group][member] = held[group][source]
        r_me, c_me = window(me, grid_cols, rows, cols)
        mine = pltpu.make_async_copy(
            outgoing[group].at[me], out_ref.at[fields, r_me, c_me], local.at[3 + group]
        )
        mine.start()
        copies = [mine]
        for offset, route in enumerate(routes, start=1):
            copy = second_copy(group, fields, offset, peer_at(route, 1))
            copy.start()
            copies.append(copy)
        seconds.append(copies)

    own_lines.wait()
    for offset, lines in zip(range(1, count), line_copies):
        sender = lax.rem(me + count - offset, count)
        lines.wait_send()
        pltpu.make_async_remote_copy(
            src_ref=alt_ref, dst_ref=lines_ref.at[sender], send_sem=send3.at[offset],
            recv_sem=recv3.at[sender], device_id={"particle": sender}, device_id_type=MESH,
        ).wait_recv()
    for group, fields in enumerate(groups):
        seconds[group][0].wait()
        for offset, route, copy in zip(range(1, count), routes, seconds[group][1:]):
            sender = peer_at(route, -1)
            r_s, c_s = window(sender, grid_cols, rows, cols)
            copy.wait_send()
            pltpu.make_async_remote_copy(
                src_ref=outgoing[group].at[me], dst_ref=out_ref.at[fields, r_s, c_s],
                send_sem=send2.at[group, offset], recv_sem=recv2.at[group, sender],
                device_id={"particle": sender}, device_id_type=MESH,
            ).wait_recv()


def resample(tile, ancestors, altimetry):
    count = lax.axis_size("particle")
    fields, height, width = tile.shape
    grid_rows = 4
    grid_cols = count // grid_rows
    rows, cols = height // grid_rows, width // grid_cols
    split = (fields + 1) // 2
    groups = (pl.ds(0, split), pl.ds(split, fields - split))
    sems = pltpu.SemaphoreType.DMA((count,))
    grouped = pltpu.SemaphoreType.DMA((len(groups), count))
    return pl.pallas_call(
        functools.partial(exchange_kernel, count, grid_cols, groups),
        out_shape=(
            jax.ShapeDtypeStruct(tile.shape, tile.dtype),
            jax.ShapeDtypeStruct((count,) + altimetry.shape, altimetry.dtype),
        ),
        in_specs=[
            pl.BlockSpec(memory_space=pltpu.SMEM),
            pl.BlockSpec(memory_space=pl.ANY),
            pl.BlockSpec(memory_space=pltpu.VMEM),
        ],
        out_specs=(
            pl.BlockSpec(memory_space=pl.ANY),
            pl.BlockSpec(memory_space=pltpu.VMEM),
        ),
        scratch_shapes=[
            pltpu.VMEM((count, split, rows, cols), tile.dtype),
            pltpu.VMEM((count, fields - split, rows, cols), tile.dtype),
            pltpu.VMEM((count, split, rows, cols), tile.dtype),
            pltpu.VMEM((count, fields - split, rows, cols), tile.dtype),
            grouped, grouped, grouped, grouped, sems, sems,
            pltpu.SemaphoreType.DMA((1 + 2 * len(groups),)),
        ],
        compiler_params=pltpu.CompilerParams(collective_id=0, has_side_effects=True),
    )(ancestors, tile, altimetry)


def stencil_kernel(coef_ref, tile_ref, aux_ref, top_ref, bottom_ref, hit_ref, out_ref, state, aux):
    fields, rows, width = tile_ref.shape
    extra = aux_ref.shape[0]
    reach = top_ref.shape[1]
    levels = coef_ref.shape[1]
    span = state.shape[1]
    state[:, :reach] = top_ref[:fields]
    state[:, reach : reach + rows] = tile_ref[...]
    state[:, reach + rows :] = bottom_ref[:fields]
    aux[:, :reach] = top_ref[fields:]
    aux[:, reach : reach + rows] = aux_ref[...]
    aux[:, reach + rows :] = bottom_ref[fields:]

    lane = lax.broadcasted_iota(jnp.int32, (span, width), 1)
    first_lane = lane == 0
    last_lane = lane == width - 1

    def east(f):
        return pltpu.roll(f, span - 1, 0)

    def west(f):
        return pltpu.roll(f, 1, 0)

    def north(f):
        return jnp.where(last_lane, 0.0, pltpu.roll(f, width - 1, 1))

    def south(f):
        return jnp.where(first_lane, 0.0, pltpu.roll(f, 1, 1))

    def parts(f):
        e, w, n, s = east(f), west(f), north(f), south(f)
        return (e - w) * 0.5, (n - s) * 0.5, e + w + n + s - 4.0 * f

    depth = aux[extra - 1]
    masks = [(k < depth).astype(jnp.float32) for k in range(levels)]
    surface = masks[0]
    for field in range(fields):
        state[field] = state[field] * masks[field % levels]
    for step in range(STEPS):
        spread = None
        for k in range(levels):
            ddx_u = parts(state[k])[0]
            ddy_v = parts(state[levels + k])[1]
            term = (coef_ref[0, k] * masks[k]) * (ddx_u + ddy_v)
            spread = term if spread is None else spread + term
        height = state[3 * levels]
        height_one = surface * (height - DT * spread)
        hit = hit_ref[step]
        height_two = surface * (height_one + NUDGE * hit * (aux[step] - height_one))
        grad_x, grad_y, unused = parts(height_two)
        for k in range(levels):
            visc = 0.2 * coef_ref[1, k]
            kappa = 0.2 * coef_ref[2, k]
            east_vel = state[k]
            north_vel = state[levels + k]
            temper = state[2 * levels + k]
            unused_x, unused_y, lap_u = parts(east_vel)
            unused_x, unused_y, lap_v = parts(north_vel)
            ddx_t, ddy_t, lap_t = parts(temper)
            state[k] = masks[k] * (
                east_vel + DT * (CORIOLIS * north_vel - grad_x + visc * lap_u)
            )
            state[levels + k] = masks[k] * (
                north_vel + DT * (-CORIOLIS * east_vel - grad_y + visc * lap_v)
            )
            state[2 * levels + k] = masks[k] * (
                temper + DT * (kappa * lap_t - east_vel * ddx_t - north_vel * ddy_t)
            )
        state[3 * levels] = height_two
    out_ref[...] = state[:, reach : reach + rows]


def run_steps(coefs, tile, aux, top, bottom, hits):
    fields, rows, width = tile.shape
    span = rows + 2 * top.shape[1]
    vmem = pl.BlockSpec(memory_space=pltpu.VMEM)
    return pl.pallas_call(
        stencil_kernel,
        out_shape=jax.ShapeDtypeStruct(tile.shape, tile.dtype),
        in_specs=[pl.BlockSpec(memory_space=pltpu.SMEM)] + [vmem] * 5,
        out_specs=vmem,
        scratch_shapes=[
            pltpu.VMEM((fields, span, width), tile.dtype),
            pltpu.VMEM((aux.shape[0], span, width), tile.dtype),
        ],
    )(coefs, tile, aux, top, bottom, hits)


def per_device(ensemble, ancestors, depth_levels, level_coefs, altimetry, obs_rows):
    width_y = ensemble.shape[3]
    reach = 8
    tile, gathered = resample(ensemble[0], ancestors, altimetry)
    all_lines = jnp.moveaxis(gathered, 0, 1).reshape(
        (altimetry.shape[0], -1) + altimetry.shape[2:]
    )
    columns = jnp.arange(width_y, dtype=jnp.int32)
    targets = []
    hits = []
    for step in range(STEPS):
        onehot = (obs_rows[step][:, None] == columns[None, :]).astype(jnp.float32)
        targets.append(
            jnp.dot(
                all_lines[step].T, onehot, precision=lax.Precision.HIGHEST,
                preferred_element_type=jnp.float32,
            )
        )
        hits.append(jnp.sum(onehot, axis=0)[None, :])
    aux = jnp.stack(targets + [depth_levels.astype(jnp.float32)], axis=0)
    count = lax.axis_size("space")
    forward = [(i, (i + 1) % count) for i in range(count)]
    backward = [(target, source) for source, target in forward]
    low = jnp.concatenate([tile[:, :reach], aux[:, :reach]], axis=0)
    high = jnp.concatenate([tile[:, -reach:], aux[:, -reach:]], axis=0)
    top = lax.ppermute(high, "space", forward)
    bottom = lax.ppermute(low, "space", backward)
    state = run_steps(level_coefs, tile, aux, top, bottom, jnp.stack(hits, axis=0))
    return state[None]


def solution(mesh):
    in_specs = (
        P("particle", None, "space", None),
        P(),
        P("space", None),
        P(),
        P(None, "particle", "space"),
        P(),
    )
    out_specs = P("particle", None, "space", None)
    return jax.shard_map(
        per_device, mesh=mesh, in_specs=in_specs, out_specs=out_specs, check_vma=False
    )
```

```python
import functools

import jax
import jax.numpy as jnp
from jax import lax
from jax.experimental import pallas as pl
from jax.experimental.pallas import tpu as pltpu
from jax.sharding import PartitionSpec as P

MESH = pl.DeviceIdType.MESH

STEPS = 3


DT = 0.2
CORIOLIS = 0.5
GRAVITY = 1.0
NUDGE = 0.5


def with_halo(block, sides, width):
    for axis, dim in sides:
        count = lax.axis_size(axis)
        forward = [(i, i + 1) for i in range(count - 1)]
        forward.append((count - 1, 0))
        backward = [(target, source) for source, target in forward]
        low = lax.ppermute(
            lax.slice_in_dim(block, block.shape[dim] - width, None, axis=dim), axis, forward
        )
        high = lax.ppermute(lax.slice_in_dim(block, 0, width, axis=dim), axis, backward)
        block = jnp.concatenate([low, block, high], axis=dim)
    return block


def pad_second(field):
    return jnp.pad(field, [(0, 0)] * (field.ndim - 1) + [(1, 1)])


def gradients(wide):
    center = wide[:, 1:-1]
    east = wide[:, 2:]
    west = wide[:, :-2]
    padded = pad_second(center)
    ddx = (east - west) * 0.5
    ddy = (padded[..., 2:] - padded[..., :-2]) * 0.5
    laplace = east + west + padded[..., 2:] + padded[..., :-2] - 4.0 * center
    return (center, ddx, ddy, laplace)


def widen_state(field):
    return with_halo(field, (("space", 1),), 1)


def widen_surface(field):
    return with_halo(field, (("space", 1),), 1)


def level_terms(coefs):
    thick = coefs[0][:, None, None]
    visc = 0.2 * coefs[1][:, None, None]
    kappa = 0.2 * coefs[2][:, None, None]
    return (thick, visc, kappa)


def finish(center, ddx, ddy, laplace, masks, visc, kappa, grad_x, grad_y, height_two):
    levels = masks.shape[0]
    east_vel = center[:levels]
    north_vel = center[levels : 2 * levels]
    temper = center[2 * levels : 3 * levels]
    east_new = masks * (
        east_vel + DT * (CORIOLIS * north_vel - GRAVITY * grad_x + visc * laplace[:levels])
    )
    north_new = masks * (
        north_vel
        + DT * (-CORIOLIS * east_vel - GRAVITY * grad_y + visc * laplace[levels : 2 * levels])
    )
    temper_new = masks * (
        temper
        + DT
        * (
            kappa * laplace[2 * levels : 3 * levels]
            - east_vel * ddx[2 * levels : 3 * levels]
            - north_vel * ddy[2 * levels : 3 * levels]
        )
    )
    return jnp.concatenate([east_new, north_new, temper_new, height_two[None]], axis=0)


def one_step(state, masks, coefs, target, hit):
    levels = masks.shape[0]
    surface = masks[0]
    center, ddx, ddy, laplace = gradients(widen_state(state))
    height = center[3 * levels]
    thick, visc, kappa = level_terms(coefs)
    spread = ddx[:levels] + ddy[levels : 2 * levels]
    height_one = surface * (height - DT * jnp.sum(thick * masks * spread, axis=0))
    height_two = surface * (height_one + NUDGE * hit * (target - height_one))
    unused, grad_x, grad_y, unused_lap = gradients(widen_surface(height_two[None]))
    return finish(center, ddx, ddy, laplace, masks, visc, kappa, grad_x, grad_y, height_two)


def window(source, grid_cols, rows, cols):
    return (pl.ds((source // grid_cols) * rows, rows), pl.ds((source % grid_cols) * cols, cols))


def exchange_kernel(
    count, grid_cols, groups, anc_ref, ens_ref, alt_ref, out_ref, lines_ref,
    held_a, held_b, outgoing_a, outgoing_b, send1, recv1, send2, recv2, send3, recv3, local,
):
    me = lax.axis_index("particle")
    held = (held_a, held_b)
    outgoing = (outgoing_a, outgoing_b)
    rows, cols = held_a.shape[2], held_a.shape[3]

    barrier = pltpu.get_barrier_semaphore()
    for offset in range(1, count):
        peer = lax.rem(me + offset, count)
        pl.semaphore_signal(barrier, inc=1, device_id={"particle": peer}, device_id_type=MESH)
    pl.semaphore_wait(barrier, count - 1)

    def chunk_of(dest, fields):
        r, c = window(dest, grid_cols, rows, cols)
        return ens_ref.at[fields, r, c]

    def first_copy(group, fields, offset, peer):
        return pltpu.make_async_remote_copy(
            src_ref=chunk_of(peer, fields), dst_ref=held[group].at[me],
            send_sem=send1.at[group, offset], recv_sem=recv1.at[group, me],
            device_id={"particle": peer}, device_id_type=MESH,
        )

    def second_copy(group, fields, offset, peer):
        r_me, c_me = window(me, grid_cols, rows, cols)
        return pltpu.make_async_remote_copy(
            src_ref=outgoing[group].at[peer], dst_ref=out_ref.at[fields, r_me, c_me],
            send_sem=send2.at[group, offset], recv_sem=recv2.at[group, me],
            device_id={"particle": peer}, device_id_type=MESH,
        )

    own_lines = pltpu.make_async_copy(alt_ref, lines_ref.at[me], local.at[0])
    own_lines.start()
    line_copies = []
    for offset in range(1, count):
        peer = lax.rem(me + offset, count)
        lines = pltpu.make_async_remote_copy(
            src_ref=alt_ref, dst_ref=lines_ref.at[me], send_sem=send3.at[offset],
            recv_sem=recv3.at[me], device_id={"particle": peer}, device_id_type=MESH,
        )
        lines.start()
        line_copies.append(lines)

    own_parts = []
    firsts = []
    for group, fields in enumerate(groups):
        own = pltpu.make_async_copy(chunk_of(me, fields), held[group].at[me], local.at[1 + group])
        own.start()
        own_parts.append(own)
        copies = []
        for offset in range(1, count):
            copy = first_copy(group, fields, offset, lax.rem(me + offset, count))
            copy.start()
            copies.append(copy)
        firsts.append(copies)

    seconds = []
    for group, fields in enumerate(groups):
        own_parts[group].wait()
        for offset, copy in zip(range(1, count), firsts[group]):
            sender = lax.rem(me + count - offset, count)
            copy.wait_send()
            pltpu.make_async_remote_copy(
                src_ref=chunk_of(me, fields), dst_ref=held[group].at[sender],
                send_sem=send1.at[group, offset], recv_sem=recv1.at[group, sender],
                device_id={"particle": sender}, device_id_type=MESH,
            ).wait_recv()
        for member in range(count):
            source = jnp.clip(anc_ref[member], 0, count - 1)
            outgoing[group][member] = held[group][source]
        r_me, c_me = window(me, grid_cols, rows, cols)
        mine = pltpu.make_async_copy(
            outgoing[group].at[me], out_ref.at[fields, r_me, c_me], local.at[3 + group]
        )
        mine.start()
        copies = [mine]
        for offset in range(1, count):
            copy = second_copy(group, fields, offset, lax.rem(me + offset, count))
            copy.start()
            copies.append(copy)
        seconds.append(copies)

    own_lines.wait()
    for offset, lines in zip(range(1, count), line_copies):
        sender = lax.rem(me + count - offset, count)
        lines.wait_send()
        pltpu.make_async_remote_copy(
            src_ref=alt_ref, dst_ref=lines_ref.at[sender], send_sem=send3.at[offset],
            recv_sem=recv3.at[sender], device_id={"particle": sender}, device_id_type=MESH,
        ).wait_recv()
    for group, fields in enumerate(groups):
        seconds[group][0].wait()
        for offset, copy in zip(range(1, count), seconds[group][1:]):
            sender = lax.rem(me + count - offset, count)
            r_s, c_s = window(sender, grid_cols, rows, cols)
            copy.wait_send()
            pltpu.make_async_remote_copy(
                src_ref=outgoing[group].at[me], dst_ref=out_ref.at[fields, r_s, c_s],
                send_sem=send2.at[group, offset], recv_sem=recv2.at[group, sender],
                device_id={"particle": sender}, device_id_type=MESH,
            ).wait_recv()


def resample(tile, ancestors, altimetry):
    count = lax.axis_size("particle")
    fields, height, width = tile.shape
    grid_rows = 4
    grid_cols = count // grid_rows
    rows, cols = height // grid_rows, width // grid_cols
    split = (fields + 1) // 2
    groups = (pl.ds(0, split), pl.ds(split, fields - split))
    sems = pltpu.SemaphoreType.DMA((count,))
    grouped = pltpu.SemaphoreType.DMA((len(groups), count))
    return pl.pallas_call(
        functools.partial(exchange_kernel, count, grid_cols, groups),
        out_shape=(
            jax.ShapeDtypeStruct(tile.shape, tile.dtype),
            jax.ShapeDtypeStruct((count,) + altimetry.shape, altimetry.dtype),
        ),
        in_specs=[
            pl.BlockSpec(memory_space=pltpu.SMEM),
            pl.BlockSpec(memory_space=pl.ANY),
            pl.BlockSpec(memory_space=pltpu.VMEM),
        ],
        out_specs=(
            pl.BlockSpec(memory_space=pl.ANY),
            pl.BlockSpec(memory_space=pltpu.VMEM),
        ),
        scratch_shapes=[
            pltpu.VMEM((count, split, rows, cols), tile.dtype),
            pltpu.VMEM((count, fields - split, rows, cols), tile.dtype),
            pltpu.VMEM((count, split, rows, cols), tile.dtype),
            pltpu.VMEM((count, fields - split, rows, cols), tile.dtype),
            grouped, grouped, grouped, grouped, sems, sems,
            pltpu.SemaphoreType.DMA((1 + 2 * len(groups),)),
        ],
        compiler_params=pltpu.CompilerParams(collective_id=0, has_side_effects=True),
    )(ancestors, tile, altimetry)


def stencil_kernel(
    coef_ref, tile_ref, aux_ref, top_ref, bottom_ref, top_aux_ref, bottom_aux_ref, hit_ref,
    out_ref, state, aux,
):
    fields, rows, width = tile_ref.shape
    extra = aux_ref.shape[0]
    reach = top_ref.shape[1]
    levels = coef_ref.shape[1]
    span = state.shape[1]
    state[:, :reach] = top_ref[...]
    state[:, reach : reach + rows] = tile_ref[...]
    state[:, reach + rows :] = bottom_ref[...]
    aux[:, :reach] = top_aux_ref[...]
    aux[:, reach : reach + rows] = aux_ref[...]
    aux[:, reach + rows :] = bottom_aux_ref[...]

    lane = lax.broadcasted_iota(jnp.int32, (span, width), 1)
    first_lane = lane == 0
    last_lane = lane == width - 1

    def east(f):
        return pltpu.roll(f, span - 1, 0)

    def west(f):
        return pltpu.roll(f, 1, 0)

    def north(f):
        return jnp.where(last_lane, 0.0, pltpu.roll(f, width - 1, 1))

    def south(f):
        return jnp.where(first_lane, 0.0, pltpu.roll(f, 1, 1))

    def parts(f):
        e, w, n, s = east(f), west(f), north(f), south(f)
        return (e - w) * 0.5, (n - s) * 0.5, e + w + n + s - 4.0 * f

    depth = aux[extra - 1]
    masks = [(k < depth).astype(jnp.float32) for k in range(levels)]
    surface = masks[0]
    for field in range(fields):
        state[field] = state[field] * masks[field % levels]
    for step in range(STEPS):
        spread = None
        for k in range(levels):
            ddx_u = parts(state[k])[0]
            ddy_v = parts(state[levels + k])[1]
            term = (coef_ref[0, k] * masks[k]) * (ddx_u + ddy_v)
            spread = term if spread is None else spread + term
        height = state[3 * levels]
        height_one = surface * (height - DT * spread)
        hit = hit_ref[step]
        height_two = surface * (height_one + NUDGE * hit * (aux[step] - height_one))
        grad_x, grad_y, unused = parts(height_two)
        for k in range(levels):
            visc = 0.2 * coef_ref[1, k]
            kappa = 0.2 * coef_ref[2, k]
            east_vel = state[k]
            north_vel = state[levels + k]
            temper = state[2 * levels + k]
            unused_x, unused_y, lap_u = parts(east_vel)
            unused_x, unused_y, lap_v = parts(north_vel)
            ddx_t, ddy_t, lap_t = parts(temper)
            state[k] = masks[k] * (
                east_vel + DT * (CORIOLIS * north_vel - grad_x + visc * lap_u)
            )
            state[levels + k] = masks[k] * (
                north_vel + DT * (-CORIOLIS * east_vel - grad_y + visc * lap_v)
            )
            state[2 * levels + k] = masks[k] * (
                temper + DT * (kappa * lap_t - east_vel * ddx_t - north_vel * ddy_t)
            )
        state[3 * levels] = height_two
    out_ref[...] = state[:, reach : reach + rows]


def run_steps(coefs, tile, aux, top, bottom, top_aux, bottom_aux, hits):
    fields, rows, width = tile.shape
    span = rows + 2 * top.shape[1]
    vmem = pl.BlockSpec(memory_space=pltpu.VMEM)
    return pl.pallas_call(
        stencil_kernel,
        out_shape=jax.ShapeDtypeStruct(tile.shape, tile.dtype),
        in_specs=[pl.BlockSpec(memory_space=pltpu.SMEM)] + [vmem] * 7,
        out_specs=vmem,
        scratch_shapes=[
            pltpu.VMEM((fields, span, width), tile.dtype),
            pltpu.VMEM((aux.shape[0], span, width), tile.dtype),
        ],
    )(coefs, tile, aux, top, bottom, top_aux, bottom_aux, hits)


def per_device(ensemble, ancestors, depth_levels, level_coefs, altimetry, obs_rows):
    width_y = ensemble.shape[3]
    reach = 8
    tile, gathered = resample(ensemble[0], ancestors, altimetry)
    count = lax.axis_size("space")
    forward = [(i, (i + 1) % count) for i in range(count)]
    backward = [(target, source) for source, target in forward]
    top = lax.ppermute(tile[:, -reach:], "space", forward)
    bottom = lax.ppermute(tile[:, :reach], "space", backward)
    all_lines = jnp.moveaxis(gathered, 0, 1).reshape(
        (altimetry.shape[0], -1) + altimetry.shape[2:]
    )
    columns = jnp.arange(width_y, dtype=jnp.int32)
    targets = []
    hits = []
    for step in range(STEPS):
        onehot = (obs_rows[step][:, None] == columns[None, :]).astype(jnp.float32)
        targets.append(
            jnp.dot(
                all_lines[step].T, onehot, precision=lax.Precision.HIGHEST,
                preferred_element_type=jnp.float32,
            )
        )
        hits.append(jnp.sum(onehot, axis=0)[None, :])
    aux = jnp.stack(targets + [depth_levels.astype(jnp.float32)], axis=0)
    top_aux = lax.ppermute(aux[:, -reach:], "space", forward)
    bottom_aux = lax.ppermute(aux[:, :reach], "space", backward)
    state = run_steps(
        level_coefs, tile, aux, top, bottom, top_aux, bottom_aux, jnp.stack(hits, axis=0)
    )
    return state[None]


def solution(mesh):
    in_specs = (
        P("particle", None, "space", None),
        P(),
        P("space", None),
        P(),
        P(None, "particle", "space"),
        P(),
    )
    out_specs = P("particle", None, "space", None)
    return jax.shard_map(
        per_device, mesh=mesh, in_specs=in_specs, out_specs=out_specs, check_vma=False
    )
```

```python
import functools

import jax
import jax.numpy as jnp
from jax import lax
from jax.experimental import pallas as pl
from jax.experimental.pallas import tpu as pltpu
from jax.sharding import PartitionSpec as P

MESH = pl.DeviceIdType.MESH

STEPS = 3


DT = 0.2
CORIOLIS = 0.5
GRAVITY = 1.0
NUDGE = 0.5


def with_halo(block, sides, width):
    for axis, dim in sides:
        count = lax.axis_size(axis)
        forward = [(i, i + 1) for i in range(count - 1)]
        forward.append((count - 1, 0))
        backward = [(target, source) for source, target in forward]
        low = lax.ppermute(
            lax.slice_in_dim(block, block.shape[dim] - width, None, axis=dim), axis, forward
        )
        high = lax.ppermute(lax.slice_in_dim(block, 0, width, axis=dim), axis, backward)
        block = jnp.concatenate([low, block, high], axis=dim)
    return block


def pad_second(field):
    return jnp.pad(field, [(0, 0)] * (field.ndim - 1) + [(1, 1)])


def gradients(wide):
    center = wide[:, 1:-1]
    east = wide[:, 2:]
    west = wide[:, :-2]
    padded = pad_second(center)
    ddx = (east - west) * 0.5
    ddy = (padded[..., 2:] - padded[..., :-2]) * 0.5
    laplace = east + west + padded[..., 2:] + padded[..., :-2] - 4.0 * center
    return (center, ddx, ddy, laplace)


def widen_state(field):
    return with_halo(field, (("space", 1),), 1)


def widen_surface(field):
    return with_halo(field, (("space", 1),), 1)


def level_terms(coefs):
    thick = coefs[0][:, None, None]
    visc = 0.2 * coefs[1][:, None, None]
    kappa = 0.2 * coefs[2][:, None, None]
    return (thick, visc, kappa)


def finish(center, ddx, ddy, laplace, masks, visc, kappa, grad_x, grad_y, height_two):
    levels = masks.shape[0]
    east_vel = center[:levels]
    north_vel = center[levels : 2 * levels]
    temper = center[2 * levels : 3 * levels]
    east_new = masks * (
        east_vel + DT * (CORIOLIS * north_vel - GRAVITY * grad_x + visc * laplace[:levels])
    )
    north_new = masks * (
        north_vel
        + DT * (-CORIOLIS * east_vel - GRAVITY * grad_y + visc * laplace[levels : 2 * levels])
    )
    temper_new = masks * (
        temper
        + DT
        * (
            kappa * laplace[2 * levels : 3 * levels]
            - east_vel * ddx[2 * levels : 3 * levels]
            - north_vel * ddy[2 * levels : 3 * levels]
        )
    )
    return jnp.concatenate([east_new, north_new, temper_new, height_two[None]], axis=0)


def one_step(state, masks, coefs, target, hit):
    levels = masks.shape[0]
    surface = masks[0]
    center, ddx, ddy, laplace = gradients(widen_state(state))
    height = center[3 * levels]
    thick, visc, kappa = level_terms(coefs)
    spread = ddx[:levels] + ddy[levels : 2 * levels]
    height_one = surface * (height - DT * jnp.sum(thick * masks * spread, axis=0))
    height_two = surface * (height_one + NUDGE * hit * (target - height_one))
    unused, grad_x, grad_y, unused_lap = gradients(widen_surface(height_two[None]))
    return finish(center, ddx, ddy, laplace, masks, visc, kappa, grad_x, grad_y, height_two)


def window(source, grid_cols, rows, cols):
    return (pl.ds((source // grid_cols) * rows, rows), pl.ds((source % grid_cols) * cols, cols))


def exchange_kernel(
    count, grid_cols, groups, reach, anc_ref, ens_ref, alt_ref, out_ref, lines_ref, low_ref, high_ref,
    held_a, held_b, outgoing_a, outgoing_b, send1, recv1, send2, recv2, send3, recv3, local, edge_sems,
):
    me = lax.axis_index("particle")
    held = (held_a, held_b)
    outgoing = (outgoing_a, outgoing_b)
    rows, cols = held_a.shape[2], held_a.shape[3]

    barrier = pltpu.get_barrier_semaphore()
    for offset in range(1, count):
        peer = lax.rem(me + offset, count)
        pl.semaphore_signal(barrier, inc=1, device_id={"particle": peer}, device_id_type=MESH)
    pl.semaphore_wait(barrier, count - 1)

    def chunk_of(dest, fields):
        r, c = window(dest, grid_cols, rows, cols)
        return ens_ref.at[fields, r, c]

    def first_copy(group, fields, offset, peer):
        return pltpu.make_async_remote_copy(
            src_ref=chunk_of(peer, fields), dst_ref=held[group].at[me],
            send_sem=send1.at[group, offset], recv_sem=recv1.at[group, me],
            device_id={"particle": peer}, device_id_type=MESH,
        )

    def second_copy(group, fields, offset, peer):
        r_me, c_me = window(me, grid_cols, rows, cols)
        return pltpu.make_async_remote_copy(
            src_ref=outgoing[group].at[peer], dst_ref=out_ref.at[fields, r_me, c_me],
            send_sem=send2.at[group, offset], recv_sem=recv2.at[group, me],
            device_id={"particle": peer}, device_id_type=MESH,
        )

    own_lines = pltpu.make_async_copy(alt_ref, lines_ref.at[me], local.at[0])
    own_lines.start()
    line_copies = []
    for offset in range(1, count):
        peer = lax.rem(me + offset, count)
        lines = pltpu.make_async_remote_copy(
            src_ref=alt_ref, dst_ref=lines_ref.at[me], send_sem=send3.at[offset],
            recv_sem=recv3.at[me], device_id={"particle": peer}, device_id_type=MESH,
        )
        lines.start()
        line_copies.append(lines)

    own_parts = []
    firsts = []
    for group, fields in enumerate(groups):
        own = pltpu.make_async_copy(chunk_of(me, fields), held[group].at[me], local.at[1 + group])
        own.start()
        own_parts.append(own)
        copies = []
        for offset in range(1, count):
            copy = first_copy(group, fields, offset, lax.rem(me + offset, count))
            copy.start()
            copies.append(copy)
        firsts.append(copies)

    seconds = []
    for group, fields in enumerate(groups):
        own_parts[group].wait()
        for offset, copy in zip(range(1, count), firsts[group]):
            sender = lax.rem(me + count - offset, count)
            copy.wait_send()
            pltpu.make_async_remote_copy(
                src_ref=chunk_of(me, fields), dst_ref=held[group].at[sender],
                send_sem=send1.at[group, offset], recv_sem=recv1.at[group, sender],
                device_id={"particle": sender}, device_id_type=MESH,
            ).wait_recv()
        for member in range(count):
            source = jnp.clip(anc_ref[member], 0, count - 1)
            outgoing[group][member] = held[group][source]
        r_me, c_me = window(me, grid_cols, rows, cols)
        mine = pltpu.make_async_copy(
            outgoing[group].at[me], out_ref.at[fields, r_me, c_me], local.at[3 + group]
        )
        mine.start()
        copies = [mine]
        for offset in range(1, count):
            copy = second_copy(group, fields, offset, lax.rem(me + offset, count))
            copy.start()
            copies.append(copy)
        seconds.append(copies)

    own_lines.wait()
    for offset, lines in zip(range(1, count), line_copies):
        sender = lax.rem(me + count - offset, count)
        lines.wait_send()
        pltpu.make_async_remote_copy(
            src_ref=alt_ref, dst_ref=lines_ref.at[sender], send_sem=send3.at[offset],
            recv_sem=recv3.at[sender], device_id={"particle": sender}, device_id_type=MESH,
        ).wait_recv()
    height = out_ref.shape[1]
    edges = []
    for group, fields in enumerate(groups):
        seconds[group][0].wait()
        for offset, copy in zip(range(1, count), seconds[group][1:]):
            sender = lax.rem(me + count - offset, count)
            r_s, c_s = window(sender, grid_cols, rows, cols)
            copy.wait_send()
            pltpu.make_async_remote_copy(
                src_ref=outgoing[group].at[me], dst_ref=out_ref.at[fields, r_s, c_s],
                send_sem=send2.at[group, offset], recv_sem=recv2.at[group, sender],
                device_id={"particle": sender}, device_id_type=MESH,
            ).wait_recv()
        for turn, (start, target) in enumerate(((0, low_ref), (height - reach, high_ref))):
            edge = pltpu.make_async_copy(
                out_ref.at[fields, pl.ds(start, reach)], target.at[fields],
                edge_sems.at[2 * group + turn],
            )
            edge.start()
            edges.append(edge)
    for edge in edges:
        edge.wait()


def resample(tile, ancestors, altimetry, reach):
    count = lax.axis_size("particle")
    fields, height, width = tile.shape
    grid_rows = 4
    grid_cols = count // grid_rows
    rows, cols = height // grid_rows, width // grid_cols
    split = (fields + 1) // 2
    groups = (pl.ds(0, split), pl.ds(split, fields - split))
    sems = pltpu.SemaphoreType.DMA((count,))
    grouped = pltpu.SemaphoreType.DMA((len(groups), count))
    return pl.pallas_call(
        functools.partial(exchange_kernel, count, grid_cols, groups, reach),
        out_shape=(
            jax.ShapeDtypeStruct(tile.shape, tile.dtype),
            jax.ShapeDtypeStruct((count,) + altimetry.shape, altimetry.dtype),
            jax.ShapeDtypeStruct((fields, reach, width), tile.dtype),
            jax.ShapeDtypeStruct((fields, reach, width), tile.dtype),
        ),
        in_specs=[
            pl.BlockSpec(memory_space=pltpu.SMEM),
            pl.BlockSpec(memory_space=pl.ANY),
            pl.BlockSpec(memory_space=pltpu.VMEM),
        ],
        out_specs=(
            pl.BlockSpec(memory_space=pl.ANY),
            pl.BlockSpec(memory_space=pltpu.VMEM),
            pl.BlockSpec(memory_space=pltpu.VMEM),
            pl.BlockSpec(memory_space=pltpu.VMEM),
        ),
        scratch_shapes=[
            pltpu.VMEM((count, split, rows, cols), tile.dtype),
            pltpu.VMEM((count, fields - split, rows, cols), tile.dtype),
            pltpu.VMEM((count, split, rows, cols), tile.dtype),
            pltpu.VMEM((count, fields - split, rows, cols), tile.dtype),
            grouped, grouped, grouped, grouped, sems, sems,
            pltpu.SemaphoreType.DMA((1 + 2 * len(groups),)),
            pltpu.SemaphoreType.DMA((2 * len(groups),)),
        ],
        compiler_params=pltpu.CompilerParams(collective_id=0, has_side_effects=True),
    )(ancestors, tile, altimetry)


def stencil_kernel(
    coef_ref, tile_ref, aux_ref, top_ref, bottom_ref, top_aux_ref, bottom_aux_ref, hit_ref,
    out_ref, state, aux,
):
    fields, rows, width = tile_ref.shape
    extra = aux_ref.shape[0]
    reach = top_ref.shape[1]
    levels = coef_ref.shape[1]
    span = state.shape[1]
    state[:, :reach] = top_ref[...]
    state[:, reach : reach + rows] = tile_ref[...]
    state[:, reach + rows :] = bottom_ref[...]
    aux[:, :reach] = top_aux_ref[...]
    aux[:, reach : reach + rows] = aux_ref[...]
    aux[:, reach + rows :] = bottom_aux_ref[...]

    lane = lax.broadcasted_iota(jnp.int32, (span, width), 1)
    first_lane = lane == 0
    last_lane = lane == width - 1

    def east(f):
        return pltpu.roll(f, span - 1, 0)

    def west(f):
        return pltpu.roll(f, 1, 0)

    def north(f):
        return jnp.where(last_lane, 0.0, pltpu.roll(f, width - 1, 1))

    def south(f):
        return jnp.where(first_lane, 0.0, pltpu.roll(f, 1, 1))

    def parts(f):
        e, w, n, s = east(f), west(f), north(f), south(f)
        return (e - w) * 0.5, (n - s) * 0.5, e + w + n + s - 4.0 * f

    depth = aux[extra - 1]
    masks = [(k < depth).astype(jnp.float32) for k in range(levels)]
    surface = masks[0]
    for field in range(fields):
        state[field] = state[field] * masks[field % levels]
    for step in range(STEPS):
        spread = None
        for k in range(levels):
            ddx_u = parts(state[k])[0]
            ddy_v = parts(state[levels + k])[1]
            term = (coef_ref[0, k] * masks[k]) * (ddx_u + ddy_v)
            spread = term if spread is None else spread + term
        height = state[3 * levels]
        height_one = surface * (height - DT * spread)
        hit = hit_ref[step]
        height_two = surface * (height_one + NUDGE * hit * (aux[step] - height_one))
        grad_x, grad_y, unused = parts(height_two)
        for k in range(levels):
            visc = 0.2 * coef_ref[1, k]
            kappa = 0.2 * coef_ref[2, k]
            east_vel = state[k]
            north_vel = state[levels + k]
            temper = state[2 * levels + k]
            unused_x, unused_y, lap_u = parts(east_vel)
            unused_x, unused_y, lap_v = parts(north_vel)
            ddx_t, ddy_t, lap_t = parts(temper)
            state[k] = masks[k] * (
                east_vel + DT * (CORIOLIS * north_vel - grad_x + visc * lap_u)
            )
            state[levels + k] = masks[k] * (
                north_vel + DT * (-CORIOLIS * east_vel - grad_y + visc * lap_v)
            )
            state[2 * levels + k] = masks[k] * (
                temper + DT * (kappa * lap_t - east_vel * ddx_t - north_vel * ddy_t)
            )
        state[3 * levels] = height_two
    out_ref[...] = state[:, reach : reach + rows]


def run_steps(coefs, tile, aux, top, bottom, top_aux, bottom_aux, hits):
    fields, rows, width = tile.shape
    span = rows + 2 * top.shape[1]
    vmem = pl.BlockSpec(memory_space=pltpu.VMEM)
    return pl.pallas_call(
        stencil_kernel,
        out_shape=jax.ShapeDtypeStruct(tile.shape, tile.dtype),
        in_specs=[pl.BlockSpec(memory_space=pltpu.SMEM)] + [vmem] * 7,
        out_specs=vmem,
        scratch_shapes=[
            pltpu.VMEM((fields, span, width), tile.dtype),
            pltpu.VMEM((aux.shape[0], span, width), tile.dtype),
        ],
    )(coefs, tile, aux, top, bottom, top_aux, bottom_aux, hits)


def per_device(ensemble, ancestors, depth_levels, level_coefs, altimetry, obs_rows):
    width_y = ensemble.shape[3]
    reach = 8
    tile, gathered, low, high = resample(ensemble[0], ancestors, altimetry, reach)
    count = lax.axis_size("space")
    forward = [(i, (i + 1) % count) for i in range(count)]
    backward = [(target, source) for source, target in forward]
    top = lax.ppermute(high, "space", forward)
    bottom = lax.ppermute(low, "space", backward)
    all_lines = jnp.moveaxis(gathered, 0, 1).reshape(
        (altimetry.shape[0], -1) + altimetry.shape[2:]
    )
    columns = jnp.arange(width_y, dtype=jnp.int32)
    targets = []
    hits = []
    for step in range(STEPS):
        onehot = (obs_rows[step][:, None] == columns[None, :]).astype(jnp.float32)
        targets.append(
            jnp.dot(
                all_lines[step].T, onehot, precision=lax.Precision.HIGHEST,
                preferred_element_type=jnp.float32,
            )
        )
        hits.append(jnp.sum(onehot, axis=0)[None, :])
    aux = jnp.stack(targets + [depth_levels.astype(jnp.float32)], axis=0)
    top_aux = lax.ppermute(aux[:, -reach:], "space", forward)
    bottom_aux = lax.ppermute(aux[:, :reach], "space", backward)
    state = run_steps(
        level_coefs, tile, aux, top, bottom, top_aux, bottom_aux, jnp.stack(hits, axis=0)
    )
    return state[None]


def solution(mesh):
    in_specs = (
        P("particle", None, "space", None),
        P(),
        P("space", None),
        P(),
        P(None, "particle", "space"),
        P(),
    )
    out_specs = P("particle", None, "space", None)
    return jax.shard_map(
        per_device, mesh=mesh, in_specs=in_specs, out_specs=out_specs, check_vma=False
    )
```

```python
import functools

import jax
import jax.numpy as jnp
from jax import lax
from jax.experimental import pallas as pl
from jax.experimental.pallas import tpu as pltpu
from jax.sharding import PartitionSpec as P

MESH = pl.DeviceIdType.MESH

STEPS = 3


DT = 0.2
CORIOLIS = 0.5
GRAVITY = 1.0
NUDGE = 0.5


def with_halo(block, sides, width):
    for axis, dim in sides:
        count = lax.axis_size(axis)
        forward = [(i, i + 1) for i in range(count - 1)]
        forward.append((count - 1, 0))
        backward = [(target, source) for source, target in forward]
        low = lax.ppermute(
            lax.slice_in_dim(block, block.shape[dim] - width, None, axis=dim), axis, forward
        )
        high = lax.ppermute(lax.slice_in_dim(block, 0, width, axis=dim), axis, backward)
        block = jnp.concatenate([low, block, high], axis=dim)
    return block


def pad_second(field):
    return jnp.pad(field, [(0, 0)] * (field.ndim - 1) + [(1, 1)])


def gradients(wide):
    center = wide[:, 1:-1]
    east = wide[:, 2:]
    west = wide[:, :-2]
    padded = pad_second(center)
    ddx = (east - west) * 0.5
    ddy = (padded[..., 2:] - padded[..., :-2]) * 0.5
    laplace = east + west + padded[..., 2:] + padded[..., :-2] - 4.0 * center
    return (center, ddx, ddy, laplace)


def widen_state(field):
    return with_halo(field, (("space", 1),), 1)


def widen_surface(field):
    return with_halo(field, (("space", 1),), 1)


def level_terms(coefs):
    thick = coefs[0][:, None, None]
    visc = 0.2 * coefs[1][:, None, None]
    kappa = 0.2 * coefs[2][:, None, None]
    return (thick, visc, kappa)


def finish(center, ddx, ddy, laplace, masks, visc, kappa, grad_x, grad_y, height_two):
    levels = masks.shape[0]
    east_vel = center[:levels]
    north_vel = center[levels : 2 * levels]
    temper = center[2 * levels : 3 * levels]
    east_new = masks * (
        east_vel + DT * (CORIOLIS * north_vel - GRAVITY * grad_x + visc * laplace[:levels])
    )
    north_new = masks * (
        north_vel
        + DT * (-CORIOLIS * east_vel - GRAVITY * grad_y + visc * laplace[levels : 2 * levels])
    )
    temper_new = masks * (
        temper
        + DT
        * (
            kappa * laplace[2 * levels : 3 * levels]
            - east_vel * ddx[2 * levels : 3 * levels]
            - north_vel * ddy[2 * levels : 3 * levels]
        )
    )
    return jnp.concatenate([east_new, north_new, temper_new, height_two[None]], axis=0)


def one_step(state, masks, coefs, target, hit):
    levels = masks.shape[0]
    surface = masks[0]
    center, ddx, ddy, laplace = gradients(widen_state(state))
    height = center[3 * levels]
    thick, visc, kappa = level_terms(coefs)
    spread = ddx[:levels] + ddy[levels : 2 * levels]
    height_one = surface * (height - DT * jnp.sum(thick * masks * spread, axis=0))
    height_two = surface * (height_one + NUDGE * hit * (target - height_one))
    unused, grad_x, grad_y, unused_lap = gradients(widen_surface(height_two[None]))
    return finish(center, ddx, ddy, laplace, masks, visc, kappa, grad_x, grad_y, height_two)


def window(source, grid_cols, rows, cols):
    return (pl.ds((source // grid_cols) * rows, rows), pl.ds((source % grid_cols) * cols, cols))


def exchange_kernel(
    count, grid_cols, groups, reach, anc_ref, ens_ref, alt_ref, out_ref, lines_ref, low_ref, high_ref,
    held_a, held_b, outgoing_a, outgoing_b, send1, recv1, send2, recv2, send3, recv3, local, edge_sems,
):
    me = lax.axis_index("particle")
    held = (held_a, held_b)
    outgoing = (outgoing_a, outgoing_b)
    rows, cols = held_a.shape[2], held_a.shape[3]

    barrier = pltpu.get_barrier_semaphore()
    for offset in range(1, count):
        peer = lax.rem(me + offset, count)
        pl.semaphore_signal(barrier, inc=1, device_id={"particle": peer}, device_id_type=MESH)
    pl.semaphore_wait(barrier, count - 1)

    def chunk_of(dest, fields):
        r, c = window(dest, grid_cols, rows, cols)
        return ens_ref.at[fields, r, c]

    def first_copy(group, fields, offset, peer):
        return pltpu.make_async_remote_copy(
            src_ref=chunk_of(peer, fields), dst_ref=held[group].at[me],
            send_sem=send1.at[group, offset], recv_sem=recv1.at[group, me],
            device_id={"particle": peer}, device_id_type=MESH,
        )

    def second_copy(group, fields, offset, peer):
        r_me, c_me = window(me, grid_cols, rows, cols)
        return pltpu.make_async_remote_copy(
            src_ref=outgoing[group].at[peer], dst_ref=out_ref.at[fields, r_me, c_me],
            send_sem=send2.at[group, offset], recv_sem=recv2.at[group, me],
            device_id={"particle": peer}, device_id_type=MESH,
        )

    own_lines = pltpu.make_async_copy(alt_ref, lines_ref.at[me], local.at[0])
    own_lines.start()
    line_copies = []
    for offset in range(1, count):
        peer = lax.rem(me + offset, count)
        lines = pltpu.make_async_remote_copy(
            src_ref=alt_ref, dst_ref=lines_ref.at[me], send_sem=send3.at[offset],
            recv_sem=recv3.at[me], device_id={"particle": peer}, device_id_type=MESH,
        )
        lines.start()
        line_copies.append(lines)

    own_parts = []
    firsts = []
    for group, fields in enumerate(groups):
        own = pltpu.make_async_copy(chunk_of(me, fields), held[group].at[me], local.at[1 + group])
        own.start()
        own_parts.append(own)
        copies = []
        for offset in range(1, count):
            copy = first_copy(group, fields, offset, lax.rem(me + offset, count))
            copy.start()
            copies.append(copy)
        firsts.append(copies)

    seconds = []
    for group, fields in enumerate(groups):
        own_parts[group].wait()
        for offset, copy in zip(range(1, count), firsts[group]):
            sender = lax.rem(me + count - offset, count)
            copy.wait_send()
            pltpu.make_async_remote_copy(
                src_ref=chunk_of(me, fields), dst_ref=held[group].at[sender],
                send_sem=send1.at[group, offset], recv_sem=recv1.at[group, sender],
                device_id={"particle": sender}, device_id_type=MESH,
            ).wait_recv()
        for member in range(count):
            source = jnp.clip(anc_ref[member], 0, count - 1)
            outgoing[group][member] = held[group][source]
        r_me, c_me = window(me, grid_cols, rows, cols)
        mine = pltpu.make_async_copy(
            outgoing[group].at[me], out_ref.at[fields, r_me, c_me], local.at[3 + group]
        )
        mine.start()
        copies = [mine]
        for offset in range(1, count):
            copy = second_copy(group, fields, offset, lax.rem(me + offset, count))
            copy.start()
            copies.append(copy)
        seconds.append(copies)

    own_lines.wait()
    for offset, lines in zip(range(1, count), line_copies):
        sender = lax.rem(me + count - offset, count)
        lines.wait_send()
        pltpu.make_async_remote_copy(
            src_ref=alt_ref, dst_ref=lines_ref.at[sender], send_sem=send3.at[offset],
            recv_sem=recv3.at[sender], device_id={"particle": sender}, device_id_type=MESH,
        ).wait_recv()
    height = out_ref.shape[1]
    edges = []
    for group, fields in enumerate(groups):
        seconds[group][0].wait()
        for offset, copy in zip(range(1, count), seconds[group][1:]):
            sender = lax.rem(me + count - offset, count)
            r_s, c_s = window(sender, grid_cols, rows, cols)
            copy.wait_send()
            pltpu.make_async_remote_copy(
                src_ref=outgoing[group].at[me], dst_ref=out_ref.at[fields, r_s, c_s],
                send_sem=send2.at[group, offset], recv_sem=recv2.at[group, sender],
                device_id={"particle": sender}, device_id_type=MESH,
            ).wait_recv()
        for turn, (start, target) in enumerate(((0, low_ref), (height - reach, high_ref))):
            edge = pltpu.make_async_copy(
                out_ref.at[fields, pl.ds(start, reach)], target.at[fields],
                edge_sems.at[2 * group + turn],
            )
            edge.start()
            edges.append(edge)
    for edge in edges:
        edge.wait()


def resample(tile, ancestors, altimetry, reach):
    count = lax.axis_size("particle")
    fields, height, width = tile.shape
    grid_rows = 4
    grid_cols = count // grid_rows
    rows, cols = height // grid_rows, width // grid_cols
    split = (fields + 1) // 2
    groups = (pl.ds(0, split), pl.ds(split, fields - split))
    sems = pltpu.SemaphoreType.DMA((count,))
    grouped = pltpu.SemaphoreType.DMA((len(groups), count))
    return pl.pallas_call(
        functools.partial(exchange_kernel, count, grid_cols, groups, reach),
        out_shape=(
            jax.ShapeDtypeStruct(tile.shape, tile.dtype),
            jax.ShapeDtypeStruct((count,) + altimetry.shape, altimetry.dtype),
            jax.ShapeDtypeStruct((fields, reach, width), tile.dtype),
            jax.ShapeDtypeStruct((fields, reach, width), tile.dtype),
        ),
        in_specs=[
            pl.BlockSpec(memory_space=pltpu.SMEM),
            pl.BlockSpec(memory_space=pl.ANY),
            pl.BlockSpec(memory_space=pltpu.VMEM),
        ],
        out_specs=(
            pl.BlockSpec(memory_space=pl.ANY),
            pl.BlockSpec(memory_space=pltpu.VMEM),
            pl.BlockSpec(memory_space=pltpu.VMEM),
            pl.BlockSpec(memory_space=pltpu.VMEM),
        ),
        scratch_shapes=[
            pltpu.VMEM((count, split, rows, cols), tile.dtype),
            pltpu.VMEM((count, fields - split, rows, cols), tile.dtype),
            pltpu.VMEM((count, split, rows, cols), tile.dtype),
            pltpu.VMEM((count, fields - split, rows, cols), tile.dtype),
            grouped, grouped, grouped, grouped, sems, sems,
            pltpu.SemaphoreType.DMA((1 + 2 * len(groups),)),
            pltpu.SemaphoreType.DMA((2 * len(groups),)),
        ],
        compiler_params=pltpu.CompilerParams(collective_id=0, has_side_effects=True),
    )(ancestors, tile, altimetry)


def stencil_kernel(
    coef_ref, tile_ref, aux_ref, top_ref, bottom_ref, top_aux_ref, bottom_aux_ref, hit_ref,
    out_ref, state, aux,
):
    fields, rows, width = tile_ref.shape
    extra = aux_ref.shape[0]
    reach = top_ref.shape[1]
    levels = coef_ref.shape[1]
    span = state.shape[1]
    state[:, :reach] = top_ref[...]
    state[:, reach : reach + rows] = tile_ref[...]
    state[:, reach + rows :] = bottom_ref[...]
    aux[:, :reach] = top_aux_ref[...]
    aux[:, reach : reach + rows] = aux_ref[...]
    aux[:, reach + rows :] = bottom_aux_ref[...]

    lane = lax.broadcasted_iota(jnp.int32, (span, width), 1)
    first_lane = lane == 0
    last_lane = lane == width - 1

    def east(f):
        return pltpu.roll(f, span - 1, 0)

    def west(f):
        return pltpu.roll(f, 1, 0)

    def north(f):
        return jnp.where(last_lane, 0.0, pltpu.roll(f, width - 1, 1))

    def south(f):
        return jnp.where(first_lane, 0.0, pltpu.roll(f, 1, 1))

    def parts(f):
        e, w, n, s = east(f), west(f), north(f), south(f)
        return (e - w) * 0.5, (n - s) * 0.5, e + w + n + s - 4.0 * f

    depth = aux[extra - 1]
    masks = [(k < depth).astype(jnp.float32) for k in range(levels)]
    surface = masks[0]
    for field in range(fields):
        state[field] = state[field] * masks[field % levels]
    for step in range(STEPS):
        spread = None
        for k in range(levels):
            ddx_u = parts(state[k])[0]
            ddy_v = parts(state[levels + k])[1]
            term = (coef_ref[0, k] * masks[k]) * (ddx_u + ddy_v)
            spread = term if spread is None else spread + term
        height = state[3 * levels]
        height_one = surface * (height - DT * spread)
        hit = hit_ref[step]
        height_two = surface * (height_one + NUDGE * hit * (aux[step] - height_one))
        grad_x, grad_y, unused = parts(height_two)
        for k in range(levels):
            visc = 0.2 * coef_ref[1, k]
            kappa = 0.2 * coef_ref[2, k]
            east_vel = state[k]
            north_vel = state[levels + k]
            temper = state[2 * levels + k]
            unused_x, unused_y, lap_u = parts(east_vel)
            unused_x, unused_y, lap_v = parts(north_vel)
            ddx_t, ddy_t, lap_t = parts(temper)
            state[k] = masks[k] * (
                east_vel + DT * (CORIOLIS * north_vel - grad_x + visc * lap_u)
            )
            state[levels + k] = masks[k] * (
                north_vel + DT * (-CORIOLIS * east_vel - grad_y + visc * lap_v)
            )
            state[2 * levels + k] = masks[k] * (
                temper + DT * (kappa * lap_t - east_vel * ddx_t - north_vel * ddy_t)
            )
        state[3 * levels] = height_two
    out_ref[...] = state[:, reach : reach + rows]


def run_steps(coefs, tile, aux, top, bottom, top_aux, bottom_aux, hits):
    fields, rows, width = tile.shape
    span = rows + 2 * top.shape[1]
    vmem = pl.BlockSpec(memory_space=pltpu.VMEM)
    return pl.pallas_call(
        stencil_kernel,
        out_shape=jax.ShapeDtypeStruct(tile.shape, tile.dtype),
        in_specs=[pl.BlockSpec(memory_space=pltpu.SMEM)] + [vmem] * 7,
        out_specs=vmem,
        scratch_shapes=[
            pltpu.VMEM((fields, span, width), tile.dtype),
            pltpu.VMEM((aux.shape[0], span, width), tile.dtype),
        ],
    )(coefs, tile, aux, top, bottom, top_aux, bottom_aux, hits)


def per_device(ensemble, ancestors, depth_levels, level_coefs, altimetry, obs_rows):
    width_y = ensemble.shape[3]
    reach = 8
    tile, gathered, low, high = resample(ensemble[0], ancestors, altimetry, reach)
    count = lax.axis_size("space")
    forward = [(i, (i + 1) % count) for i in range(count)]
    backward = [(target, source) for source, target in forward]
    all_lines = jnp.moveaxis(gathered, 0, 1).reshape(
        (altimetry.shape[0], -1) + altimetry.shape[2:]
    )
    columns = jnp.arange(width_y, dtype=jnp.int32)
    targets = []
    hits = []
    for step in range(STEPS):
        onehot = (obs_rows[step][:, None] == columns[None, :]).astype(jnp.float32)
        targets.append(
            jnp.dot(
                all_lines[step].T, onehot, precision=lax.Precision.HIGHEST,
                preferred_element_type=jnp.float32,
            )
        )
        hits.append(jnp.sum(onehot, axis=0)[None, :])
    aux = jnp.stack(targets + [depth_levels.astype(jnp.float32)], axis=0)
    fields = tile.shape[0]
    top = lax.ppermute(jnp.concatenate([high, aux[:, -reach:]], axis=0), "space", forward)
    bottom = lax.ppermute(jnp.concatenate([low, aux[:, :reach]], axis=0), "space", backward)
    state = run_steps(
        level_coefs, tile, aux, top[:fields], bottom[:fields], top[fields:], bottom[fields:],
        jnp.stack(hits, axis=0),
    )
    return state[None]


def solution(mesh):
    in_specs = (
        P("particle", None, "space", None),
        P(),
        P("space", None),
        P(),
        P(None, "particle", "space"),
        P(),
    )
    out_specs = P("particle", None, "space", None)
    return jax.shard_map(
        per_device, mesh=mesh, in_specs=in_specs, out_specs=out_specs, check_vma=False
    )
```

```python
import functools

import jax
import jax.numpy as jnp
from jax import lax
from jax.experimental import pallas as pl
from jax.experimental.pallas import tpu as pltpu
from jax.sharding import PartitionSpec as P

MESH = pl.DeviceIdType.MESH

STEPS = 3


DT = 0.2
CORIOLIS = 0.5
GRAVITY = 1.0
NUDGE = 0.5


def with_halo(block, sides, width):
    for axis, dim in sides:
        count = lax.axis_size(axis)
        forward = [(i, i + 1) for i in range(count - 1)]
        forward.append((count - 1, 0))
        backward = [(target, source) for source, target in forward]
        low = lax.ppermute(
            lax.slice_in_dim(block, block.shape[dim] - width, None, axis=dim), axis, forward
        )
        high = lax.ppermute(lax.slice_in_dim(block, 0, width, axis=dim), axis, backward)
        block = jnp.concatenate([low, block, high], axis=dim)
    return block


def pad_second(field):
    return jnp.pad(field, [(0, 0)] * (field.ndim - 1) + [(1, 1)])


def gradients(wide):
    center = wide[:, 1:-1]
    east = wide[:, 2:]
    west = wide[:, :-2]
    padded = pad_second(center)
    ddx = (east - west) * 0.5
    ddy = (padded[..., 2:] - padded[..., :-2]) * 0.5
    laplace = east + west + padded[..., 2:] + padded[..., :-2] - 4.0 * center
    return (center, ddx, ddy, laplace)


def widen_state(field):
    return with_halo(field, (("space", 1),), 1)


def widen_surface(field):
    return with_halo(field, (("space", 1),), 1)


def level_terms(coefs):
    thick = coefs[0][:, None, None]
    visc = 0.2 * coefs[1][:, None, None]
    kappa = 0.2 * coefs[2][:, None, None]
    return (thick, visc, kappa)


def finish(center, ddx, ddy, laplace, masks, visc, kappa, grad_x, grad_y, height_two):
    levels = masks.shape[0]
    east_vel = center[:levels]
    north_vel = center[levels : 2 * levels]
    temper = center[2 * levels : 3 * levels]
    east_new = masks * (
        east_vel + DT * (CORIOLIS * north_vel - GRAVITY * grad_x + visc * laplace[:levels])
    )
    north_new = masks * (
        north_vel
        + DT * (-CORIOLIS * east_vel - GRAVITY * grad_y + visc * laplace[levels : 2 * levels])
    )
    temper_new = masks * (
        temper
        + DT
        * (
            kappa * laplace[2 * levels : 3 * levels]
            - east_vel * ddx[2 * levels : 3 * levels]
            - north_vel * ddy[2 * levels : 3 * levels]
        )
    )
    return jnp.concatenate([east_new, north_new, temper_new, height_two[None]], axis=0)


def one_step(state, masks, coefs, target, hit):
    levels = masks.shape[0]
    surface = masks[0]
    center, ddx, ddy, laplace = gradients(widen_state(state))
    height = center[3 * levels]
    thick, visc, kappa = level_terms(coefs)
    spread = ddx[:levels] + ddy[levels : 2 * levels]
    height_one = surface * (height - DT * jnp.sum(thick * masks * spread, axis=0))
    height_two = surface * (height_one + NUDGE * hit * (target - height_one))
    unused, grad_x, grad_y, unused_lap = gradients(widen_surface(height_two[None]))
    return finish(center, ddx, ddy, laplace, masks, visc, kappa, grad_x, grad_y, height_two)


def window(source, grid_cols, rows, cols):
    return (pl.ds((source // grid_cols) * rows, rows), pl.ds((source % grid_cols) * cols, cols))


def exchange_kernel(
    count, grid_cols, groups, reach, anc_ref, ens_ref, alt_ref, out_ref, lines_ref, low_ref, high_ref,
    held_a, held_b, outgoing_a, outgoing_b, send1, recv1, send2, recv2, send3, recv3, local, edge_sems,
):
    me = lax.axis_index("particle")
    held = (held_a, held_b)
    outgoing = (outgoing_a, outgoing_b)
    rows, cols = held_a.shape[2], held_a.shape[3]

    barrier = pltpu.get_barrier_semaphore()
    for offset in range(1, count):
        peer = lax.rem(me + offset, count)
        pl.semaphore_signal(barrier, inc=1, device_id={"particle": peer}, device_id_type=MESH)
    pl.semaphore_wait(barrier, count - 1)

    def chunk_of(dest, fields):
        r, c = window(dest, grid_cols, rows, cols)
        return ens_ref.at[fields, r, c]

    def first_copy(group, fields, offset, peer):
        return pltpu.make_async_remote_copy(
            src_ref=chunk_of(peer, fields), dst_ref=held[group].at[me],
            send_sem=send1.at[group, offset], recv_sem=recv1.at[group, me],
            device_id={"particle": peer}, device_id_type=MESH,
        )

    def second_copy(group, fields, offset, peer):
        r_me, c_me = window(me, grid_cols, rows, cols)
        return pltpu.make_async_remote_copy(
            src_ref=outgoing[group].at[peer], dst_ref=out_ref.at[fields, r_me, c_me],
            send_sem=send2.at[group, offset], recv_sem=recv2.at[group, me],
            device_id={"particle": peer}, device_id_type=MESH,
        )

    own_lines = pltpu.make_async_copy(alt_ref, lines_ref.at[me], local.at[0])
    own_lines.start()
    line_copies = []
    for offset in range(1, count):
        peer = lax.rem(me + offset, count)
        lines = pltpu.make_async_remote_copy(
            src_ref=alt_ref, dst_ref=lines_ref.at[me], send_sem=send3.at[offset],
            recv_sem=recv3.at[me], device_id={"particle": peer}, device_id_type=MESH,
        )
        lines.start()
        line_copies.append(lines)

    own_parts = []
    firsts = []
    for group, fields in enumerate(groups):
        own = pltpu.make_async_copy(chunk_of(me, fields), held[group].at[me], local.at[1 + group])
        own.start()
        own_parts.append(own)
        copies = []
        for offset in range(1, count):
            copy = first_copy(group, fields, offset, lax.rem(me + offset, count))
            copy.start()
            copies.append(copy)
        firsts.append(copies)

    seconds = []
    for group, fields in enumerate(groups):
        own_parts[group].wait()
        for offset, copy in zip(range(1, count), firsts[group]):
            sender = lax.rem(me + count - offset, count)
            copy.wait_send()
            pltpu.make_async_remote_copy(
                src_ref=chunk_of(me, fields), dst_ref=held[group].at[sender],
                send_sem=send1.at[group, offset], recv_sem=recv1.at[group, sender],
                device_id={"particle": sender}, device_id_type=MESH,
            ).wait_recv()
        for member in range(count):
            source = jnp.clip(anc_ref[member], 0, count - 1)
            outgoing[group][member] = held[group][source]
        r_me, c_me = window(me, grid_cols, rows, cols)
        mine = pltpu.make_async_copy(
            outgoing[group].at[me], out_ref.at[fields, r_me, c_me], local.at[3 + group]
        )
        mine.start()
        copies = [mine]
        for offset in range(1, count):
            copy = second_copy(group, fields, offset, lax.rem(me + offset, count))
            copy.start()
            copies.append(copy)
        seconds.append(copies)

    own_lines.wait()
    for offset, lines in zip(range(1, count), line_copies):
        sender = lax.rem(me + count - offset, count)
        lines.wait_send()
        pltpu.make_async_remote_copy(
            src_ref=alt_ref, dst_ref=lines_ref.at[sender], send_sem=send3.at[offset],
            recv_sem=recv3.at[sender], device_id={"particle": sender}, device_id_type=MESH,
        ).wait_recv()
    height = out_ref.shape[1]
    edges = []
    for group, fields in enumerate(groups):
        seconds[group][0].wait()
        for offset, copy in zip(range(1, count), seconds[group][1:]):
            sender = lax.rem(me + count - offset, count)
            r_s, c_s = window(sender, grid_cols, rows, cols)
            copy.wait_send()
            pltpu.make_async_remote_copy(
                src_ref=outgoing[group].at[me], dst_ref=out_ref.at[fields, r_s, c_s],
                send_sem=send2.at[group, offset], recv_sem=recv2.at[group, sender],
                device_id={"particle": sender}, device_id_type=MESH,
            ).wait_recv()
        for turn, (start, target) in enumerate(((0, low_ref), (height - reach, high_ref))):
            edge = pltpu.make_async_copy(
                out_ref.at[fields, pl.ds(start, reach)], target.at[fields],
                edge_sems.at[2 * group + turn],
            )
            edge.start()
            edges.append(edge)
    for edge in edges:
        edge.wait()


def resample(tile, ancestors, altimetry, reach):
    count = lax.axis_size("particle")
    fields, height, width = tile.shape
    grid_rows = 4
    grid_cols = count // grid_rows
    rows, cols = height // grid_rows, width // grid_cols
    split = (fields + 1) // 2
    groups = (pl.ds(0, split), pl.ds(split, fields - split))
    sems = pltpu.SemaphoreType.DMA((count,))
    grouped = pltpu.SemaphoreType.DMA((len(groups), count))
    return pl.pallas_call(
        functools.partial(exchange_kernel, count, grid_cols, groups, reach),
        out_shape=(
            jax.ShapeDtypeStruct(tile.shape, tile.dtype),
            jax.ShapeDtypeStruct((count,) + altimetry.shape, altimetry.dtype),
            jax.ShapeDtypeStruct((fields, reach, width), tile.dtype),
            jax.ShapeDtypeStruct((fields, reach, width), tile.dtype),
        ),
        in_specs=[
            pl.BlockSpec(memory_space=pltpu.SMEM),
            pl.BlockSpec(memory_space=pl.ANY),
            pl.BlockSpec(memory_space=pltpu.VMEM),
        ],
        out_specs=(
            pl.BlockSpec(memory_space=pl.ANY),
            pl.BlockSpec(memory_space=pltpu.VMEM),
            pl.BlockSpec(memory_space=pltpu.VMEM),
            pl.BlockSpec(memory_space=pltpu.VMEM),
        ),
        scratch_shapes=[
            pltpu.VMEM((count, split, rows, cols), tile.dtype),
            pltpu.VMEM((count, fields - split, rows, cols), tile.dtype),
            pltpu.VMEM((count, split, rows, cols), tile.dtype),
            pltpu.VMEM((count, fields - split, rows, cols), tile.dtype),
            grouped, grouped, grouped, grouped, sems, sems,
            pltpu.SemaphoreType.DMA((1 + 2 * len(groups),)),
            pltpu.SemaphoreType.DMA((2 * len(groups),)),
        ],
        compiler_params=pltpu.CompilerParams(collective_id=0, has_side_effects=True),
    )(ancestors, tile, altimetry)


def stencil_kernel(
    coef_ref, tile_ref, aux_ref, top_ref, bottom_ref, top_aux_ref, bottom_aux_ref, hit_ref,
    out_ref, state, aux,
):
    fields, rows, width = tile_ref.shape
    extra = aux_ref.shape[0]
    reach = top_ref.shape[1]
    levels = coef_ref.shape[1]
    span = state.shape[1]
    state[:, :reach] = top_ref[...]
    state[:, reach : reach + rows] = tile_ref[...]
    state[:, reach + rows :] = bottom_ref[...]
    aux[:, :reach] = top_aux_ref[...]
    aux[:, reach : reach + rows] = aux_ref[...]
    aux[:, reach + rows :] = bottom_aux_ref[...]

    lane = lax.broadcasted_iota(jnp.int32, (span, width), 1)
    first_lane = lane == 0
    last_lane = lane == width - 1

    def east(f):
        return pltpu.roll(f, span - 1, 0)

    def west(f):
        return pltpu.roll(f, 1, 0)

    def north(f):
        return jnp.where(last_lane, 0.0, pltpu.roll(f, width - 1, 1))

    def south(f):
        return jnp.where(first_lane, 0.0, pltpu.roll(f, 1, 1))

    def parts(f):
        e, w, n, s = east(f), west(f), north(f), south(f)
        return (e - w) * 0.5, (n - s) * 0.5, e + w + n + s - 4.0 * f

    depth = aux[extra - 1]
    masks = [(k < depth).astype(jnp.float32) for k in range(levels)]
    surface = masks[0]
    for field in range(fields):
        state[field] = state[field] * masks[field % levels]
    for step in range(STEPS):
        spread = None
        for k in range(levels):
            ddx_u = parts(state[k])[0]
            ddy_v = parts(state[levels + k])[1]
            term = (coef_ref[0, k] * masks[k]) * (ddx_u + ddy_v)
            spread = term if spread is None else spread + term
        height = state[3 * levels]
        height_one = surface * (height - DT * spread)
        hit = hit_ref[step]
        height_two = surface * (height_one + NUDGE * hit * (aux[step] - height_one))
        grad_x, grad_y, unused = parts(height_two)
        for k in range(levels):
            visc = 0.2 * coef_ref[1, k]
            kappa = 0.2 * coef_ref[2, k]
            east_vel = state[k]
            north_vel = state[levels + k]
            temper = state[2 * levels + k]
            unused_x, unused_y, lap_u = parts(east_vel)
            unused_x, unused_y, lap_v = parts(north_vel)
            ddx_t, ddy_t, lap_t = parts(temper)
            state[k] = masks[k] * (
                east_vel + DT * (CORIOLIS * north_vel - grad_x + visc * lap_u)
            )
            state[levels + k] = masks[k] * (
                north_vel + DT * (-CORIOLIS * east_vel - grad_y + visc * lap_v)
            )
            state[2 * levels + k] = masks[k] * (
                temper + DT * (kappa * lap_t - east_vel * ddx_t - north_vel * ddy_t)
            )
        state[3 * levels] = height_two
    out_ref[...] = state[:, reach : reach + rows]


def run_steps(coefs, tile, aux, top, bottom, top_aux, bottom_aux, hits):
    fields, rows, width = tile.shape
    span = rows + 2 * top.shape[1]
    vmem = pl.BlockSpec(memory_space=pltpu.VMEM)
    return pl.pallas_call(
        stencil_kernel,
        out_shape=jax.ShapeDtypeStruct(tile.shape, tile.dtype),
        in_specs=[pl.BlockSpec(memory_space=pltpu.SMEM)] + [vmem] * 7,
        out_specs=vmem,
        scratch_shapes=[
            pltpu.VMEM((fields, span, width), tile.dtype),
            pltpu.VMEM((aux.shape[0], span, width), tile.dtype),
        ],
    )(coefs, tile, aux, top, bottom, top_aux, bottom_aux, hits)


def per_device(ensemble, ancestors, depth_levels, level_coefs, altimetry, obs_rows):
    width_y = ensemble.shape[3]
    reach = 8
    tile, gathered, low, high = resample(ensemble[0], ancestors, altimetry, reach)
    count = lax.axis_size("space")
    forward = [(i, (i + 1) % count) for i in range(count)]
    backward = [(target, source) for source, target in forward]
    top = lax.ppermute(high, "space", forward)
    bottom = lax.ppermute(low, "space", backward)
    own_lines = jnp.moveaxis(gathered, 0, 1).reshape(
        (altimetry.shape[0], -1) + altimetry.shape[2:]
    )
    lines_above = lax.ppermute(own_lines[..., -reach:], "space", forward)
    lines_below = lax.ppermute(own_lines[..., :reach], "space", backward)
    depth = depth_levels.astype(jnp.float32)
    depth_above = lax.ppermute(depth[-reach:], "space", forward)
    depth_below = lax.ppermute(depth[:reach], "space", backward)
    all_lines = jnp.concatenate([lines_above, own_lines, lines_below], axis=-1)
    columns = jnp.arange(width_y, dtype=jnp.int32)
    targets = []
    hits = []
    for step in range(STEPS):
        onehot = (obs_rows[step][:, None] == columns[None, :]).astype(jnp.float32)
        targets.append(
            jnp.dot(
                all_lines[step].T, onehot, precision=lax.Precision.HIGHEST,
                preferred_element_type=jnp.float32,
            )
        )
        hits.append(jnp.sum(onehot, axis=0)[None, :])
    targets = jnp.stack(targets, axis=0)
    rows = tile.shape[1]
    aux = jnp.concatenate([targets[:, reach : reach + rows], depth[None]], axis=0)
    top_aux = jnp.concatenate([targets[:, :reach], depth_above[None]], axis=0)
    bottom_aux = jnp.concatenate([targets[:, reach + rows :], depth_below[None]], axis=0)
    state = run_steps(
        level_coefs, tile, aux, top, bottom, top_aux, bottom_aux, jnp.stack(hits, axis=0)
    )
    return state[None]


def solution(mesh):
    in_specs = (
        P("particle", None, "space", None),
        P(),
        P("space", None),
        P(),
        P(None, "particle", "space"),
        P(),
    )
    out_specs = P("particle", None, "space", None)
    return jax.shard_map(
        per_device, mesh=mesh, in_specs=in_specs, out_specs=out_specs, check_vma=False
    )
```

```python
import functools

import jax
import jax.numpy as jnp
from jax import lax
from jax.experimental import pallas as pl
from jax.experimental.pallas import tpu as pltpu
from jax.sharding import PartitionSpec as P

MESH = pl.DeviceIdType.MESH

STEPS = 3


DT = 0.2
CORIOLIS = 0.5
GRAVITY = 1.0
NUDGE = 0.5


def with_halo(block, sides, width):
    for axis, dim in sides:
        count = lax.axis_size(axis)
        forward = [(i, i + 1) for i in range(count - 1)]
        forward.append((count - 1, 0))
        backward = [(target, source) for source, target in forward]
        low = lax.ppermute(
            lax.slice_in_dim(block, block.shape[dim] - width, None, axis=dim), axis, forward
        )
        high = lax.ppermute(lax.slice_in_dim(block, 0, width, axis=dim), axis, backward)
        block = jnp.concatenate([low, block, high], axis=dim)
    return block


def pad_second(field):
    return jnp.pad(field, [(0, 0)] * (field.ndim - 1) + [(1, 1)])


def gradients(wide):
    center = wide[:, 1:-1]
    east = wide[:, 2:]
    west = wide[:, :-2]
    padded = pad_second(center)
    ddx = (east - west) * 0.5
    ddy = (padded[..., 2:] - padded[..., :-2]) * 0.5
    laplace = east + west + padded[..., 2:] + padded[..., :-2] - 4.0 * center
    return (center, ddx, ddy, laplace)


def widen_state(field):
    return with_halo(field, (("space", 1),), 1)


def widen_surface(field):
    return with_halo(field, (("space", 1),), 1)


def level_terms(coefs):
    thick = coefs[0][:, None, None]
    visc = 0.2 * coefs[1][:, None, None]
    kappa = 0.2 * coefs[2][:, None, None]
    return (thick, visc, kappa)


def finish(center, ddx, ddy, laplace, masks, visc, kappa, grad_x, grad_y, height_two):
    levels = masks.shape[0]
    east_vel = center[:levels]
    north_vel = center[levels : 2 * levels]
    temper = center[2 * levels : 3 * levels]
    east_new = masks * (
        east_vel + DT * (CORIOLIS * north_vel - GRAVITY * grad_x + visc * laplace[:levels])
    )
    north_new = masks * (
        north_vel
        + DT * (-CORIOLIS * east_vel - GRAVITY * grad_y + visc * laplace[levels : 2 * levels])
    )
    temper_new = masks * (
        temper
        + DT
        * (
            kappa * laplace[2 * levels : 3 * levels]
            - east_vel * ddx[2 * levels : 3 * levels]
            - north_vel * ddy[2 * levels : 3 * levels]
        )
    )
    return jnp.concatenate([east_new, north_new, temper_new, height_two[None]], axis=0)


def one_step(state, masks, coefs, target, hit):
    levels = masks.shape[0]
    surface = masks[0]
    center, ddx, ddy, laplace = gradients(widen_state(state))
    height = center[3 * levels]
    thick, visc, kappa = level_terms(coefs)
    spread = ddx[:levels] + ddy[levels : 2 * levels]
    height_one = surface * (height - DT * jnp.sum(thick * masks * spread, axis=0))
    height_two = surface * (height_one + NUDGE * hit * (target - height_one))
    unused, grad_x, grad_y, unused_lap = gradients(widen_surface(height_two[None]))
    return finish(center, ddx, ddy, laplace, masks, visc, kappa, grad_x, grad_y, height_two)


def window(source, grid_cols, rows, cols):
    return (pl.ds((source // grid_cols) * rows, rows), pl.ds((source % grid_cols) * cols, cols))


def exchange_kernel(
    count, grid_cols, groups, reach, anc_ref, ens_ref, alt_ref, out_ref, lines_ref, low_ref, high_ref,
    held_a, held_b, outgoing_a, outgoing_b, send1, recv1, send2, recv2, send3, recv3, local, edge_sems,
):
    me = lax.axis_index("particle")
    held = (held_a, held_b)
    outgoing = (outgoing_a, outgoing_b)
    rows, cols = held_a.shape[2], held_a.shape[3]

    barrier = pltpu.get_barrier_semaphore()
    for offset in range(1, count):
        peer = lax.rem(me + offset, count)
        pl.semaphore_signal(barrier, inc=1, device_id={"particle": peer}, device_id_type=MESH)
    pl.semaphore_wait(barrier, count - 1)

    def chunk_of(dest, fields):
        r, c = window(dest, grid_cols, rows, cols)
        return ens_ref.at[fields, r, c]

    def first_copy(group, fields, offset, peer):
        return pltpu.make_async_remote_copy(
            src_ref=chunk_of(peer, fields), dst_ref=held[group].at[me],
            send_sem=send1.at[group, offset], recv_sem=recv1.at[group, me],
            device_id={"particle": peer}, device_id_type=MESH,
        )

    def second_copy(group, fields, offset, peer):
        r_me, c_me = window(me, grid_cols, rows, cols)
        return pltpu.make_async_remote_copy(
            src_ref=outgoing[group].at[peer], dst_ref=out_ref.at[fields, r_me, c_me],
            send_sem=send2.at[group, offset], recv_sem=recv2.at[group, me],
            device_id={"particle": peer}, device_id_type=MESH,
        )

    own_lines = pltpu.make_async_copy(alt_ref, lines_ref.at[me], local.at[0])
    own_lines.start()
    line_copies = []
    for offset in range(1, count):
        peer = lax.rem(me + offset, count)
        lines = pltpu.make_async_remote_copy(
            src_ref=alt_ref, dst_ref=lines_ref.at[me], send_sem=send3.at[offset],
            recv_sem=recv3.at[me], device_id={"particle": peer}, device_id_type=MESH,
        )
        lines.start()
        line_copies.append(lines)

    own_parts = []
    firsts = []
    for group, fields in enumerate(groups):
        own = pltpu.make_async_copy(chunk_of(me, fields), held[group].at[me], local.at[1 + group])
        own.start()
        own_parts.append(own)
        copies = []
        for offset in range(1, count):
            copy = first_copy(group, fields, offset, lax.rem(me + offset, count))
            copy.start()
            copies.append(copy)
        firsts.append(copies)

    seconds = []
    for group, fields in enumerate(groups):
        own_parts[group].wait()
        for offset, copy in zip(range(1, count), firsts[group]):
            sender = lax.rem(me + count - offset, count)
            copy.wait_send()
            pltpu.make_async_remote_copy(
                src_ref=chunk_of(me, fields), dst_ref=held[group].at[sender],
                send_sem=send1.at[group, offset], recv_sem=recv1.at[group, sender],
                device_id={"particle": sender}, device_id_type=MESH,
            ).wait_recv()
        for member in range(count):
            source = jnp.clip(anc_ref[member], 0, count - 1)
            outgoing[group][member] = held[group][source]
        r_me, c_me = window(me, grid_cols, rows, cols)
        mine = pltpu.make_async_copy(
            outgoing[group].at[me], out_ref.at[fields, r_me, c_me], local.at[3 + group]
        )
        mine.start()
        copies = [mine]
        for offset in range(1, count):
            copy = second_copy(group, fields, offset, lax.rem(me + offset, count))
            copy.start()
            copies.append(copy)
        seconds.append(copies)

    own_lines.wait()
    for offset, lines in zip(range(1, count), line_copies):
        sender = lax.rem(me + count - offset, count)
        lines.wait_send()
        pltpu.make_async_remote_copy(
            src_ref=alt_ref, dst_ref=lines_ref.at[sender], send_sem=send3.at[offset],
            recv_sem=recv3.at[sender], device_id={"particle": sender}, device_id_type=MESH,
        ).wait_recv()
    height = out_ref.shape[1]
    edges = []
    for group, fields in enumerate(groups):
        seconds[group][0].wait()
        for offset, copy in zip(range(1, count), seconds[group][1:]):
            sender = lax.rem(me + count - offset, count)
            r_s, c_s = window(sender, grid_cols, rows, cols)
            copy.wait_send()
            pltpu.make_async_remote_copy(
                src_ref=outgoing[group].at[me], dst_ref=out_ref.at[fields, r_s, c_s],
                send_sem=send2.at[group, offset], recv_sem=recv2.at[group, sender],
                device_id={"particle": sender}, device_id_type=MESH,
            ).wait_recv()
        for turn, (start, target) in enumerate(((0, low_ref), (height - reach, high_ref))):
            edge = pltpu.make_async_copy(
                out_ref.at[fields, pl.ds(start, reach)], target.at[fields],
                edge_sems.at[2 * group + turn],
            )
            edge.start()
            edges.append(edge)
    for edge in edges:
        edge.wait()


def resample(tile, ancestors, altimetry, reach):
    count = lax.axis_size("particle")
    fields, height, width = tile.shape
    grid_rows = 4
    grid_cols = count // grid_rows
    rows, cols = height // grid_rows, width // grid_cols
    split = (fields + 1) // 2
    groups = (pl.ds(0, split), pl.ds(split, fields - split))
    sems = pltpu.SemaphoreType.DMA((count,))
    grouped = pltpu.SemaphoreType.DMA((len(groups), count))
    return pl.pallas_call(
        functools.partial(exchange_kernel, count, grid_cols, groups, reach),
        out_shape=(
            jax.ShapeDtypeStruct(tile.shape, tile.dtype),
            jax.ShapeDtypeStruct((count,) + altimetry.shape, altimetry.dtype),
            jax.ShapeDtypeStruct((fields, reach, width), tile.dtype),
            jax.ShapeDtypeStruct((fields, reach, width), tile.dtype),
        ),
        in_specs=[
            pl.BlockSpec(memory_space=pltpu.SMEM),
            pl.BlockSpec(memory_space=pl.ANY),
            pl.BlockSpec(memory_space=pltpu.VMEM),
        ],
        out_specs=(
            pl.BlockSpec(memory_space=pl.ANY),
            pl.BlockSpec(memory_space=pltpu.VMEM),
            pl.BlockSpec(memory_space=pltpu.VMEM),
            pl.BlockSpec(memory_space=pltpu.VMEM),
        ),
        scratch_shapes=[
            pltpu.VMEM((count, split, rows, cols), tile.dtype),
            pltpu.VMEM((count, fields - split, rows, cols), tile.dtype),
            pltpu.VMEM((count, split, rows, cols), tile.dtype),
            pltpu.VMEM((count, fields - split, rows, cols), tile.dtype),
            grouped, grouped, grouped, grouped, sems, sems,
            pltpu.SemaphoreType.DMA((1 + 2 * len(groups),)),
            pltpu.SemaphoreType.DMA((2 * len(groups),)),
        ],
        compiler_params=pltpu.CompilerParams(collective_id=0, has_side_effects=True),
    )(ancestors, tile, altimetry)


def stencil_kernel(
    coef_ref, tile_ref, aux_ref, top_ref, bottom_ref, top_aux_ref, bottom_aux_ref, hit_ref,
    out_ref, state, aux,
):
    fields, rows, width = tile_ref.shape
    extra = aux_ref.shape[0]
    reach = top_ref.shape[1]
    levels = coef_ref.shape[1]
    span = state.shape[1]
    state[:, :reach] = top_ref[...]
    state[:, reach : reach + rows] = tile_ref[...]
    state[:, reach + rows :] = bottom_ref[...]
    aux[:, :reach] = top_aux_ref[...]
    aux[:, reach : reach + rows] = aux_ref[...]
    aux[:, reach + rows :] = bottom_aux_ref[...]

    lane = lax.broadcasted_iota(jnp.int32, (span, width), 1)
    first_lane = lane == 0
    last_lane = lane == width - 1

    def east(f):
        return pltpu.roll(f, span - 1, 0)

    def west(f):
        return pltpu.roll(f, 1, 0)

    def north(f):
        return jnp.where(last_lane, 0.0, pltpu.roll(f, width - 1, 1))

    def south(f):
        return jnp.where(first_lane, 0.0, pltpu.roll(f, 1, 1))

    def parts(f):
        e, w, n, s = east(f), west(f), north(f), south(f)
        return (e - w) * 0.5, (n - s) * 0.5, e + w + n + s - 4.0 * f

    depth = aux[extra - 1]
    masks = [(k < depth).astype(jnp.float32) for k in range(levels)]
    surface = masks[0]
    for field in range(fields):
        state[field] = state[field] * masks[field % levels]
    for step in range(STEPS):
        spread = None
        for k in range(levels):
            ddx_u = parts(state[k])[0]
            ddy_v = parts(state[levels + k])[1]
            term = (coef_ref[0, k] * masks[k]) * (ddx_u + ddy_v)
            spread = term if spread is None else spread + term
        height = state[3 * levels]
        height_one = surface * (height - DT * spread)
        hit = hit_ref[step]
        height_two = surface * (height_one + NUDGE * hit * (aux[step] - height_one))
        grad_x, grad_y, unused = parts(height_two)
        for k in range(levels):
            visc = 0.2 * coef_ref[1, k]
            kappa = 0.2 * coef_ref[2, k]
            east_vel = state[k]
            north_vel = state[levels + k]
            temper = state[2 * levels + k]
            unused_x, unused_y, lap_u = parts(east_vel)
            unused_x, unused_y, lap_v = parts(north_vel)
            ddx_t, ddy_t, lap_t = parts(temper)
            state[k] = masks[k] * (
                east_vel + DT * (CORIOLIS * north_vel - grad_x + visc * lap_u)
            )
            state[levels + k] = masks[k] * (
                north_vel + DT * (-CORIOLIS * east_vel - grad_y + visc * lap_v)
            )
            state[2 * levels + k] = masks[k] * (
                temper + DT * (kappa * lap_t - east_vel * ddx_t - north_vel * ddy_t)
            )
        state[3 * levels] = height_two
    out_ref[...] = state[:, reach : reach + rows]


def run_steps(coefs, tile, aux, top, bottom, top_aux, bottom_aux, hits):
    fields, rows, width = tile.shape
    span = rows + 2 * top.shape[1]
    vmem = pl.BlockSpec(memory_space=pltpu.VMEM)
    return pl.pallas_call(
        stencil_kernel,
        out_shape=jax.ShapeDtypeStruct(tile.shape, tile.dtype),
        in_specs=[pl.BlockSpec(memory_space=pltpu.SMEM)] + [vmem] * 7,
        out_specs=vmem,
        scratch_shapes=[
            pltpu.VMEM((fields, span, width), tile.dtype),
            pltpu.VMEM((aux.shape[0], span, width), tile.dtype),
        ],
    )(coefs, tile, aux, top, bottom, top_aux, bottom_aux, hits)


def per_device(ensemble, ancestors, depth_levels, level_coefs, altimetry, obs_rows):
    width_y = ensemble.shape[3]
    reach = 8
    tile, gathered, low, high = resample(ensemble[0], ancestors, altimetry, reach)
    count = lax.axis_size("space")
    forward = [(i, (i + 1) % count) for i in range(count)]
    backward = [(target, source) for source, target in forward]
    own_lines = jnp.moveaxis(gathered, 0, 1).reshape(
        (altimetry.shape[0], -1) + altimetry.shape[2:]
    )
    lines_above = lax.ppermute(own_lines[..., -reach:], "space", forward)
    lines_below = lax.ppermute(own_lines[..., :reach], "space", backward)
    depth = depth_levels.astype(jnp.float32)
    depth_high, depth_low, high, low = lax.optimization_barrier(
        (depth[-reach:], depth[:reach], high, low)
    )
    depth_above = lax.ppermute(depth_high, "space", forward)
    depth_below = lax.ppermute(depth_low, "space", backward)
    top = lax.ppermute(high, "space", forward)
    bottom = lax.ppermute(low, "space", backward)
    all_lines = jnp.concatenate([lines_above, own_lines, lines_below], axis=-1)
    columns = jnp.arange(width_y, dtype=jnp.int32)
    targets = []
    hits = []
    for step in range(STEPS):
        onehot = (obs_rows[step][:, None] == columns[None, :]).astype(jnp.float32)
        targets.append(
            jnp.dot(
                all_lines[step].T, onehot, precision=lax.Precision.HIGHEST,
                preferred_element_type=jnp.float32,
            )
        )
        hits.append(jnp.sum(onehot, axis=0)[None, :])
    targets = jnp.stack(targets, axis=0)
    rows = tile.shape[1]
    aux = jnp.concatenate([targets[:, reach : reach + rows], depth[None]], axis=0)
    top_aux = jnp.concatenate([targets[:, :reach], depth_above[None]], axis=0)
    bottom_aux = jnp.concatenate([targets[:, reach + rows :], depth_below[None]], axis=0)
    state = run_steps(
        level_coefs, tile, aux, top, bottom, top_aux, bottom_aux, jnp.stack(hits, axis=0)
    )
    return state[None]


def solution(mesh):
    in_specs = (
        P("particle", None, "space", None),
        P(),
        P("space", None),
        P(),
        P(None, "particle", "space"),
        P(),
    )
    out_specs = P("particle", None, "space", None)
    return jax.shard_map(
        per_device, mesh=mesh, in_specs=in_specs, out_specs=out_specs, check_vma=False
    )
```

```python
import functools

import jax
import jax.numpy as jnp
from jax import lax
from jax.experimental import pallas as pl
from jax.experimental.pallas import tpu as pltpu
from jax.sharding import PartitionSpec as P

MESH = pl.DeviceIdType.MESH

STEPS = 3


DT = 0.2
CORIOLIS = 0.5
GRAVITY = 1.0
NUDGE = 0.5


def with_halo(block, sides, width):
    for axis, dim in sides:
        count = lax.axis_size(axis)
        forward = [(i, i + 1) for i in range(count - 1)]
        forward.append((count - 1, 0))
        backward = [(target, source) for source, target in forward]
        low = lax.ppermute(
            lax.slice_in_dim(block, block.shape[dim] - width, None, axis=dim), axis, forward
        )
        high = lax.ppermute(lax.slice_in_dim(block, 0, width, axis=dim), axis, backward)
        block = jnp.concatenate([low, block, high], axis=dim)
    return block


def pad_second(field):
    return jnp.pad(field, [(0, 0)] * (field.ndim - 1) + [(1, 1)])


def gradients(wide):
    center = wide[:, 1:-1]
    east = wide[:, 2:]
    west = wide[:, :-2]
    padded = pad_second(center)
    ddx = (east - west) * 0.5
    ddy = (padded[..., 2:] - padded[..., :-2]) * 0.5
    laplace = east + west + padded[..., 2:] + padded[..., :-2] - 4.0 * center
    return (center, ddx, ddy, laplace)


def widen_state(field):
    return with_halo(field, (("space", 1),), 1)


def widen_surface(field):
    return with_halo(field, (("space", 1),), 1)


def level_terms(coefs):
    thick = coefs[0][:, None, None]
    visc = 0.2 * coefs[1][:, None, None]
    kappa = 0.2 * coefs[2][:, None, None]
    return (thick, visc, kappa)


def finish(center, ddx, ddy, laplace, masks, visc, kappa, grad_x, grad_y, height_two):
    levels = masks.shape[0]
    east_vel = center[:levels]
    north_vel = center[levels : 2 * levels]
    temper = center[2 * levels : 3 * levels]
    east_new = masks * (
        east_vel + DT * (CORIOLIS * north_vel - GRAVITY * grad_x + visc * laplace[:levels])
    )
    north_new = masks * (
        north_vel
        + DT * (-CORIOLIS * east_vel - GRAVITY * grad_y + visc * laplace[levels : 2 * levels])
    )
    temper_new = masks * (
        temper
        + DT
        * (
            kappa * laplace[2 * levels : 3 * levels]
            - east_vel * ddx[2 * levels : 3 * levels]
            - north_vel * ddy[2 * levels : 3 * levels]
        )
    )
    return jnp.concatenate([east_new, north_new, temper_new, height_two[None]], axis=0)


def one_step(state, masks, coefs, target, hit):
    levels = masks.shape[0]
    surface = masks[0]
    center, ddx, ddy, laplace = gradients(widen_state(state))
    height = center[3 * levels]
    thick, visc, kappa = level_terms(coefs)
    spread = ddx[:levels] + ddy[levels : 2 * levels]
    height_one = surface * (height - DT * jnp.sum(thick * masks * spread, axis=0))
    height_two = surface * (height_one + NUDGE * hit * (target - height_one))
    unused, grad_x, grad_y, unused_lap = gradients(widen_surface(height_two[None]))
    return finish(center, ddx, ddy, laplace, masks, visc, kappa, grad_x, grad_y, height_two)


def window(source, grid_cols, rows, cols):
    return (pl.ds((source // grid_cols) * rows, rows), pl.ds((source % grid_cols) * cols, cols))


def exchange_kernel(
    count, grid_cols, groups, reach, anc_ref, ens_ref, alt_ref, out_ref, lines_ref, low_ref, high_ref,
    held_a, held_b, outgoing_a, outgoing_b, send1, recv1, send2, recv2, send3, recv3, local, edge_sems,
):
    me = lax.axis_index("particle")
    held = (held_a, held_b)
    outgoing = (outgoing_a, outgoing_b)
    rows, cols = held_a.shape[2], held_a.shape[3]

    barrier = pltpu.get_barrier_semaphore()
    for offset in range(1, count):
        peer = lax.rem(me + offset, count)
        pl.semaphore_signal(barrier, inc=1, device_id={"particle": peer}, device_id_type=MESH)
    pl.semaphore_wait(barrier, count - 1)

    def chunk_of(dest, fields):
        r, c = window(dest, grid_cols, rows, cols)
        return ens_ref.at[fields, r, c]

    def first_copy(group, fields, offset, peer):
        return pltpu.make_async_remote_copy(
            src_ref=chunk_of(peer, fields), dst_ref=held[group].at[me],
            send_sem=send1.at[group, offset], recv_sem=recv1.at[group, me],
            device_id={"particle": peer}, device_id_type=MESH,
        )

    def second_copy(group, fields, offset, peer):
        r_me, c_me = window(me, grid_cols, rows, cols)
        return pltpu.make_async_remote_copy(
            src_ref=outgoing[group].at[peer], dst_ref=out_ref.at[fields, r_me, c_me],
            send_sem=send2.at[group, offset], recv_sem=recv2.at[group, me],
            device_id={"particle": peer}, device_id_type=MESH,
        )

    own_lines = pltpu.make_async_copy(alt_ref, lines_ref.at[me], local.at[0])
    own_lines.start()
    line_copies = []
    for offset in range(1, count):
        peer = lax.rem(me + offset, count)
        lines = pltpu.make_async_remote_copy(
            src_ref=alt_ref, dst_ref=lines_ref.at[me], send_sem=send3.at[offset],
            recv_sem=recv3.at[me], device_id={"particle": peer}, device_id_type=MESH,
        )
        lines.start()
        line_copies.append(lines)

    own_parts = []
    firsts = []
    for group, fields in enumerate(groups):
        own = pltpu.make_async_copy(chunk_of(me, fields), held[group].at[me], local.at[1 + group])
        own.start()
        own_parts.append(own)
        copies = []
        for offset in range(1, count):
            copy = first_copy(group, fields, offset, lax.rem(me + offset, count))
            copy.start()
            copies.append(copy)
        firsts.append(copies)

    seconds = []
    for group, fields in enumerate(groups):
        own_parts[group].wait()
        for offset, copy in zip(range(1, count), firsts[group]):
            sender = lax.rem(me + count - offset, count)
            copy.wait_send()
            pltpu.make_async_remote_copy(
                src_ref=chunk_of(me, fields), dst_ref=held[group].at[sender],
                send_sem=send1.at[group, offset], recv_sem=recv1.at[group, sender],
                device_id={"particle": sender}, device_id_type=MESH,
            ).wait_recv()
        for member in range(count):
            source = jnp.clip(anc_ref[member], 0, count - 1)
            outgoing[group][member] = held[group][source]
        r_me, c_me = window(me, grid_cols, rows, cols)
        mine = pltpu.make_async_copy(
            outgoing[group].at[me], out_ref.at[fields, r_me, c_me], local.at[3 + group]
        )
        mine.start()
        copies = [mine]
        for offset in range(1, count):
            copy = second_copy(group, fields, offset, lax.rem(me + offset, count))
            copy.start()
            copies.append(copy)
        seconds.append(copies)

    own_lines.wait()
    for offset, lines in zip(range(1, count), line_copies):
        sender = lax.rem(me + count - offset, count)
        lines.wait_send()
        pltpu.make_async_remote_copy(
            src_ref=alt_ref, dst_ref=lines_ref.at[sender], send_sem=send3.at[offset],
            recv_sem=recv3.at[sender], device_id={"particle": sender}, device_id_type=MESH,
        ).wait_recv()
    height = out_ref.shape[1]
    edges = []
    for group, fields in enumerate(groups):
        seconds[group][0].wait()
        for offset, copy in zip(range(1, count), seconds[group][1:]):
            sender = lax.rem(me + count - offset, count)
            r_s, c_s = window(sender, grid_cols, rows, cols)
            copy.wait_send()
            pltpu.make_async_remote_copy(
                src_ref=outgoing[group].at[me], dst_ref=out_ref.at[fields, r_s, c_s],
                send_sem=send2.at[group, offset], recv_sem=recv2.at[group, sender],
                device_id={"particle": sender}, device_id_type=MESH,
            ).wait_recv()
        for turn, (start, target) in enumerate(((0, low_ref), (height - reach, high_ref))):
            edge = pltpu.make_async_copy(
                out_ref.at[fields, pl.ds(start, reach)], target.at[fields],
                edge_sems.at[2 * group + turn],
            )
            edge.start()
            edges.append(edge)
    for edge in edges:
        edge.wait()


def resample(tile, ancestors, altimetry, reach):
    count = lax.axis_size("particle")
    fields, height, width = tile.shape
    grid_rows = 4
    grid_cols = count // grid_rows
    rows, cols = height // grid_rows, width // grid_cols
    split = (fields + 1) // 2
    groups = (pl.ds(0, split), pl.ds(split, fields - split))
    sems = pltpu.SemaphoreType.DMA((count,))
    grouped = pltpu.SemaphoreType.DMA((len(groups), count))
    return pl.pallas_call(
        functools.partial(exchange_kernel, count, grid_cols, groups, reach),
        out_shape=(
            jax.ShapeDtypeStruct(tile.shape, tile.dtype),
            jax.ShapeDtypeStruct((count,) + altimetry.shape, altimetry.dtype),
            jax.ShapeDtypeStruct((fields, reach, width), tile.dtype),
            jax.ShapeDtypeStruct((fields, reach, width), tile.dtype),
        ),
        in_specs=[
            pl.BlockSpec(memory_space=pltpu.SMEM),
            pl.BlockSpec(memory_space=pl.ANY),
            pl.BlockSpec(memory_space=pltpu.VMEM),
        ],
        out_specs=(
            pl.BlockSpec(memory_space=pl.ANY),
            pl.BlockSpec(memory_space=pltpu.VMEM),
            pl.BlockSpec(memory_space=pltpu.VMEM),
            pl.BlockSpec(memory_space=pltpu.VMEM),
        ),
        scratch_shapes=[
            pltpu.VMEM((count, split, rows, cols), tile.dtype),
            pltpu.VMEM((count, fields - split, rows, cols), tile.dtype),
            pltpu.VMEM((count, split, rows, cols), tile.dtype),
            pltpu.VMEM((count, fields - split, rows, cols), tile.dtype),
            grouped, grouped, grouped, grouped, sems, sems,
            pltpu.SemaphoreType.DMA((1 + 2 * len(groups),)),
            pltpu.SemaphoreType.DMA((2 * len(groups),)),
        ],
        compiler_params=pltpu.CompilerParams(collective_id=0, has_side_effects=True),
    )(ancestors, tile, altimetry)


def stencil_kernel(
    coef_ref, tile_ref, aux_ref, top_ref, bottom_ref, top_aux_ref, bottom_aux_ref, hit_ref,
    out_ref, state, aux,
):
    fields, rows, width = tile_ref.shape
    extra = aux_ref.shape[0]
    reach = top_ref.shape[1]
    levels = coef_ref.shape[1]
    span = state.shape[1]
    state[:, :reach] = top_ref[...]
    state[:, reach : reach + rows] = tile_ref[...]
    state[:, reach + rows :] = bottom_ref[...]
    aux[:, :reach] = top_aux_ref[...]
    aux[:, reach : reach + rows] = aux_ref[...]
    aux[:, reach + rows :] = bottom_aux_ref[...]

    lane = lax.broadcasted_iota(jnp.int32, (span, width), 1)
    first_lane = lane == 0
    last_lane = lane == width - 1

    def east(f):
        return pltpu.roll(f, span - 1, 0)

    def west(f):
        return pltpu.roll(f, 1, 0)

    def north(f):
        return jnp.where(last_lane, 0.0, pltpu.roll(f, width - 1, 1))

    def south(f):
        return jnp.where(first_lane, 0.0, pltpu.roll(f, 1, 1))

    def parts(f):
        e, w, n, s = east(f), west(f), north(f), south(f)
        return (e - w) * 0.5, (n - s) * 0.5, e + w + n + s - 4.0 * f

    depth = aux[extra - 1]
    masks = [(k < depth).astype(jnp.float32) for k in range(levels)]
    surface = masks[0]
    for field in range(fields):
        state[field] = state[field] * masks[field % levels]
    for step in range(STEPS):
        spread = None
        for k in range(levels):
            ddx_u = parts(state[k])[0]
            ddy_v = parts(state[levels + k])[1]
            term = (coef_ref[0, k] * masks[k]) * (ddx_u + ddy_v)
            spread = term if spread is None else spread + term
        height = state[3 * levels]
        height_one = surface * (height - DT * spread)
        hit = hit_ref[step]
        height_two = surface * (height_one + NUDGE * hit * (aux[step] - height_one))
        grad_x, grad_y, unused = parts(height_two)
        for k in range(levels):
            visc = 0.2 * coef_ref[1, k]
            kappa = 0.2 * coef_ref[2, k]
            east_vel = state[k]
            north_vel = state[levels + k]
            temper = state[2 * levels + k]
            unused_x, unused_y, lap_u = parts(east_vel)
            unused_x, unused_y, lap_v = parts(north_vel)
            ddx_t, ddy_t, lap_t = parts(temper)
            state[k] = masks[k] * (
                east_vel + DT * (CORIOLIS * north_vel - grad_x + visc * lap_u)
            )
            state[levels + k] = masks[k] * (
                north_vel + DT * (-CORIOLIS * east_vel - grad_y + visc * lap_v)
            )
            state[2 * levels + k] = masks[k] * (
                temper + DT * (kappa * lap_t - east_vel * ddx_t - north_vel * ddy_t)
            )
        state[3 * levels] = height_two
    out_ref[...] = state[:, reach : reach + rows]


def run_steps(coefs, tile, aux, top, bottom, top_aux, bottom_aux, hits):
    fields, rows, width = tile.shape
    span = rows + 2 * top.shape[1]
    vmem = pl.BlockSpec(memory_space=pltpu.VMEM)
    return pl.pallas_call(
        stencil_kernel,
        out_shape=jax.ShapeDtypeStruct(tile.shape, tile.dtype),
        in_specs=[pl.BlockSpec(memory_space=pltpu.SMEM)] + [vmem] * 7,
        out_specs=vmem,
        scratch_shapes=[
            pltpu.VMEM((fields, span, width), tile.dtype),
            pltpu.VMEM((aux.shape[0], span, width), tile.dtype),
        ],
    )(coefs, tile, aux, top, bottom, top_aux, bottom_aux, hits)


def per_device(ensemble, ancestors, depth_levels, level_coefs, altimetry, obs_rows):
    width_y = ensemble.shape[3]
    reach = 8
    tile, gathered, low, high = resample(ensemble[0], ancestors, altimetry, reach)
    count = lax.axis_size("space")
    forward = [(i, (i + 1) % count) for i in range(count)]
    backward = [(target, source) for source, target in forward]
    top = lax.ppermute(high, "space", forward)
    bottom = lax.ppermute(low, "space", backward)
    columns = jnp.arange(width_y, dtype=jnp.int32)
    targets = []
    hits = []
    for step in range(STEPS):
        onehot = (obs_rows[step][:, None] == columns[None, :]).astype(jnp.float32)
        targets.append(
            jnp.einsum(
                "jix,jiy->xy", gathered[:, step], onehot.reshape(gathered.shape[0], -1, width_y),
                precision=lax.Precision.HIGHEST, preferred_element_type=jnp.float32,
            )
        )
        hits.append(jnp.sum(onehot, axis=0)[None, :])
    aux = jnp.stack(targets + [depth_levels.astype(jnp.float32)], axis=0)
    top_aux = lax.ppermute(aux[:, -reach:], "space", forward)
    bottom_aux = lax.ppermute(aux[:, :reach], "space", backward)
    state = run_steps(
        level_coefs, tile, aux, top, bottom, top_aux, bottom_aux, jnp.stack(hits, axis=0)
    )
    return state[None]


def solution(mesh):
    in_specs = (
        P("particle", None, "space", None),
        P(),
        P("space", None),
        P(),
        P(None, "particle", "space"),
        P(),
    )
    out_specs = P("particle", None, "space", None)
    return jax.shard_map(
        per_device, mesh=mesh, in_specs=in_specs, out_specs=out_specs, check_vma=False
    )
```
